128 devices in a mesh: grp: 16 (over x, y), blk: 8 (over z, core).
Axes of the slice: x: 4, y: 4, z: 4, core: 2. Of those that a mesh axis runs over, the one named last changes fastest.
Arguments:
- visual: bfloat16 [98304, 3584], P(('grp', 'blk')), may hold values from -6 to 6
- text_queries: float32 [4096, 3584], P(('grp', 'blk')), may hold values from -100 to 100
- kv_weight: bfloat16 [3584, 1024], replicated, may hold values from -0.09375 to 0.09375
- placement: int32 [12288, 1], P(('grp', 'blk')), may hold values from 0 to 127; in each aligned block of 96 rows (0 to 95, 96 to 191, ...) at most 2 rows name the same one
Outputs:
- attended: float32 [4096, 3584], P(('grp', 'blk'))
The draws below stay inside these ranges and needn't reach their ends.
Inputs may be any that keep to these rules, and one draw needn't show every extreme that they name: `placement`: among the 96 blocks of one frame owner at most 2 name the same attention owner, a bound that some block reaches; every attention owner is named by some block.
All inputs are finite; a program needn't handle non-finite values.
Results may differ from the reference program's by a relative error of at most 0.0003.
Values sent between devices are 32-bit elements; how exact they have to be, the bound alone decides.
No kernel may reach another device: no remote copies, remote signals or barrier semaphores. Data moves between devices by JAX's collectives and lax.ppermute only.
A program may use at most 128 MiB of HBM per device.

```python
import math
import jax
import jax.numpy as jnp
import numpy as np
from jax import lax

DV = 3584
HEADS = 28
KV_HEADS = 4
HEAD_DIM = 128
QROWS = 32
BLOCKS = 96
BLOCK_ROWS = 8
PER_PAIR = 2
TEXT = 4096
VISUAL = 98304
N_GRP = 16
N_BLK = 8
DEVICES = 128


def draw_text_queries(key, part):
    base = jax.random.normal(key, (TEXT, HEADS * HEAD_DIM), jnp.float32)
    return jnp.clip(base, -100.0, 100.0)


def shard_levels(rng, shape, cuts, smallest, largest):
    gain = 1.0
    for dim, blocks in cuts:
        draws = jax.random.uniform(jax.random.fold_in(jax.random.fold_in(rng, 6), dim), (blocks,), jnp.float32, smallest / len(cuts), largest / len(cuts))
        gain = gain * jnp.repeat(jnp.exp(draws), shape[dim] // blocks).reshape((-1,) + (1,) * (len(shape) - 1 - dim))
    return gain


def assign_block(rng, own, number, rows, number_of, top, bound, skew):
    sequence = jax.random.permutation(rng, number_of)
    packed, common = portions_of(number_of, rows * top, bound, skew, True), portions_of(number_of, rows * top, bound, skew, False)
    places = jnp.arange(number_of)

    def named(sizes, rotation):
        used = int((sizes > 0).sum())
        fixed = max(1, used // 4)
        shifted = fixed + (places - fixed + rotation * (used - fixed)) % max(1, number_of - fixed)
        return jnp.zeros((number_of,), jnp.int32).at[sequence[jnp.where(places < fixed, places, shifted)]].set(jnp.asarray(sizes, jnp.int32))

    sizes = jnp.where(number % 4 == 0, named(packed, number // 4), named(common, number - number // 4 - 1))
    mixed = jax.random.permutation(jax.random.fold_in(own, 3), number_of)
    source_of, taker = mixed[0:number_of // 2 * 2:2], mixed[1:number_of // 2 * 2:2]
    slack = jnp.minimum(sizes[source_of] - 1, bound - sizes[taker]) // 2
    slack = jnp.where((source_of == sequence[0]) | (taker == sequence[0]) | (sizes[taker] == 0), 0, jnp.maximum(slack, 0))
    shifted = jax.random.randint(jax.random.fold_in(own, 4), (number_of // 2,), 0, 1 << 20) % (slack + 1)
    sizes = sizes.at[source_of].add(-shifted).at[taker].add(shifted)
    labels = jnp.searchsorted(jnp.cumsum(sizes), jnp.arange(rows * top), side="right").astype(jnp.int32)
    table = labels.reshape(top, rows).T
    table = table[jax.random.permutation(jax.random.fold_in(own, 1), rows)]
    rotation = jax.random.randint(jax.random.fold_in(own, 2), (rows, 1), 0, top)
    return jnp.take_along_axis(table, (jnp.arange(top)[None, :] + rotation) % top, axis=1)


def portions_of(number_of, total, most, skew, full):
    loads = [(1 << 20) // math.isqrt(rank ** skew) + 1 for rank in range(1, number_of + 1)]
    largest = most if full else min(most, max(-(-total // number_of), total * loads[0] // sum(loads)))
    least = 1 if total - largest >= number_of - 1 else 0
    holding, surplus = [largest] + [least] * (number_of - 1), total - largest - least * (number_of - 1)
    while surplus > 0:
        movable = [i for i in range(1, number_of) if holding[i] < largest] or [i for i in range(1, number_of) if holding[i] < most]
        pool, left = sum([loads[i] for i in movable]), surplus
        for i in movable:
            more = min(most - holding[i], max(1, left * loads[i] // pool), surplus)
            holding[i] = holding[i] + more
            surplus = surplus - more
    return np.array(holding)


def scatter_about(own_key, extent, scale, most, pieces=(), kind=jnp.bfloat16):
    factor_of = shard_levels(own_key, extent, pieces, -0.22, 0.18) if pieces else 1.0
    entries = jax.random.normal(own_key, extent, jnp.float32) * scale * factor_of
    return jnp.minimum(jnp.maximum(entries, -most), most).astype(kind)


def setup_inputs(seed: int = 0) -> dict:
    key_of = jax.random.split(jax.random.key(seed), 5)
    visual = scatter_about(key_of[0], (VISUAL, DV), 1.0, 6.0, ((0, 128),))
    text_queries = draw_text_queries(jax.random.fold_in(key_of[4], 71), 0)
    kv_weight = scatter_about(key_of[2], (DV, 2 * KV_HEADS * HEAD_DIM), DV ** -0.5, 0.09375)
    placement_keys = jax.random.split(jax.random.fold_in(key_of[3], 1), (BLOCKS * DEVICES) // BLOCKS)
    placement_turns = jax.random.permutation(jax.random.fold_in(key_of[3], 3), (BLOCKS * DEVICES) // BLOCKS)
    placement = jax.vmap(lambda own, number: assign_block(jax.random.fold_in(key_of[3], 2), own, number, BLOCKS, DEVICES, 1, PER_PAIR, 2))(placement_keys, placement_turns).reshape((BLOCKS * DEVICES, 1))
    return dict(visual=visual, text_queries=text_queries, kv_weight=kv_weight, placement=placement)


def reference(visual, text_queries, kv_weight, placement):
    devices = N_GRP * N_BLK
    group = HEADS // KV_HEADS
    width = 2 * KV_HEADS * HEAD_DIM
    kv = jnp.dot(visual, kv_weight, preferred_element_type=jnp.float32)
    flat_blocks = kv.reshape(devices * BLOCKS, BLOCK_ROWS * width)
    owner = placement.reshape(devices, BLOCKS).astype(jnp.int32)
    index = jnp.arange(BLOCKS, dtype=jnp.int32)
    earlier = (owner[:, :, None] == owner[:, None, :]) & (index[None, None, :] < index[None, :, None])
    rank = jnp.sum(earlier.astype(jnp.int32), axis=2, dtype=jnp.int32)
    source = jnp.arange(devices, dtype=jnp.int32)[:, None]
    slot = owner * (devices * PER_PAIR) + source * PER_PAIR + rank
    span = N_BLK * devices * PER_PAIR
    scale = HEAD_DIM ** -0.5

    def segment(seg):
        local = slot - seg * span
        inside = (local >= 0) & (local < span)
        target = jnp.where(inside, local, span).reshape(-1).astype(jnp.int32)
        buffer = jnp.zeros((span, BLOCK_ROWS * width), jnp.float32).at[target].set(flat_blocks, mode="drop")
        marks = jnp.zeros((span, BLOCK_ROWS), jnp.float32).at[target].set(1.0, mode="drop")
        keys_all = buffer.reshape(span * BLOCK_ROWS, width)
        valid = marks.reshape(-1) > 0.5
        key_heads = keys_all[:, :KV_HEADS * HEAD_DIM].reshape(-1, KV_HEADS, HEAD_DIM)
        value_heads = keys_all[:, KV_HEADS * HEAD_DIM:].reshape(-1, KV_HEADS, HEAD_DIM)
        rows = lax.dynamic_slice_in_dim(text_queries, seg * N_BLK * QROWS, N_BLK * QROWS, 0)
        query_heads = rows.reshape(-1, KV_HEADS, group, HEAD_DIM)
        scores = jnp.einsum("rgjd,kgd->rgjk", query_heads, key_heads, precision=lax.Precision.HIGHEST) * scale
        scores = jnp.where(valid[None, None, None, :], scores, -1e30)
        weights = jax.nn.softmax(scores, axis=-1)
        result = jnp.einsum("rgjk,kgd->rgjd", weights, value_heads, precision=lax.Precision.HIGHEST)
        return result.reshape(N_BLK * QROWS, HEADS * HEAD_DIM)

    results = lax.map(segment, jnp.arange(N_GRP, dtype=jnp.int32))
    return results.reshape(TEXT, HEADS * HEAD_DIM)
```

```python
import functools
import math

import jax
import jax.numpy as jnp
from jax import lax
from jax.experimental import pallas as pl
from jax.experimental.pallas import tpu as pltpu
from jax.sharding import PartitionSpec as P

HEADS = 28
KV_HEADS = 4
GROUP = HEADS // KV_HEADS
LANES = 128
HALVES = 2
CAPS = (3, 2)
BIAS = -(2.0**99)
ROWS8 = 8


def project_and_pack(placement, visual, kv_weight, caps, segments):
    rows, dv = visual.shape
    width = kv_weight.shape[1]
    blocks = placement.shape[0]
    block_rows = rows // blocks
    owners = KV_HEADS * HALVES
    tile = 2 * LANES
    steps = width // tile
    starts = [sum(caps[:i]) for i in range(len(caps))]

    def body(owner_ref, x_ref, w_ref, *rest):
        outs, (buf, count, sem) = rest[: len(caps)], rest[len(caps) :]
        n = pl.program_id(0)
        part = jnp.dot(x_ref[...], w_ref[...], preferred_element_type=jnp.float32)
        kind = n // (steps // 2)
        head = 2 * (n % (steps // 2))
        buf[head, kind] = part[:, :LANES]
        buf[head + 1, kind] = part[:, LANES:]

        @pl.when(n == steps - 1)
        def _():
            def clear(g, c):
                count[g] = 0
                return c

            lax.fori_loop(0, segments, clear, 0)

            def send(j, c):
                seg = owner_ref[j] // owners
                rank = count[seg]
                count[seg] = rank + 1
                half = rank % HALVES
                slot = rank // HALVES
                src = buf.at[:, :, pl.ds(pl.multiple_of(j * block_rows, ROWS8), block_rows), :]
                for out, start, cap in zip(outs, starts, caps):

                    @pl.when((slot >= start) & (slot < start + cap))
                    def _():
                        at = pl.multiple_of((slot - start) * block_rows, ROWS8)
                        dst = out.at[seg, :, half, :, pl.ds(at, block_rows), :]
                        pltpu.make_async_copy(src, dst, sem).start()

                return c

            lax.fori_loop(0, blocks, send, 0)
            pltpu.make_async_copy(buf, buf, sem).wait()

    shapes = [
        jax.ShapeDtypeStruct((segments, KV_HEADS, HALVES, 2, cap * block_rows, LANES), jnp.float32)
        for cap in caps
    ]
    return pl.pallas_call(
        body,
        out_shape=shapes,
        grid_spec=pltpu.PrefetchScalarGridSpec(
            num_scalar_prefetch=1,
            grid=(steps,),
            in_specs=[
                pl.BlockSpec((rows, dv), lambda n, o: (0, 0)),
                pl.BlockSpec((dv, tile), lambda n, o: (0, n)),
            ],
            out_specs=[pl.BlockSpec(memory_space=pl.ANY) for _ in caps],
            scratch_shapes=[
                pltpu.VMEM((KV_HEADS, 2, rows, LANES), jnp.float32),
                pltpu.SMEM((segments,), jnp.int32),
                pltpu.SemaphoreType.DMA(()),
            ],
        ),
        compiler_params=pltpu.CompilerParams(vmem_limit_bytes=40 * 2**20),
        name="project_and_pack",
    )(placement, visual, kv_weight)


def split_queries(q):
    sources, rows, width = q.shape
    group = width // LANES
    every = sources * rows
    scale = LANES ** (-0.5) * math.log2(math.e)

    def body(q_ref, o_ref):
        ones = (lax.broadcasted_iota(jnp.int32, (every, LANES), 1) == 0).astype(jnp.float32)
        ones = ones.astype(jnp.bfloat16)
        for j in range(group):
            x = q_ref[:, :, j * LANES : (j + 1) * LANES].reshape(every, LANES) * scale
            hi = x.astype(jnp.bfloat16)
            lo = (x - hi.astype(jnp.float32)).astype(jnp.bfloat16)
            o_ref[j, :, 0 * LANES : 1 * LANES] = hi
            o_ref[j, :, 1 * LANES : 2 * LANES] = lo
            o_ref[j, :, 2 * LANES : 3 * LANES] = hi
            o_ref[j, :, 3 * LANES : 4 * LANES] = ones

    return pl.pallas_call(
        body,
        out_shape=jax.ShapeDtypeStruct((group, every, 4 * LANES), jnp.bfloat16),
        compiler_params=pltpu.CompilerParams(vmem_limit_bytes=30 * 2**20),
        name="split_queries",
    )(q)


def attend(state, queries, kv, valid_rows, rows):
    group, every, depth = queries.shape
    sources, _, slots, _ = kv.shape
    take = 32
    while sources % take:
        take //= 2
    keys = take * slots
    steps = sources // take
    first = state is None
    owners = every // rows
    columns = (group + 1) * LANES

    def body(*refs):
        if first:
            q_ref, kv_ref, n_ref, o_ref, m_s, l_s, acc_s, k_s, v_s = refs
        else:
            s_ref, q_ref, kv_ref, n_ref, o_ref, m_s, l_s, acc_s, k_s, v_s = refs
        step = pl.program_id(0)

        @pl.when(step == 0)
        def _():
            if first:
                m_s[...] = jnp.full(m_s.shape, BIAS, jnp.float32)
                l_s[...] = jnp.zeros(l_s.shape, jnp.float32)
                acc_s[...] = jnp.zeros(acc_s.shape, jnp.float32)
            else:
                stats = s_ref[:, :, group * LANES :].reshape(every, LANES)
                lane0 = lax.broadcasted_iota(jnp.int32, (every, LANES), 1) == 0
                for j in range(group):
                    acc_s[j] = s_ref[:, :, j * LANES : (j + 1) * LANES].reshape(every, LANES)
                    m_s[j] = jnp.broadcast_to(stats[:, j : j + 1], (every, LANES))
                    total = jnp.broadcast_to(
                        stats[:, LANES // 2 + j : LANES // 2 + j + 1], (every, LANES)
                    )
                    l_s[j] = jnp.where(lane0, total, 0.0)

        live = lax.broadcasted_iota(jnp.int32, (take, slots, LANES), 1) < n_ref[...]
        key = jnp.where(live, kv_ref[:, 0], 0.0).reshape(keys, LANES)
        value = jnp.where(live, kv_ref[:, 1], 0.0).reshape(keys, LANES)
        lane = lax.broadcasted_iota(jnp.int32, (take, slots, LANES), 2)
        bias = jnp.where(live | (lane != 0), 0.0, BIAS).reshape(keys, LANES)
        k_hi = key.astype(jnp.bfloat16)
        k_s[:, 0 * LANES : 1 * LANES] = k_hi
        k_s[:, 1 * LANES : 2 * LANES] = k_hi
        k_s[:, 2 * LANES : 3 * LANES] = (key - k_hi.astype(jnp.float32)).astype(jnp.bfloat16)
        k_s[:, 3 * LANES : 4 * LANES] = bias.astype(jnp.bfloat16)
        v_hi = value.astype(jnp.bfloat16)
        v_s[:, :LANES] = v_hi
        v_s[:, LANES:] = (value - v_hi.astype(jnp.float32)).astype(jnp.bfloat16)

        for j in range(group):
            scores = lax.dot_general(
                q_ref[j], k_s[...], (((1,), (1,)), ((), ())), preferred_element_type=jnp.float32
            )
            old = m_s[j]
            fresh = jnp.maximum(old, jnp.max(scores, axis=1, keepdims=True))
            factor = jnp.exp2(old - fresh)
            weights = jnp.exp2(scores - jnp.tile(fresh, (1, keys // LANES)))
            sums = weights[:, :LANES]
            for t in range(1, keys // LANES):
                sums = sums + weights[:, t * LANES : (t + 1) * LANES]
            l_s[j] = l_s[j] * factor + sums
            m_s[j] = fresh
            w_hi = weights.astype(jnp.bfloat16)
            w_lo = (weights - w_hi.astype(jnp.float32)).astype(jnp.bfloat16)
            both = jnp.dot(w_hi, v_s[...], preferred_element_type=jnp.float32)
            rest = jnp.dot(w_lo, v_s[:, :LANES], preferred_element_type=jnp.float32)
            acc_s[j] = acc_s[j] * factor + (both[:, :LANES] + both[:, LANES:] + rest)

        @pl.when(step == steps - 1)
        def _():
            lane = lax.broadcasted_iota(jnp.int32, (every, LANES), 1)
            stats = jnp.zeros((every, LANES), jnp.float32)
            for j in range(group):
                o_ref[:, :, j * LANES : (j + 1) * LANES] = acc_s[j].reshape(owners, rows, LANES)
                total = jnp.sum(l_s[j], axis=1, keepdims=True)
                stats = jnp.where(lane == j, m_s[j], stats)
                stats = jnp.where(lane == LANES // 2 + j, total, stats)
            o_ref[:, :, group * LANES :] = stats.reshape(owners, rows, LANES)

    state_spec = pl.BlockSpec((owners, rows, columns), lambda i: (0, 0, 0))
    in_specs = [
        pl.BlockSpec((group, every, depth), lambda i: (0, 0, 0)),
        pl.BlockSpec((take, 2, slots, LANES), lambda i: (i, 0, 0, 0)),
        pl.BlockSpec((take, 1, LANES), lambda i: (i, 0, 0)),
    ]
    args = (queries, kv, valid_rows)
    if not first:
        in_specs = [state_spec] + in_specs
        args = (state,) + args
    return pl.pallas_call(
        body,
        out_shape=jax.ShapeDtypeStruct((owners, rows, columns), jnp.float32),
        grid=(steps,),
        in_specs=in_specs,
        out_specs=state_spec,
        scratch_shapes=[
            pltpu.VMEM((group, every, LANES), jnp.float32),
            pltpu.VMEM((group, every, LANES), jnp.float32),
            pltpu.VMEM((group, every, LANES), jnp.float32),
            pltpu.VMEM((keys, 4 * LANES), jnp.bfloat16),
            pltpu.VMEM((keys, 2 * LANES), jnp.bfloat16),
        ],
        compiler_params=pltpu.CompilerParams(vmem_limit_bytes=50 * 2**20),
        name="attend_first" if first else "attend_more",
    )(*args)


def combine(parts):
    owners, rows, columns = parts.shape
    group = columns // LANES - 1

    def body(x_ref, o_ref):
        for h in range(owners // HALVES):
            a, b = HALVES * h, HALVES * h + 1
            stats_a = x_ref[a, :, group * LANES :]
            stats_b = x_ref[b, :, group * LANES :]
            peak = jnp.maximum(stats_a, stats_b)
            fa, fb = jnp.exp2(stats_a - peak), jnp.exp2(stats_b - peak)
            total = pltpu.roll(stats_a, LANES // 2, 1) * fa + pltpu.roll(stats_b, LANES // 2, 1) * fb
            fa, fb = fa / total, fb / total
            for j in range(group):
                cols = slice(j * LANES, (j + 1) * LANES)
                out = x_ref[a, :, cols] * fa[:, j : j + 1] + x_ref[b, :, cols] * fb[:, j : j + 1]
                o_ref[:, (h * group + j) * LANES : (h * group + j + 1) * LANES] = out

    return pl.pallas_call(
        body,
        out_shape=jax.ShapeDtypeStruct((rows, owners // HALVES * group * LANES), jnp.float32),
        compiler_params=pltpu.CompilerParams(vmem_limit_bytes=20 * 2**20),
        name="combine",
    )(parts)


def on_device(visual, text_queries, kv_weight, placement):
    axes = ("grp", "blk")
    segments = lax.axis_size("grp")
    owners = lax.axis_size("blk")
    devices = segments * owners
    blocks = placement.shape[0]
    block_rows = visual.shape[0] // blocks
    rows = text_queries.shape[0]
    per_pair = max(2, blocks // devices + 1)
    most = owners * per_pair // HALVES
    caps = CAPS + (most - sum(CAPS),)

    table = lax.all_gather(placement.reshape(1, blocks), axes, axis=0, tiled=True)
    segment_of = table // owners
    hits = (segment_of[:, None, :] == jnp.arange(segments, dtype=jnp.int32)[None, :, None])
    named = jnp.sum(hits.astype(jnp.int32), axis=2)
    overflow = jnp.max(named) > HALVES * sum(CAPS)
    mine = jnp.sum((segment_of == lax.axis_index("grp")).astype(jnp.int32), axis=1)
    half = lax.axis_index("blk") % HALVES
    held = (mine + (HALVES - 1) - half) // HALVES

    q = text_queries.reshape(rows, KV_HEADS, -1).transpose(1, 0, 2)
    q = jnp.broadcast_to(q[:, None], (KV_HEADS, HALVES, *q.shape[1:]))
    q = q.reshape(owners, rows, -1)
    q = lax.all_to_all(q, "blk", 0, 0, tiled=True)

    packed = project_and_pack(placement.reshape(blocks), visual, kv_weight, caps, segments)

    def exchange(chunk):
        chunk = chunk.reshape(devices, 2, -1, LANES)
        return lax.all_to_all(chunk, axes, 0, 0, tiled=True)

    def live(i):
        count = jnp.clip(held - sum(caps[:i]), 0, caps[i]) * block_rows
        return jnp.broadcast_to(count[:, None, None], (devices, 1, LANES))

    queries = split_queries(q)
    first = exchange(packed[0])
    second = exchange(packed[1])
    state = attend(None, queries, first, live(0), rows)
    state = attend(state, queries, second, live(1), rows)
    state = lax.cond(
        overflow,
        lambda s: attend(s, queries, exchange(packed[2]), live(2), rows),
        lambda s: s,
        state,
    )
    parts = lax.all_to_all(state, "blk", 0, 0, tiled=True)
    return combine(parts)


def solution(mesh):
    placed = (P(("grp", "blk"), None), P(("grp", "blk"), None), P(), P(("grp", "blk"), None))
    return jax.shard_map(
        on_device, mesh=mesh, in_specs=placed, out_specs=P(("grp", "blk"), None), check_vma=False
    )
```

```python
import functools
import math

import jax
import jax.numpy as jnp
from jax import lax
from jax.experimental import pallas as pl
from jax.experimental.pallas import tpu as pltpu
from jax.sharding import PartitionSpec as P

HEADS = 28
KV_HEADS = 4
GROUP = HEADS // KV_HEADS
LANES = 128
HALVES = 2
CAPS = (4, 1)
BIAS = -(2.0**99)
ROWS8 = 8
TILE = 1024


def project_and_pack(placement, visual, kv_weight, caps, segments):
    rows, dv = visual.shape
    width = kv_weight.shape[1]
    blocks = placement.shape[0]
    block_rows = rows // blocks
    owners = KV_HEADS * HALVES
    tile = 2 * LANES
    steps = width // tile
    starts = [sum(caps[:i]) for i in range(len(caps))]

    def body(owner_ref, x_ref, w_ref, *rest):
        outs, (buf, count, sem) = rest[: len(caps)], rest[len(caps) :]
        n = pl.program_id(0)
        part = jnp.dot(x_ref[...], w_ref[...], preferred_element_type=jnp.float32)
        kind = n // (steps // 2)
        head = 2 * (n % (steps // 2))
        buf[head, kind] = part[:, :LANES]
        buf[head + 1, kind] = part[:, LANES:]

        @pl.when(n == steps - 1)
        def _():
            def clear(g, c):
                count[g] = 0
                return c

            lax.fori_loop(0, segments, clear, 0)

            def send(j, c):
                seg = owner_ref[j] // owners
                rank = count[seg]
                count[seg] = rank + 1
                half = rank % HALVES
                slot = rank // HALVES
                src = buf.at[:, :, pl.ds(pl.multiple_of(j * block_rows, ROWS8), block_rows), :]
                for out, start, cap in zip(outs, starts, caps):

                    @pl.when((slot >= start) & (slot < start + cap))
                    def _():
                        at = pl.multiple_of((slot - start) * block_rows, ROWS8)
                        dst = out.at[seg, :, half, :, pl.ds(at, block_rows), :]
                        pltpu.make_async_copy(src, dst, sem).start()

                return c

            lax.fori_loop(0, blocks, send, 0)
            pltpu.make_async_copy(buf, buf, sem).wait()

    shapes = [
        jax.ShapeDtypeStruct((segments, KV_HEADS, HALVES, 2, cap * block_rows, LANES), jnp.float32)
        for cap in caps
    ]
    return pl.pallas_call(
        body,
        out_shape=shapes,
        grid_spec=pltpu.PrefetchScalarGridSpec(
            num_scalar_prefetch=1,
            grid=(steps,),
            in_specs=[
                pl.BlockSpec((rows, dv), lambda n, o: (0, 0)),
                pl.BlockSpec((dv, tile), lambda n, o: (0, n)),
            ],
            out_specs=[pl.BlockSpec(memory_space=pltpu.HBM) for _ in caps],
            scratch_shapes=[
                pltpu.VMEM((KV_HEADS, 2, rows, LANES), jnp.float32),
                pltpu.SMEM((segments,), jnp.int32),
                pltpu.SemaphoreType.DMA(()),
            ],
        ),
        compiler_params=pltpu.CompilerParams(vmem_limit_bytes=40 * 2**20),
        name="project_and_pack",
    )(placement, visual, kv_weight)


def split_queries(q):
    sources, rows, width = q.shape
    group = width // LANES
    every = sources * rows
    scale = LANES ** (-0.5) * math.log2(math.e)

    def body(q_ref, o_ref):
        ones = (lax.broadcasted_iota(jnp.int32, (every, LANES), 1) == 0).astype(jnp.float32)
        ones = ones.astype(jnp.bfloat16)
        for j in range(group):
            x = q_ref[:, :, j * LANES : (j + 1) * LANES].reshape(every, LANES) * scale
            hi = x.astype(jnp.bfloat16)
            lo = (x - hi.astype(jnp.float32)).astype(jnp.bfloat16)
            o_ref[j, :, 0 * LANES : 1 * LANES] = hi
            o_ref[j, :, 1 * LANES : 2 * LANES] = lo
            o_ref[j, :, 2 * LANES : 3 * LANES] = hi
            o_ref[j, :, 3 * LANES : 4 * LANES] = ones

    return pl.pallas_call(
        body,
        out_shape=jax.ShapeDtypeStruct((group, every, 4 * LANES), jnp.bfloat16),
        compiler_params=pltpu.CompilerParams(vmem_limit_bytes=30 * 2**20),
        name="split_queries",
    )(q)


def attend(state, queries, kv, valid_rows, rows):
    group, every, depth = queries.shape
    sources, _, slots, _ = kv.shape
    take = min(sources, 1 << (TILE // slots).bit_length() - 1)
    while sources % take:
        take //= 2
    keys = take * slots
    steps = sources // take
    first = state is None
    owners = every // rows
    columns = (group + 1) * LANES

    def body(*refs):
        if first:
            q_ref, kv_ref, n_ref, o_ref, m_s, l_s, acc_s, k_s, v_s = refs
        else:
            s_ref, q_ref, kv_ref, n_ref, o_ref, m_s, l_s, acc_s, k_s, v_s = refs
        step = pl.program_id(0)

        @pl.when(step == 0)
        def _():
            if first:
                m_s[...] = jnp.full(m_s.shape, BIAS, jnp.float32)
                l_s[...] = jnp.zeros(l_s.shape, jnp.float32)
                acc_s[...] = jnp.zeros(acc_s.shape, jnp.float32)
            else:
                stats = s_ref[:, :, group * LANES :].reshape(every, LANES)
                lane0 = lax.broadcasted_iota(jnp.int32, (every, LANES), 1) == 0
                for j in range(group):
                    acc_s[j] = s_ref[:, :, j * LANES : (j + 1) * LANES].reshape(every, LANES)
                    m_s[j] = jnp.broadcast_to(stats[:, j : j + 1], (every, LANES))
                    total = jnp.broadcast_to(
                        stats[:, LANES // 2 + j : LANES // 2 + j + 1], (every, LANES)
                    )
                    l_s[j] = jnp.where(lane0, total, 0.0)

        live = lax.broadcasted_iota(jnp.int32, (take, slots, LANES), 1) < n_ref[...]
        key = jnp.where(live, kv_ref[:, 0], 0.0).reshape(keys, LANES)
        value = jnp.where(live, kv_ref[:, 1], 0.0).reshape(keys, LANES)
        lane = lax.broadcasted_iota(jnp.int32, (take, slots, LANES), 2)
        bias = jnp.where(live | (lane != 0), 0.0, BIAS).reshape(keys, LANES)
        k_hi = key.astype(jnp.bfloat16)
        k_s[:, 0 * LANES : 1 * LANES] = k_hi
        k_s[:, 1 * LANES : 2 * LANES] = k_hi
        k_s[:, 2 * LANES : 3 * LANES] = (key - k_hi.astype(jnp.float32)).astype(jnp.bfloat16)
        k_s[:, 3 * LANES : 4 * LANES] = bias.astype(jnp.bfloat16)
        v_hi = value.astype(jnp.bfloat16)
        v_s[:, :LANES] = v_hi
        v_s[:, LANES:] = (value - v_hi.astype(jnp.float32)).astype(jnp.bfloat16)

        for j in range(group):
            scores = lax.dot_general(
                q_ref[j], k_s[...], (((1,), (1,)), ((), ())), preferred_element_type=jnp.float32
            )
            old = m_s[j]
            fresh = jnp.maximum(old, jnp.max(scores, axis=1, keepdims=True))
            factor = jnp.exp2(old - fresh)
            weights = jnp.exp2(scores - jnp.tile(fresh, (1, keys // LANES)))
            sums = weights[:, :LANES]
            for t in range(1, keys // LANES):
                sums = sums + weights[:, t * LANES : (t + 1) * LANES]
            l_s[j] = l_s[j] * factor + sums
            m_s[j] = fresh
            w_hi = weights.astype(jnp.bfloat16)
            w_lo = (weights - w_hi.astype(jnp.float32)).astype(jnp.bfloat16)
            both = jnp.dot(w_hi, v_s[...], preferred_element_type=jnp.float32)
            rest = jnp.dot(w_lo, v_s[:, :LANES], preferred_element_type=jnp.float32)
            acc_s[j] = acc_s[j] * factor + (both[:, :LANES] + both[:, LANES:] + rest)

        @pl.when(step == steps - 1)
        def _():
            lane = lax.broadcasted_iota(jnp.int32, (every, LANES), 1)
            stats = jnp.zeros((every, LANES), jnp.float32)
            for j in range(group):
                o_ref[:, :, j * LANES : (j + 1) * LANES] = acc_s[j].reshape(owners, rows, LANES)
                total = jnp.sum(l_s[j], axis=1, keepdims=True)
                stats = jnp.where(lane == j, m_s[j], stats)
                stats = jnp.where(lane == LANES // 2 + j, total, stats)
            o_ref[:, :, group * LANES :] = stats.reshape(owners, rows, LANES)

    state_spec = pl.BlockSpec((owners, rows, columns), lambda i: (0, 0, 0))
    in_specs = [
        pl.BlockSpec((group, every, depth), lambda i: (0, 0, 0)),
        pl.BlockSpec((take, 2, slots, LANES), lambda i: (i, 0, 0, 0)),
        pl.BlockSpec((take, 1, LANES), lambda i: (i, 0, 0)),
    ]
    args = (queries, kv, valid_rows)
    if not first:
        in_specs = [state_spec] + in_specs
        args = (state,) + args
    return pl.pallas_call(
        body,
        out_shape=jax.ShapeDtypeStruct((owners, rows, columns), jnp.float32),
        grid=(steps,),
        in_specs=in_specs,
        out_specs=state_spec,
        scratch_shapes=[
            pltpu.VMEM((group, every, LANES), jnp.float32),
            pltpu.VMEM((group, every, LANES), jnp.float32),
            pltpu.VMEM((group, every, LANES), jnp.float32),
            pltpu.VMEM((keys, 4 * LANES), jnp.bfloat16),
            pltpu.VMEM((keys, 2 * LANES), jnp.bfloat16),
        ],
        compiler_params=pltpu.CompilerParams(vmem_limit_bytes=50 * 2**20),
        name="attend_first" if first else "attend_more",
    )(*args)


def combine(parts):
    owners, rows, columns = parts.shape
    group = columns // LANES - 1

    def body(x_ref, o_ref):
        for h in range(owners // HALVES):
            a, b = HALVES * h, HALVES * h + 1
            stats_a = x_ref[a, :, group * LANES :]
            stats_b = x_ref[b, :, group * LANES :]
            peak = jnp.maximum(stats_a, stats_b)
            fa, fb = jnp.exp2(stats_a - peak), jnp.exp2(stats_b - peak)
            total = pltpu.roll(stats_a, LANES // 2, 1) * fa + pltpu.roll(stats_b, LANES // 2, 1) * fb
            fa, fb = fa / total, fb / total
            for j in range(group):
                cols = slice(j * LANES, (j + 1) * LANES)
                out = x_ref[a, :, cols] * fa[:, j : j + 1] + x_ref[b, :, cols] * fb[:, j : j + 1]
                o_ref[:, (h * group + j) * LANES : (h * group + j + 1) * LANES] = out

    return pl.pallas_call(
        body,
        out_shape=jax.ShapeDtypeStruct((rows, owners // HALVES * group * LANES), jnp.float32),
        compiler_params=pltpu.CompilerParams(vmem_limit_bytes=20 * 2**20),
        name="combine",
    )(parts)


def on_device(visual, text_queries, kv_weight, placement):
    axes = ("grp", "blk")
    segments = lax.axis_size("grp")
    owners = lax.axis_size("blk")
    devices = segments * owners
    blocks = placement.shape[0]
    block_rows = visual.shape[0] // blocks
    rows = text_queries.shape[0]
    per_pair = max(2, blocks // devices + 1)
    most = owners * per_pair // HALVES
    caps = CAPS + (most - sum(CAPS),)

    row = jnp.pad(placement.reshape(1, blocks), ((0, ROWS8 - 1), (0, -blocks % LANES)))
    table = lax.all_gather(row.astype(jnp.float32), axes, axis=0, tiled=True)
    table = table.reshape(devices, ROWS8, -1)[:, 0, :blocks]
    segment_of = table.astype(jnp.int32) // owners
    hits = (segment_of[:, None, :] == jnp.arange(segments, dtype=jnp.int32)[None, :, None])
    named = jnp.sum(hits.astype(jnp.int32), axis=2)
    overflow = jnp.max(named) > HALVES * sum(CAPS)
    mine = jnp.sum((segment_of == lax.axis_index("grp")).astype(jnp.int32), axis=1)
    half = lax.axis_index("blk") % HALVES
    held = (mine + (HALVES - 1) - half) // HALVES

    q = text_queries.reshape(rows, KV_HEADS, -1).transpose(1, 0, 2)
    q = jnp.broadcast_to(q[:, None], (KV_HEADS, HALVES, *q.shape[1:]))
    q = q.reshape(owners, rows, -1)
    q = lax.all_to_all(q, "blk", 0, 0, tiled=True)

    packed = project_and_pack(placement.reshape(blocks), visual, kv_weight, caps, segments)

    def exchange(chunk):
        chunk = chunk.reshape(devices, 2, -1, LANES)
        return lax.all_to_all(chunk, axes, 0, 0, tiled=True)

    def live(i):
        count = jnp.clip(held - sum(caps[:i]), 0, caps[i]) * block_rows
        return jnp.broadcast_to(count[:, None, None], (devices, 1, LANES))

    queries = split_queries(q)
    first = exchange(packed[0])
    second = exchange(packed[1])
    state = attend(None, queries, first, live(0), rows)
    state = attend(state, queries, second, live(1), rows)
    state = lax.cond(
        overflow,
        lambda s: attend(s, queries, exchange(packed[2]), live(2), rows),
        lambda s: s,
        state,
    )
    parts = lax.all_to_all(state, "blk", 0, 0, tiled=True)
    return combine(parts)


def solution(mesh):
    placed = (P(("grp", "blk"), None), P(("grp", "blk"), None), P(), P(("grp", "blk"), None))
    return jax.shard_map(
        on_device, mesh=mesh, in_specs=placed, out_specs=P(("grp", "blk"), None), check_vma=False
    )
```

```python
import functools
import math

import jax
import jax.numpy as jnp
from jax import lax
from jax.experimental import pallas as pl
from jax.experimental.pallas import tpu as pltpu
from jax.sharding import PartitionSpec as P

HEADS = 28
KV_HEADS = 4
GROUP = HEADS // KV_HEADS
LANES = 128
HALVES = 2
CAPS = (4, 1)
SPARE = 1
BIAS = -(2.0**99)
EMPTY = (1e30, 4e30, 16e30)
LIVE_BELOW = 1e29
ROWS8 = 8
TILE = 1024
PART = 512


def project_and_pack(placement, visual, kv_weight, caps, segments):
    rows, dv = visual.shape
    width = kv_weight.shape[1]
    blocks = placement.shape[0]
    block_rows = rows // blocks
    owners = KV_HEADS * HALVES
    deep = 512
    while dv % deep:
        deep //= 2
    steps = dv // deep
    common = caps[0] + caps[1]

    def body(owner_ref, x_ref, w_ref, o1, o2, o3, buf, mark1, mark2, count, ranks, sem, sem1, sem2):
        n = pl.program_id(0)
        fill2 = pltpu.make_async_copy(o2.at[:, :, :, 0], o2.at[:, :, :, 0], sem2)
        fill1 = pltpu.make_async_copy(o1.at[:, :, :, 0], o1.at[:, :, :, 0], sem1)

        @pl.when(n == 0)
        def _():
            def clear(g, c):
                count[g] = 0
                return c

            def rank(j, top):
                seg = owner_ref[j] // owners
                r = count[seg]
                count[seg] = r + 1
                ranks[j] = r
                return jnp.maximum(top, r + 1)

            lax.fori_loop(0, segments, clear, 0)
            top = lax.fori_loop(0, blocks, rank, 0)
            level = (top > HALVES * common).astype(jnp.int32)
            level = level + (top > HALVES * (common + SPARE)).astype(jnp.int32)
            count[segments] = level
            mark1[...] = jnp.full(mark1.shape, EMPTY[0], jnp.float32)
            mark = jnp.where(level == 0, EMPTY[0], jnp.where(level == 1, EMPTY[1], EMPTY[2]))
            mark2[...] = jnp.broadcast_to(mark.astype(jnp.float32), mark2.shape)

            def fill(g, c):
                pltpu.make_async_copy(mark1, o1.at[g, :, :, 0], sem1).start()
                pltpu.make_async_copy(mark2, o2.at[g, :, :, 0], sem2).start()
                return c

            lax.fori_loop(0, segments, fill, 0)

        part = jnp.dot(x_ref[...], w_ref[...], preferred_element_type=jnp.float32)
        for kind in range(2):
            for h in range(KV_HEADS):
                c = (kind * KV_HEADS + h) * LANES
                piece = part[:, c : c + LANES]

                @pl.when(n == 0)
                def _():
                    buf[h, kind] = piece

                @pl.when(n > 0)
                def _():
                    buf[h, kind] += piece

        @pl.when(n == steps - 1)
        def _():
            fill1.wait()
            fill2.wait()
            level = count[segments]

            def send(j, c):
                seg = owner_ref[j] // owners
                r = ranks[j]
                half = r % HALVES
                slot = r // HALVES
                src = buf.at[:, :, pl.ds(pl.multiple_of(j * block_rows, ROWS8), block_rows), :]

                def copy(out, at):
                    at = pl.multiple_of(at * block_rows, ROWS8)
                    dst = out.at[seg, :, half, :, pl.ds(at, block_rows), :]
                    pltpu.make_async_copy(src, dst, sem).start()

                @pl.when(slot < caps[0])
                def _():
                    copy(o1, slot)

                @pl.when((slot >= caps[0]) & (level == 0))
                def _():
                    copy(o2, slot - caps[0])

                @pl.when((slot >= caps[0]) & (level > 0))
                def _():
                    copy(o3, slot - caps[0])

                return c

            lax.fori_loop(0, blocks, send, 0)
            pltpu.make_async_copy(buf, buf, sem).wait()

    shapes = [
        pltpu.HBM((segments, KV_HEADS, HALVES, 2, cap * block_rows, LANES), jnp.float32)
        for cap in caps
    ]
    return pl.pallas_call(
        body,
        out_shape=shapes,
        grid_spec=pltpu.PrefetchScalarGridSpec(
            num_scalar_prefetch=1,
            grid=(steps,),
            in_specs=[
                pl.BlockSpec((rows, deep), lambda n, o: (0, n)),
                pl.BlockSpec((deep, width), lambda n, o: (n, 0)),
            ],
            out_specs=[pl.BlockSpec(memory_space=pltpu.HBM) for _ in caps],
            scratch_shapes=[
                pltpu.VMEM((KV_HEADS, 2, rows, LANES), jnp.float32),
                pltpu.VMEM((KV_HEADS, HALVES, caps[0] * block_rows, LANES), jnp.float32),
                pltpu.VMEM((KV_HEADS, HALVES, caps[1] * block_rows, LANES), jnp.float32),
                pltpu.SMEM((segments + 1,), jnp.int32),
                pltpu.SMEM((blocks,), jnp.int32),
                pltpu.SemaphoreType.DMA(()),
                pltpu.SemaphoreType.DMA(()),
                pltpu.SemaphoreType.DMA(()),
            ],
        ),
        compiler_params=pltpu.CompilerParams(vmem_limit_bytes=40 * 2**20),
        name="project_and_pack",
    )(
        placement,
        pltpu.with_memory_space_constraint(visual, pltpu.HBM),
        pltpu.with_memory_space_constraint(kv_weight, pltpu.HBM),
    )


def split_queries(q):
    sources, rows, width = q.shape
    group = width // LANES
    every = sources * rows
    scale = LANES ** (-0.5) * math.log2(math.e)

    def body(q_ref, o_ref):
        ones = (lax.broadcasted_iota(jnp.int32, (every, LANES), 1) == 0).astype(jnp.float32)
        ones = ones.astype(jnp.bfloat16)
        for j in range(group):
            x = q_ref[:, :, j * LANES : (j + 1) * LANES].reshape(every, LANES) * scale
            hi = x.astype(jnp.bfloat16)
            lo = (x - hi.astype(jnp.float32)).astype(jnp.bfloat16)
            o_ref[j, :, 0 * LANES : 1 * LANES] = hi
            o_ref[j, :, 1 * LANES : 2 * LANES] = lo
            o_ref[j, :, 2 * LANES : 3 * LANES] = hi
            o_ref[j, :, 3 * LANES : 4 * LANES] = ones

    return pl.pallas_call(
        body,
        out_shape=jax.ShapeDtypeStruct((group, every, 4 * LANES), jnp.bfloat16),
        compiler_params=pltpu.CompilerParams(vmem_limit_bytes=30 * 2**20),
        name="split_queries",
    )(q)


def attend(state, queries, kv, rows, with_mark=False):
    group, every, depth = queries.shape
    sources, _, slots, _ = kv.shape
    take = min(sources, 1 << (TILE // slots).bit_length() - 1)
    while sources % take:
        take //= 2
    keys = take * slots
    part = PART
    while keys % part:
        part //= 2
    steps = sources // take
    first = state is None
    owners = every // rows
    columns = (group + 1) * LANES

    def body(*refs):
        refs = list(refs)
        s_ref = None if first else refs.pop(0)
        q_ref, kv_ref, o_ref = refs[:3]
        f_ref = refs[3] if with_mark else None
        m_s, l_s, acc_s, k_s, v_s = refs[-5:]
        step = pl.program_id(0)

        @pl.when(step == 0)
        def _():
            if first:
                m_s[...] = jnp.full(m_s.shape, BIAS, jnp.float32)
                l_s[...] = jnp.zeros(l_s.shape, jnp.float32)
                acc_s[...] = jnp.zeros(acc_s.shape, jnp.float32)
            else:
                stats = s_ref[:, :, group * LANES :].reshape(every, LANES)
                lane0 = lax.broadcasted_iota(jnp.int32, (every, LANES), 1) == 0
                for j in range(group):
                    acc_s[j] = s_ref[:, :, j * LANES : (j + 1) * LANES].reshape(every, LANES)
                    m_s[j] = jnp.broadcast_to(stats[:, j : j + 1], (every, LANES))
                    total = jnp.broadcast_to(
                        stats[:, LANES // 2 + j : LANES // 2 + j + 1], (every, LANES)
                    )
                    l_s[j] = jnp.where(lane0, total, 0.0)

        live = kv_ref[:, 0] < LIVE_BELOW
        key = jnp.where(live, kv_ref[:, 0], 0.0).reshape(keys, LANES)
        value = jnp.where(live, kv_ref[:, 1], 0.0).reshape(keys, LANES)
        lane = lax.broadcasted_iota(jnp.int32, (take, slots, LANES), 2)
        bias = jnp.where(live | (lane != 0), 0.0, BIAS).reshape(keys, LANES)
        k_hi = key.astype(jnp.bfloat16)
        k_s[:, 0 * LANES : 1 * LANES] = k_hi
        k_s[:, 1 * LANES : 2 * LANES] = k_hi
        k_s[:, 2 * LANES : 3 * LANES] = (key - k_hi.astype(jnp.float32)).astype(jnp.bfloat16)
        k_s[:, 3 * LANES : 4 * LANES] = bias.astype(jnp.bfloat16)
        v_hi = value.astype(jnp.bfloat16)
        v_s[:, :LANES] = v_hi
        v_s[:, LANES:] = (value - v_hi.astype(jnp.float32)).astype(jnp.bfloat16)
        if with_mark:
            mark = jnp.max(jnp.max(kv_ref[:, 0].reshape(keys, LANES), axis=0, keepdims=True))
            mark = jnp.broadcast_to(mark, f_ref.shape)

            @pl.when(step == 0)
            def _():
                f_ref[...] = mark

            @pl.when(step > 0)
            def _():
                f_ref[...] = jnp.maximum(f_ref[...], mark)

        def score(t, j):
            return lax.dot_general(
                q_ref[j],
                k_s[t * part : (t + 1) * part],
                (((1,), (1,)), ((), ())),
                preferred_element_type=jnp.float32,
            )

        def weigh(j, scores):
            old = m_s[j]
            fresh = jnp.maximum(old, jnp.max(scores, axis=1, keepdims=True))
            factor = jnp.exp2(old - fresh)
            weights = jnp.exp2(scores - jnp.tile(fresh, (1, part // LANES)))
            sums = weights[:, :LANES]
            for i in range(1, part // LANES):
                sums = sums + weights[:, i * LANES : (i + 1) * LANES]
            l_s[j] = l_s[j] * factor + sums
            m_s[j] = fresh
            w_hi = weights.astype(jnp.bfloat16)
            return factor, w_hi, (weights - w_hi.astype(jnp.float32)).astype(jnp.bfloat16)

        def gather(t, j, factor, w_hi, w_lo):
            at = slice(t * part, (t + 1) * part)
            both = jnp.dot(w_hi, v_s[at], preferred_element_type=jnp.float32)
            rest = jnp.dot(w_lo, v_s[at, :LANES], preferred_element_type=jnp.float32)
            acc_s[j] = acc_s[j] * factor + (both[:, :LANES] + both[:, LANES:] + rest)

        items = [(t, j) for t in range(keys // part) for j in range(group)]
        scores = score(*items[0])
        behind = None
        for n, item in enumerate(items):
            ahead = score(*items[n + 1]) if n + 1 < len(items) else None
            weighed = weigh(item[1], scores)
            if behind is not None:
                gather(*behind)
            behind = (*item, *weighed)
            scores = ahead
        gather(*behind)

        @pl.when(step == steps - 1)
        def _():
            lane = lax.broadcasted_iota(jnp.int32, (every, LANES), 1)
            stats = jnp.zeros((every, LANES), jnp.float32)
            for j in range(group):
                o_ref[:, :, j * LANES : (j + 1) * LANES] = acc_s[j].reshape(owners, rows, LANES)
                total = jnp.sum(l_s[j], axis=1, keepdims=True)
                stats = jnp.where(lane == j, m_s[j], stats)
                stats = jnp.where(lane == LANES // 2 + j, total, stats)
            o_ref[:, :, group * LANES :] = stats.reshape(owners, rows, LANES)

    state_spec = pl.BlockSpec((owners, rows, columns), lambda i: (0, 0, 0))
    in_specs = [
        pl.BlockSpec((group, every, depth), lambda i: (0, 0, 0)),
        pl.BlockSpec((take, 2, slots, LANES), lambda i: (i, 0, 0, 0)),
    ]
    args = (queries, kv)
    if not first:
        in_specs = [state_spec] + in_specs
        args = (state,) + args
    out_shape = [jax.ShapeDtypeStruct((owners, rows, columns), jnp.float32)]
    out_specs = [state_spec]
    if with_mark:
        out_shape.append(jax.ShapeDtypeStruct((ROWS8, LANES), jnp.float32))
        out_specs.append(pl.BlockSpec((ROWS8, LANES), lambda i: (0, 0)))
    out = pl.pallas_call(
        body,
        out_shape=out_shape,
        grid=(steps,),
        in_specs=in_specs,
        out_specs=out_specs,
        scratch_shapes=[
            pltpu.VMEM((group, every, LANES), jnp.float32),
            pltpu.VMEM((group, every, LANES), jnp.float32),
            pltpu.VMEM((group, every, LANES), jnp.float32),
            pltpu.VMEM((keys, 4 * LANES), jnp.bfloat16),
            pltpu.VMEM((keys, 2 * LANES), jnp.bfloat16),
        ],
        compiler_params=pltpu.CompilerParams(vmem_limit_bytes=50 * 2**20),
        name="attend_first" if first else "attend_more",
    )(*args)
    return out if with_mark else out[0]


def combine(parts):
    owners, rows, columns = parts.shape
    group = columns // LANES - 1

    def body(x_ref, o_ref):
        for h in range(owners // HALVES):
            a, b = HALVES * h, HALVES * h + 1
            stats_a = x_ref[a, :, group * LANES :]
            stats_b = x_ref[b, :, group * LANES :]
            peak = jnp.maximum(stats_a, stats_b)
            fa, fb = jnp.exp2(stats_a - peak), jnp.exp2(stats_b - peak)
            total = pltpu.roll(stats_a, LANES // 2, 1) * fa + pltpu.roll(stats_b, LANES // 2, 1) * fb
            fa, fb = fa / total, fb / total
            for j in range(group):
                cols = slice(j * LANES, (j + 1) * LANES)
                out = x_ref[a, :, cols] * fa[:, j : j + 1] + x_ref[b, :, cols] * fb[:, j : j + 1]
                o_ref[:, (h * group + j) * LANES : (h * group + j + 1) * LANES] = out

    return pl.pallas_call(
        body,
        out_shape=jax.ShapeDtypeStruct((rows, owners // HALVES * group * LANES), jnp.float32),
        compiler_params=pltpu.CompilerParams(vmem_limit_bytes=20 * 2**20),
        name="combine",
    )(parts)


def on_device(visual, text_queries, kv_weight, placement):
    axes = ("grp", "blk")
    segments = lax.axis_size("grp")
    owners = lax.axis_size("blk")
    devices = segments * owners
    blocks = placement.shape[0]
    block_rows = visual.shape[0] // blocks
    rows = text_queries.shape[0]
    per_pair = max(2, blocks // devices + 1)
    most = owners * per_pair // HALVES
    caps = CAPS + (most - CAPS[0],)
    common = sum(CAPS)

    q = text_queries.reshape(rows, KV_HEADS, -1).transpose(1, 0, 2)
    q = jnp.broadcast_to(q[:, None], (KV_HEADS, HALVES, *q.shape[1:]))
    q = q.reshape(owners, rows, -1)
    q = lax.all_to_all(q, "blk", 0, 0, tiled=True)

    owner = placement.reshape(blocks)
    packed = project_and_pack(owner, visual, kv_weight, caps, segments)

    def exchange(chunk):
        chunk = chunk.reshape(devices, 2, -1, LANES)
        return lax.all_to_all(chunk, axes, 0, 0, tiled=True)

    def beyond(slots, state):
        counts = jnp.sum(
            (owner[None, :] // owners == jnp.arange(segments)[:, None]).astype(jnp.int32), axis=1
        )
        mine = jnp.max(counts) > HALVES * common
        half = jnp.arange(HALVES)[None, :]
        held = (counts[:, None] + (HALVES - 1) - half) // HALVES - caps[0]
        held = jnp.where(mine, held, 0)[:, None, :, None, None, None]
        slot = (jnp.arange(slots * block_rows) // block_rows)[:, None]
        chunk = packed[2][:, :, :, :, : slots * block_rows]
        chunk = jnp.where(slot < held, chunk, EMPTY[0])
        return attend(state, queries, exchange(chunk), rows)

    queries = split_queries(q)
    first = exchange(packed[0])
    second = exchange(packed[1])
    state = attend(None, queries, first, rows)
    state, mark = attend(state, queries, second, rows, with_mark=True)
    mark = mark[0, 0]
    level = (mark > 2 * EMPTY[0]).astype(jnp.int32) + (mark > 2 * EMPTY[1]).astype(jnp.int32)
    state = lax.switch(
        level,
        [
            lambda s: s,
            lambda s: beyond(CAPS[1] + SPARE, s),
            lambda s: beyond(caps[2], s),
        ],
        state,
    )
    parts = lax.all_to_all(state, "blk", 0, 0, tiled=True)
    return combine(parts)


def solution(mesh):
    placed = (P(("grp", "blk"), None), P(("grp", "blk"), None), P(), P(("grp", "blk"), None))
    return jax.shard_map(
        on_device, mesh=mesh, in_specs=placed, out_specs=P(("grp", "blk"), None), check_vma=False
    )
```

```python
import functools
import math

import jax
import jax.numpy as jnp
from jax import lax
from jax.experimental import pallas as pl
from jax.experimental.pallas import tpu as pltpu
from jax.sharding import PartitionSpec as P

HEADS = 28
KV_HEADS = 4
GROUP = HEADS // KV_HEADS
LANES = 128
HALVES = 2
CAPS = (4, 1)
SPARE = 1
BIAS = -(2.0**99)
EMPTY = (1e30, 4e30, 16e30)
LIVE_BELOW = 1e29
ROWS8 = 8
TILE = 1024
PART = 512
DEPTHS = (512, 1024)


def project_and_pack(placement, visual, kv_weight, caps, segments):
    rows, dv = visual.shape
    width = kv_weight.shape[1]
    blocks = placement.shape[0]
    block_rows = rows // blocks
    owners = KV_HEADS * HALVES
    common = caps[0] + caps[1]
    cuts = [0]
    while cuts[-1] < dv:
        cuts.append(min(dv, cuts[-1] + DEPTHS[min(len(cuts) - 1, len(DEPTHS) - 1)]))
    parts = list(zip(cuts[:-1], cuts[1:]))
    few = math.gcd(segments, 4)

    def body(owner_ref, x_hbm, w_hbm, o1, o2, o3, x, w, buf, mark1, mark2, code, table, sems):
        loads = []
        for i, (a, b) in enumerate(parts):
            loads.append(
                (
                    pltpu.make_async_copy(x_hbm.at[:, a:b], x.at[:, a:b], sems.at[2 * i]),
                    pltpu.make_async_copy(w_hbm.at[a:b], w.at[a:b], sems.at[2 * i + 1]),
                )
            )
            for load in loads[-1]:
                load.start()
        sem, sem2 = (sems.at[2 * len(parts) + i] for i in range(2))
        sem1 = sems.at[2 * len(parts) + 2 :]

        segment = lax.shift_right_logical(owner_ref[...], owners.bit_length() - 1)
        segment = segment.astype(jnp.float32)
        shape = (blocks, blocks)
        i = lax.broadcasted_iota(jnp.int32, shape, 0)
        j = lax.broadcasted_iota(jnp.int32, shape, 1)
        column = jnp.broadcast_to(segment, shape)
        line = jnp.sum(jnp.where(i == j, column, 0.0), axis=0, keepdims=True)
        before = jnp.where((column == line) & (i < j), 1.0, 0.0)
        rank = jnp.sum(before, axis=0, keepdims=True)
        top = jnp.max(rank) + 1.0
        rank = rank.astype(jnp.int32)
        half = jnp.bitwise_and(rank, HALVES - 1)
        slot = lax.shift_right_logical(rank, HALVES.bit_length() - 1)
        code[...] = (line.astype(jnp.int32) * HALVES + half) * ROWS8 + slot
        codes = pltpu.make_async_copy(code, table, sem)
        codes.start()
        level = (top > HALVES * common).astype(jnp.int32)
        level = level + (top > HALVES * (common + SPARE)).astype(jnp.int32)
        mark1[...] = jnp.full(mark1.shape, EMPTY[0], jnp.float32)
        mark = jnp.where(level == 0, EMPTY[0], jnp.where(level == 1, EMPTY[1], EMPTY[2]))
        mark2[...] = jnp.broadcast_to(mark.astype(jnp.float32), mark2.shape)
        fills = [pltpu.make_async_copy(mark2, o2.at[:, :, :, 0], sem2)]
        for g in range(0, segments, mark1.shape[0]):
            to = o1.at[g : g + mark1.shape[0], :, :, 0]
            fills.append(pltpu.make_async_copy(mark1, to, sem1.at[g // mark1.shape[0]]))
        for copy in fills:
            copy.start()
        codes.wait()

        for i, (a, b) in enumerate(parts):
            for load in loads[i]:
                load.wait()
            for kind in range(2):
                for h in range(0, KV_HEADS, 2):
                    c = (kind * KV_HEADS + h) * LANES
                    part = jnp.dot(
                        x[:, a:b], w[a:b, c : c + 2 * LANES], preferred_element_type=jnp.float32
                    )
                    for k in range(2):
                        piece = part[:, k * LANES : (k + 1) * LANES]
                        buf[h + k, kind] = piece if i == 0 else buf[h + k, kind] + piece

        for copy in fills:
            copy.wait()

        def send(j, c):
            at = table[0, j]
            slot = at % ROWS8
            half = at // ROWS8 % HALVES
            seg = at // (ROWS8 * HALVES)
            src = buf.at[:, :, pl.ds(pl.multiple_of(j * block_rows, ROWS8), block_rows), :]

            def copy(out, slot):
                rows_at = pl.ds(pl.multiple_of(slot * block_rows, ROWS8), block_rows)
                dst = out.at[seg, :, half, :, rows_at, :]
                pltpu.make_async_copy(src, dst, sem).start()

            @pl.when(slot < caps[0])
            def _():
                copy(o1, slot)

            @pl.when(slot >= caps[0])
            def _():
                @pl.when(level == 0)
                def _():
                    copy(o2, slot - caps[0])

                @pl.when(level > 0)
                def _():
                    copy(o3, slot - caps[0])

            return c

        lax.fori_loop(0, blocks, send, 0, unroll=4)
        pltpu.make_async_copy(buf, buf, sem).wait()

    shapes = [
        pltpu.HBM((segments, KV_HEADS, HALVES, 2, cap * block_rows, LANES), jnp.float32)
        for cap in caps
    ]
    hbm = pl.BlockSpec(memory_space=pltpu.HBM)
    return pl.pallas_call(
        body,
        out_shape=shapes,
        in_specs=[pl.BlockSpec(memory_space=pltpu.VMEM), hbm, hbm],
        out_specs=[hbm for _ in caps],
        scratch_shapes=[
            pltpu.VMEM((rows, dv), jnp.bfloat16),
            pltpu.VMEM((dv, width), jnp.bfloat16),
            pltpu.VMEM((KV_HEADS, 2, rows, LANES), jnp.float32),
            pltpu.VMEM((few, KV_HEADS, HALVES, caps[0] * block_rows, LANES), jnp.float32),
            pltpu.VMEM((segments, KV_HEADS, HALVES, caps[1] * block_rows, LANES), jnp.float32),
            pltpu.VMEM((1, blocks), jnp.int32),
            pltpu.SMEM((1, blocks), jnp.int32),
            pltpu.SemaphoreType.DMA((2 * len(parts) + 2 + segments // few,)),
        ],
        compiler_params=pltpu.CompilerParams(vmem_limit_bytes=40 * 2**20),
        name="project_and_pack",
    )(
        placement,
        pltpu.with_memory_space_constraint(visual, pltpu.HBM),
        pltpu.with_memory_space_constraint(kv_weight, pltpu.HBM),
    )


def attend(state, queries, kv, rows, with_mark=False):
    every, width = queries.shape
    group = width // LANES
    sources, _, slots, _ = kv.shape
    scale = LANES ** (-0.5) * math.log2(math.e)
    take = min(sources, 1 << (TILE // slots).bit_length() - 1)
    while sources % take:
        take //= 2
    keys = take * slots
    part = PART
    while keys % part:
        part //= 2
    steps = sources // take
    first = state is None
    owners = every // rows
    columns = (group + 1) * LANES

    def body(*refs):
        refs = list(refs)
        s_ref = None if first else refs.pop(0)
        q_ref, kv_ref, o_ref = refs[:3]
        f_ref = refs[3] if with_mark else None
        q_s, m_s, l_s, acc_s, k_s, v_s = refs[-6:]
        step = pl.program_id(0)

        @pl.when(step == 0)
        def _():
            ones = (lax.broadcasted_iota(jnp.int32, (every, LANES), 1) == 0).astype(jnp.float32)
            ones = ones.astype(jnp.bfloat16)
            for j in range(group):
                x = q_ref[:, j * LANES : (j + 1) * LANES] * scale
                hi = x.astype(jnp.bfloat16)
                q_s[j, :, 0 * LANES : 1 * LANES] = hi
                q_s[j, :, 1 * LANES : 2 * LANES] = (x - hi.astype(jnp.float32)).astype(jnp.bfloat16)
                q_s[j, :, 2 * LANES : 3 * LANES] = hi
                q_s[j, :, 3 * LANES : 4 * LANES] = ones
            if first:
                m_s[...] = jnp.full(m_s.shape, BIAS, jnp.float32)
                l_s[...] = jnp.zeros(l_s.shape, jnp.float32)
                acc_s[...] = jnp.zeros(acc_s.shape, jnp.float32)
            else:
                stats = s_ref[:, :, group * LANES :].reshape(every, LANES)
                lane0 = lax.broadcasted_iota(jnp.int32, (every, LANES), 1) == 0
                for j in range(group):
                    acc_s[j] = s_ref[:, :, j * LANES : (j + 1) * LANES].reshape(every, LANES)
                    m_s[j] = jnp.broadcast_to(stats[:, j : j + 1], (every, LANES))
                    total = jnp.broadcast_to(
                        stats[:, LANES // 2 + j : LANES // 2 + j + 1], (every, LANES)
                    )
                    l_s[j] = jnp.where(lane0, total, 0.0)

        live = kv_ref[:, 0] < LIVE_BELOW
        key = jnp.where(live, kv_ref[:, 0], 0.0).reshape(keys, LANES)
        value = jnp.where(live, kv_ref[:, 1], 0.0).reshape(keys, LANES)
        lane = lax.broadcasted_iota(jnp.int32, (take, slots, LANES), 2)
        bias = jnp.where(live | (lane != 0), 0.0, BIAS).reshape(keys, LANES)
        k_hi = key.astype(jnp.bfloat16)
        k_s[:, 0 * LANES : 1 * LANES] = k_hi
        k_s[:, 1 * LANES : 2 * LANES] = k_hi
        k_s[:, 2 * LANES : 3 * LANES] = (key - k_hi.astype(jnp.float32)).astype(jnp.bfloat16)
        k_s[:, 3 * LANES : 4 * LANES] = bias.astype(jnp.bfloat16)
        v_hi = value.astype(jnp.bfloat16)
        v_s[:, :LANES] = v_hi
        v_s[:, LANES:] = (value - v_hi.astype(jnp.float32)).astype(jnp.bfloat16)
        if with_mark:
            mark = jnp.max(jnp.max(kv_ref[:, 0].reshape(keys, LANES), axis=0, keepdims=True))
            mark = jnp.broadcast_to(mark, f_ref.shape)

            @pl.when(step == 0)
            def _():
                f_ref[...] = mark

            @pl.when(step > 0)
            def _():
                f_ref[...] = jnp.maximum(f_ref[...], mark)

        def score(t, j):
            return lax.dot_general(
                q_s[j],
                k_s[t * part : (t + 1) * part],
                (((1,), (1,)), ((), ())),
                preferred_element_type=jnp.float32,
            )

        def weigh(j, scores):
            old = m_s[j]
            fresh = jnp.maximum(old, jnp.max(scores, axis=1, keepdims=True))
            factor = jnp.exp2(old - fresh)
            weights = jnp.exp2(scores - jnp.tile(fresh, (1, part // LANES)))
            sums = weights[:, :LANES]
            for i in range(1, part // LANES):
                sums = sums + weights[:, i * LANES : (i + 1) * LANES]
            l_s[j] = l_s[j] * factor + sums
            m_s[j] = fresh
            w_hi = weights.astype(jnp.bfloat16)
            return factor, w_hi, (weights - w_hi.astype(jnp.float32)).astype(jnp.bfloat16)

        def gather(t, j, factor, w_hi, w_lo):
            at = slice(t * part, (t + 1) * part)
            both = jnp.dot(w_hi, v_s[at], preferred_element_type=jnp.float32)
            rest = jnp.dot(w_lo, v_s[at, :LANES], preferred_element_type=jnp.float32)
            acc_s[j] = acc_s[j] * factor + (both[:, :LANES] + both[:, LANES:] + rest)

        items = [(t, j) for t in range(keys // part) for j in range(group)]
        scores = score(*items[0])
        behind = None
        for n, item in enumerate(items):
            ahead = score(*items[n + 1]) if n + 1 < len(items) else None
            weighed = weigh(item[1], scores)
            if behind is not None:
                gather(*behind)
            behind = (*item, *weighed)
            scores = ahead
        gather(*behind)

        @pl.when(step == steps - 1)
        def _():
            lane = lax.broadcasted_iota(jnp.int32, (every, LANES), 1)
            stats = jnp.zeros((every, LANES), jnp.float32)
            for j in range(group):
                o_ref[:, :, j * LANES : (j + 1) * LANES] = acc_s[j].reshape(owners, rows, LANES)
                total = jnp.sum(l_s[j], axis=1, keepdims=True)
                stats = jnp.where(lane == j, m_s[j], stats)
                stats = jnp.where(lane == LANES // 2 + j, total, stats)
            o_ref[:, :, group * LANES :] = stats.reshape(owners, rows, LANES)

    state_spec = pl.BlockSpec((owners, rows, columns), lambda i: (0, 0, 0))
    in_specs = [
        pl.BlockSpec((every, width), lambda i: (0, 0)),
        pl.BlockSpec((take, 2, slots, LANES), lambda i: (i, 0, 0, 0)),
    ]
    args = (queries, kv)
    if not first:
        in_specs = [state_spec] + in_specs
        args = (state,) + args
    out_shape = [jax.ShapeDtypeStruct((owners, rows, columns), jnp.float32)]
    out_specs = [state_spec]
    if with_mark:
        out_shape.append(jax.ShapeDtypeStruct((ROWS8, LANES), jnp.float32))
        out_specs.append(pl.BlockSpec((ROWS8, LANES), lambda i: (0, 0)))
    out = pl.pallas_call(
        body,
        out_shape=out_shape,
        grid=(steps,),
        in_specs=in_specs,
        out_specs=out_specs,
        scratch_shapes=[
            pltpu.VMEM((group, every, 4 * LANES), jnp.bfloat16),
            pltpu.VMEM((group, every, LANES), jnp.float32),
            pltpu.VMEM((group, every, LANES), jnp.float32),
            pltpu.VMEM((group, every, LANES), jnp.float32),
            pltpu.VMEM((keys, 4 * LANES), jnp.bfloat16),
            pltpu.VMEM((keys, 2 * LANES), jnp.bfloat16),
        ],
        compiler_params=pltpu.CompilerParams(vmem_limit_bytes=50 * 2**20),
        name="attend_first" if first else "attend_more",
    )(*args)
    return out if with_mark else out[0]


def combine(parts):
    owners, rows, columns = parts.shape
    group = columns // LANES - 1

    def body(x_ref, o_ref):
        for h in range(owners // HALVES):
            a, b = HALVES * h, HALVES * h + 1
            stats_a = x_ref[a, :, group * LANES :]
            stats_b = x_ref[b, :, group * LANES :]
            peak = jnp.maximum(stats_a, stats_b)
            fa, fb = jnp.exp2(stats_a - peak), jnp.exp2(stats_b - peak)
            total = pltpu.roll(stats_a, LANES // 2, 1) * fa + pltpu.roll(stats_b, LANES // 2, 1) * fb
            fa, fb = fa / total, fb / total
            for j in range(group):
                cols = slice(j * LANES, (j + 1) * LANES)
                out = x_ref[a, :, cols] * fa[:, j : j + 1] + x_ref[b, :, cols] * fb[:, j : j + 1]
                o_ref[:, (h * group + j) * LANES : (h * group + j + 1) * LANES] = out

    return pl.pallas_call(
        body,
        out_shape=jax.ShapeDtypeStruct((rows, owners // HALVES * group * LANES), jnp.float32),
        compiler_params=pltpu.CompilerParams(vmem_limit_bytes=20 * 2**20),
        name="combine",
    )(parts)


def on_device(visual, text_queries, kv_weight, placement):
    axes = ("grp", "blk")
    segments = lax.axis_size("grp")
    owners = lax.axis_size("blk")
    devices = segments * owners
    blocks = placement.shape[0]
    block_rows = visual.shape[0] // blocks
    rows = text_queries.shape[0]
    per_pair = max(2, blocks // devices + 1)
    most = owners * per_pair // HALVES
    caps = CAPS + (most - CAPS[0],)
    common = sum(CAPS)

    q = text_queries.reshape(rows, KV_HEADS, -1).transpose(1, 0, 2)
    q = jnp.broadcast_to(q[:, None], (KV_HEADS, HALVES, *q.shape[1:]))
    q = q.reshape(owners, rows, -1)
    q = lax.all_to_all(q, "blk", 0, 0, tiled=True)

    owner = placement.reshape(blocks)
    packed = project_and_pack(placement, visual, kv_weight, caps, segments)

    def exchange(chunk):
        chunk = chunk.reshape(devices, 2, -1, LANES)
        return lax.all_to_all(chunk, axes, 0, 0, tiled=True)

    def beyond(slots, state):
        counts = jnp.sum(
            (owner[None, :] // owners == jnp.arange(segments)[:, None]).astype(jnp.int32), axis=1
        )
        mine = jnp.max(counts) > HALVES * common
        half = jnp.arange(HALVES)[None, :]
        held = (counts[:, None] + (HALVES - 1) - half) // HALVES - caps[0]
        held = jnp.where(mine, held, 0)[:, None, :, None, None, None]
        slot = (jnp.arange(slots * block_rows) // block_rows)[:, None]
        chunk = packed[2][:, :, :, :, : slots * block_rows]
        chunk = jnp.where(slot < held, chunk, EMPTY[0])
        return attend(state, queries, exchange(chunk), rows)

    queries = q.reshape(owners * rows, -1)
    first = exchange(packed[0])
    second = exchange(packed[1])
    state = attend(None, queries, first, rows)
    state, mark = attend(state, queries, second, rows, with_mark=True)
    mark = mark[0, 0]
    level = (mark > 2 * EMPTY[0]).astype(jnp.int32) + (mark > 2 * EMPTY[1]).astype(jnp.int32)
    state = lax.switch(
        level,
        [
            lambda s: s,
            lambda s: beyond(CAPS[1] + SPARE, s),
            lambda s: beyond(caps[2], s),
        ],
        state,
    )
    parts = lax.all_to_all(state, "blk", 0, 0, tiled=True)
    return combine(parts)


def solution(mesh):
    placed = (P(("grp", "blk"), None), P(("grp", "blk"), None), P(), P(("grp", "blk"), None))
    return jax.shard_map(
        on_device, mesh=mesh, in_specs=placed, out_specs=P(("grp", "blk"), None), check_vma=False
    )
```

```python
import functools
import math

import jax
import jax.numpy as jnp
from jax import lax
from jax.experimental import pallas as pl
from jax.experimental.pallas import tpu as pltpu
from jax.sharding import PartitionSpec as P

HEADS = 28
KV_HEADS = 4
GROUP = HEADS // KV_HEADS
LANES = 128
HALVES = 2
CAPS = (4, 1)
SPARE = 1
BIAS = -(2.0**99)
EMPTY = (1e30, 4e30, 16e30)
LIVE_BELOW = 1e29
ROWS8 = 8
TILE = 1024
PART = 512
DEPTHS = (512, 1024)


def project_and_pack(placement, visual, kv_weight, caps, segments):
    rows, dv = visual.shape
    width = kv_weight.shape[1]
    blocks = placement.shape[0]
    block_rows = rows // blocks
    owners = KV_HEADS * HALVES
    common = caps[0] + caps[1]
    cuts = [0]
    while cuts[-1] < dv:
        cuts.append(min(dv, cuts[-1] + DEPTHS[min(len(cuts) - 1, len(DEPTHS) - 1)]))
    parts = list(zip(cuts[:-1], cuts[1:]))
    few = math.gcd(segments, 4)

    def body(owner_ref, x_hbm, w_hbm, o1, o2, o3, x, w, buf, mark1, mark2, code, table, sems):
        loads = []
        for i, (a, b) in enumerate(parts):
            loads.append(
                (
                    pltpu.make_async_copy(x_hbm.at[:, a:b], x.at[:, a:b], sems.at[2 * i]),
                    pltpu.make_async_copy(w_hbm.at[a:b], w.at[a:b], sems.at[2 * i + 1]),
                )
            )
            for load in loads[-1]:
                load.start()
        sem, sem2 = (sems.at[2 * len(parts) + i] for i in range(2))
        sem1 = sems.at[2 * len(parts) + 2 :]

        segment = lax.shift_right_logical(owner_ref[...], owners.bit_length() - 1)
        segment = segment.astype(jnp.float32)
        shape = (blocks, blocks)
        i = lax.broadcasted_iota(jnp.int32, shape, 0)
        j = lax.broadcasted_iota(jnp.int32, shape, 1)
        column = jnp.broadcast_to(segment, shape)
        line = jnp.sum(jnp.where(i == j, column, 0.0), axis=0, keepdims=True)
        before = jnp.where((column == line) & (i < j), 1.0, 0.0)
        rank = jnp.sum(before, axis=0, keepdims=True)
        top = jnp.max(rank) + 1.0
        rank = rank.astype(jnp.int32)
        half = jnp.bitwise_and(rank, HALVES - 1)
        slot = lax.shift_right_logical(rank, HALVES.bit_length() - 1)
        code[...] = (line.astype(jnp.int32) * HALVES + half) * ROWS8 + slot
        codes = pltpu.make_async_copy(code, table, sem)
        codes.start()
        level = (top > HALVES * common).astype(jnp.int32)
        level = level + (top > HALVES * (common + SPARE)).astype(jnp.int32)
        mark1[...] = jnp.full(mark1.shape, EMPTY[0], jnp.float32)
        mark = jnp.where(level == 0, EMPTY[0], jnp.where(level == 1, EMPTY[1], EMPTY[2]))
        mark2[...] = jnp.broadcast_to(mark.astype(jnp.float32), mark2.shape)
        fills = [pltpu.make_async_copy(mark2, o2.at[:, :, :, 0], sem2)]
        for g in range(0, segments, mark1.shape[0]):
            to = o1.at[g : g + mark1.shape[0], :, :, 0]
            fills.append(pltpu.make_async_copy(mark1, to, sem1.at[g // mark1.shape[0]]))
        for copy in fills:
            copy.start()
        codes.wait()

        for i, (a, b) in enumerate(parts):
            for load in loads[i]:
                load.wait()
            for kind in range(2):
                for h in range(0, KV_HEADS, 2):
                    c = (kind * KV_HEADS + h) * LANES
                    part = jnp.dot(
                        x[:, a:b], w[a:b, c : c + 2 * LANES], preferred_element_type=jnp.float32
                    )
                    for k in range(2):
                        piece = part[:, k * LANES : (k + 1) * LANES]
                        buf[h + k, kind] = piece if i == 0 else buf[h + k, kind] + piece

        for copy in fills:
            copy.wait()

        def send(j, c):
            at = table[0, j]
            slot = at % ROWS8
            half = at // ROWS8 % HALVES
            seg = at // (ROWS8 * HALVES)
            src = buf.at[:, :, pl.ds(pl.multiple_of(j * block_rows, ROWS8), block_rows), :]

            def copy(out, slot):
                rows_at = pl.ds(pl.multiple_of(slot * block_rows, ROWS8), block_rows)
                dst = out.at[seg, :, half, :, rows_at, :]
                pltpu.make_async_copy(src, dst, sem).start()

            @pl.when(slot < caps[0])
            def _():
                copy(o1, slot)

            @pl.when(slot >= caps[0])
            def _():
                @pl.when(level == 0)
                def _():
                    copy(o2, slot - caps[0])

                @pl.when(level > 0)
                def _():
                    copy(o3, slot - caps[0])

            return c

        lax.fori_loop(0, blocks, send, 0, unroll=4)
        pltpu.make_async_copy(buf, buf, sem).wait()

    shapes = [
        pltpu.HBM((segments, KV_HEADS, HALVES, 2, cap * block_rows, LANES), jnp.float32)
        for cap in caps
    ]
    hbm = pl.BlockSpec(memory_space=pltpu.HBM)
    return pl.pallas_call(
        body,
        out_shape=shapes,
        in_specs=[pl.BlockSpec(memory_space=pltpu.VMEM), hbm, hbm],
        out_specs=[hbm for _ in caps],
        scratch_shapes=[
            pltpu.VMEM((rows, dv), jnp.bfloat16),
            pltpu.VMEM((dv, width), jnp.bfloat16),
            pltpu.VMEM((KV_HEADS, 2, rows, LANES), jnp.float32),
            pltpu.VMEM((few, KV_HEADS, HALVES, caps[0] * block_rows, LANES), jnp.float32),
            pltpu.VMEM((segments, KV_HEADS, HALVES, caps[1] * block_rows, LANES), jnp.float32),
            pltpu.VMEM((1, blocks), jnp.int32),
            pltpu.SMEM((1, blocks), jnp.int32),
            pltpu.SemaphoreType.DMA((2 * len(parts) + 2 + segments // few,)),
        ],
        compiler_params=pltpu.CompilerParams(vmem_limit_bytes=40 * 2**20),
        name="project_and_pack",
    )(
        placement,
        pltpu.with_memory_space_constraint(visual, pltpu.HBM),
        pltpu.with_memory_space_constraint(kv_weight, pltpu.HBM),
    )


def attend(state, queries, head, kv, rows, with_mark=False):
    every = queries.shape[0]
    group = GROUP
    width = group * LANES
    sources, _, slots, _ = kv.shape
    scale = LANES ** (-0.5) * math.log2(math.e)
    take = min(sources, 1 << (TILE // slots).bit_length() - 1)
    while sources % take:
        take //= 2
    keys = take * slots
    part = PART
    while keys % part:
        part //= 2
    steps = sources // take
    first = state is None
    owners = every // rows
    columns = (group + 1) * LANES

    def body(_, *refs):
        refs = list(refs)
        s_ref = None if first else refs.pop(0)
        q_ref, kv_ref, o_ref = refs[:3]
        f_ref = refs[3] if with_mark else None
        q_s, m_s, l_s, acc_s, k_s, v_s = refs[-6:]
        step = pl.program_id(0)

        @pl.when(step == 0)
        def _():
            ones = (lax.broadcasted_iota(jnp.int32, (every, LANES), 1) == 0).astype(jnp.float32)
            ones = ones.astype(jnp.bfloat16)
            for j in range(group):
                x = q_ref[:, j * LANES : (j + 1) * LANES] * scale
                hi = x.astype(jnp.bfloat16)
                q_s[j, :, 0 * LANES : 1 * LANES] = hi
                q_s[j, :, 1 * LANES : 2 * LANES] = (x - hi.astype(jnp.float32)).astype(jnp.bfloat16)
                q_s[j, :, 2 * LANES : 3 * LANES] = hi
                q_s[j, :, 3 * LANES : 4 * LANES] = ones
            if first:
                m_s[...] = jnp.full(m_s.shape, BIAS, jnp.float32)
                l_s[...] = jnp.zeros(l_s.shape, jnp.float32)
                acc_s[...] = jnp.zeros(acc_s.shape, jnp.float32)
            else:
                stats = s_ref[:, :, group * LANES :].reshape(every, LANES)
                lane0 = lax.broadcasted_iota(jnp.int32, (every, LANES), 1) == 0
                for j in range(group):
                    acc_s[j] = s_ref[:, :, j * LANES : (j + 1) * LANES].reshape(every, LANES)
                    m_s[j] = jnp.broadcast_to(stats[:, j : j + 1], (every, LANES))
                    total = jnp.broadcast_to(
                        stats[:, LANES // 2 + j : LANES // 2 + j + 1], (every, LANES)
                    )
                    l_s[j] = jnp.where(lane0, total, 0.0)

        live = kv_ref[:, 0] < LIVE_BELOW
        key = jnp.where(live, kv_ref[:, 0], 0.0).reshape(keys, LANES)
        value = jnp.where(live, kv_ref[:, 1], 0.0).reshape(keys, LANES)
        lane = lax.broadcasted_iota(jnp.int32, (take, slots, LANES), 2)
        bias = jnp.where(live | (lane != 0), 0.0, BIAS).reshape(keys, LANES)
        k_hi = key.astype(jnp.bfloat16)
        k_s[:, 0 * LANES : 1 * LANES] = k_hi
        k_s[:, 1 * LANES : 2 * LANES] = k_hi
        k_s[:, 2 * LANES : 3 * LANES] = (key - k_hi.astype(jnp.float32)).astype(jnp.bfloat16)
        k_s[:, 3 * LANES : 4 * LANES] = bias.astype(jnp.bfloat16)
        v_hi = value.astype(jnp.bfloat16)
        v_s[:, :LANES] = v_hi
        v_s[:, LANES:] = (value - v_hi.astype(jnp.float32)).astype(jnp.bfloat16)
        if with_mark:
            mark = jnp.max(jnp.max(kv_ref[:, 0].reshape(keys, LANES), axis=0, keepdims=True))
            mark = jnp.broadcast_to(mark, f_ref.shape)

            @pl.when(step == 0)
            def _():
                f_ref[...] = mark

            @pl.when(step > 0)
            def _():
                f_ref[...] = jnp.maximum(f_ref[...], mark)

        def score(t, j):
            return lax.dot_general(
                q_s[j],
                k_s[t * part : (t + 1) * part],
                (((1,), (1,)), ((), ())),
                preferred_element_type=jnp.float32,
            )

        def weigh(j, scores):
            old = m_s[j]
            fresh = jnp.maximum(old, jnp.max(scores, axis=1, keepdims=True))
            factor = jnp.exp2(old - fresh)
            weights = jnp.exp2(scores - jnp.tile(fresh, (1, part // LANES)))
            sums = weights[:, :LANES]
            for i in range(1, part // LANES):
                sums = sums + weights[:, i * LANES : (i + 1) * LANES]
            l_s[j] = l_s[j] * factor + sums
            m_s[j] = fresh
            w_hi = weights.astype(jnp.bfloat16)
            return factor, w_hi, (weights - w_hi.astype(jnp.float32)).astype(jnp.bfloat16)

        def gather(t, j, factor, w_hi, w_lo):
            at = slice(t * part, (t + 1) * part)
            both = jnp.dot(w_hi, v_s[at], preferred_element_type=jnp.float32)
            rest = jnp.dot(w_lo, v_s[at, :LANES], preferred_element_type=jnp.float32)
            acc_s[j] = acc_s[j] * factor + (both[:, :LANES] + both[:, LANES:] + rest)

        items = [(t, j) for t in range(keys // part) for j in range(group)]
        scores = score(*items[0])
        behind = None
        for n, item in enumerate(items):
            ahead = score(*items[n + 1]) if n + 1 < len(items) else None
            weighed = weigh(item[1], scores)
            if behind is not None:
                gather(*behind)
            behind = (*item, *weighed)
            scores = ahead
        gather(*behind)

        @pl.when(step == steps - 1)
        def _():
            lane = lax.broadcasted_iota(jnp.int32, (every, LANES), 1)
            stats = jnp.zeros((every, LANES), jnp.float32)
            for j in range(group):
                o_ref[:, :, j * LANES : (j + 1) * LANES] = acc_s[j].reshape(owners, rows, LANES)
                total = jnp.sum(l_s[j], axis=1, keepdims=True)
                stats = jnp.where(lane == j, m_s[j], stats)
                stats = jnp.where(lane == LANES // 2 + j, total, stats)
            o_ref[:, :, group * LANES :] = stats.reshape(owners, rows, LANES)

    state_spec = pl.BlockSpec((owners, rows, columns), lambda i, h: (0, 0, 0))
    in_specs = [
        pl.BlockSpec((every, width), lambda i, h: (0, h[0])),
        pl.BlockSpec((take, 2, slots, LANES), lambda i, h: (i, 0, 0, 0)),
    ]
    args = (queries, kv)
    if not first:
        in_specs = [state_spec] + in_specs
        args = (state,) + args
    out_shape = [jax.ShapeDtypeStruct((owners, rows, columns), jnp.float32)]
    out_specs = [state_spec]
    if with_mark:
        out_shape.append(jax.ShapeDtypeStruct((ROWS8, LANES), jnp.float32))
        out_specs.append(pl.BlockSpec((ROWS8, LANES), lambda i, h: (0, 0)))
    out = pl.pallas_call(
        body,
        out_shape=out_shape,
        grid_spec=pltpu.PrefetchScalarGridSpec(
            num_scalar_prefetch=1,
            grid=(steps,),
            in_specs=in_specs,
            out_specs=out_specs,
            scratch_shapes=[
                pltpu.VMEM((group, every, 4 * LANES), jnp.bfloat16),
                pltpu.VMEM((group, every, LANES), jnp.float32),
                pltpu.VMEM((group, every, LANES), jnp.float32),
                pltpu.VMEM((group, every, LANES), jnp.float32),
                pltpu.VMEM((keys, 4 * LANES), jnp.bfloat16),
                pltpu.VMEM((keys, 2 * LANES), jnp.bfloat16),
            ],
        ),
        compiler_params=pltpu.CompilerParams(vmem_limit_bytes=50 * 2**20),
        name="attend_first" if first else "attend_more",
    )(head, *args)
    return out if with_mark else out[0]


def combine(parts):
    owners, rows, columns = parts.shape
    group = columns // LANES - 1

    def body(x_ref, o_ref):
        for h in range(owners // HALVES):
            a, b = HALVES * h, HALVES * h + 1
            stats_a = x_ref[a, :, group * LANES :]
            stats_b = x_ref[b, :, group * LANES :]
            peak = jnp.maximum(stats_a, stats_b)
            fa, fb = jnp.exp2(stats_a - peak), jnp.exp2(stats_b - peak)
            total = pltpu.roll(stats_a, LANES // 2, 1) * fa + pltpu.roll(stats_b, LANES // 2, 1) * fb
            fa, fb = fa / total, fb / total
            for j in range(group):
                cols = slice(j * LANES, (j + 1) * LANES)
                out = x_ref[a, :, cols] * fa[:, j : j + 1] + x_ref[b, :, cols] * fb[:, j : j + 1]
                o_ref[:, (h * group + j) * LANES : (h * group + j + 1) * LANES] = out

    return pl.pallas_call(
        body,
        out_shape=jax.ShapeDtypeStruct((rows, owners // HALVES * group * LANES), jnp.float32),
        compiler_params=pltpu.CompilerParams(vmem_limit_bytes=20 * 2**20),
        name="combine",
    )(parts)


def on_device(visual, text_queries, kv_weight, placement):
    axes = ("grp", "blk")
    segments = lax.axis_size("grp")
    owners = lax.axis_size("blk")
    devices = segments * owners
    blocks = placement.shape[0]
    block_rows = visual.shape[0] // blocks
    rows = text_queries.shape[0]
    per_pair = max(2, blocks // devices + 1)
    most = owners * per_pair // HALVES
    caps = CAPS + (most - CAPS[0],)
    common = sum(CAPS)

    queries = lax.all_gather(text_queries, "blk", axis=0, tiled=True)
    head = (lax.axis_index("blk") // HALVES).astype(jnp.int32).reshape(1)

    owner = placement.reshape(blocks)
    packed = project_and_pack(placement, visual, kv_weight, caps, segments)

    def exchange(chunk):
        chunk = chunk.reshape(devices, 2, -1, LANES)
        return lax.all_to_all(chunk, axes, 0, 0, tiled=True)

    def beyond(slots, state):
        counts = jnp.sum(
            (owner[None, :] // owners == jnp.arange(segments)[:, None]).astype(jnp.int32), axis=1
        )
        mine = jnp.max(counts) > HALVES * common
        half = jnp.arange(HALVES)[None, :]
        held = (counts[:, None] + (HALVES - 1) - half) // HALVES - caps[0]
        held = jnp.where(mine, held, 0)[:, None, :, None, None, None]
        slot = (jnp.arange(slots * block_rows) // block_rows)[:, None]
        chunk = packed[2][:, :, :, :, : slots * block_rows]
        chunk = jnp.where(slot < held, chunk, EMPTY[0])
        return attend(state, queries, head, exchange(chunk), rows)

    first = exchange(packed[0])
    second = exchange(packed[1])
    state = attend(None, queries, head, first, rows)
    state, mark = attend(state, queries, head, second, rows, with_mark=True)
    mark = mark[0, 0]
    level = (mark > 2 * EMPTY[0]).astype(jnp.int32) + (mark > 2 * EMPTY[1]).astype(jnp.int32)
    state = lax.switch(
        level,
        [
            lambda s: s,
            lambda s: beyond(CAPS[1] + SPARE, s),
            lambda s: beyond(caps[2], s),
        ],
        state,
    )
    parts = lax.all_to_all(state, "blk", 0, 0, tiled=True)
    return combine(parts)


def solution(mesh):
    placed = (P(("grp", "blk"), None), P(("grp", "blk"), None), P(), P(("grp", "blk"), None))
    return jax.shard_map(
        on_device, mesh=mesh, in_specs=placed, out_specs=P(("grp", "blk"), None), check_vma=False
    )
```

```python
import functools
import math

import jax
import jax.numpy as jnp
from jax import lax
from jax.experimental import pallas as pl
from jax.experimental.pallas import tpu as pltpu
from jax.sharding import PartitionSpec as P

HEADS = 28
KV_HEADS = 4
GROUP = HEADS // KV_HEADS
LANES = 128
HALVES = 2
CAPS = (4, 1)
SPARE = 1
BIAS = -(2.0**99)
EMPTY = (1e30, 4e30, 16e30)
LIVE_BELOW = 1e29
ROWS8 = 8
TILE = 1024
PART = 512
DEPTHS = (512, 1024)


def project_and_pack(placement, visual, kv_weight, caps, segments):
    rows, dv = visual.shape
    width = kv_weight.shape[1]
    blocks = placement.shape[0]
    block_rows = rows // blocks
    owners = KV_HEADS * HALVES
    common = caps[0] + caps[1]
    cuts = [0]
    while cuts[-1] < dv:
        cuts.append(min(dv, cuts[-1] + DEPTHS[min(len(cuts) - 1, len(DEPTHS) - 1)]))
    parts = list(zip(cuts[:-1], cuts[1:]))
    few = math.gcd(segments, 4)

    def body(owner_ref, x_hbm, w_hbm, o1, o2, o3, x, w, buf, mark1, mark2, code, table, sems):
        loads = []
        for i, (a, b) in enumerate(parts):
            loads.append(
                (
                    pltpu.make_async_copy(x_hbm.at[:, a:b], x.at[:, a:b], sems.at[2 * i]),
                    pltpu.make_async_copy(w_hbm.at[a:b], w.at[a:b], sems.at[2 * i + 1]),
                )
            )
            for load in loads[-1]:
                load.start()
        sem, sem2 = (sems.at[2 * len(parts) + i] for i in range(2))
        sem1 = sems.at[2 * len(parts) + 2 :]

        segment = lax.shift_right_logical(owner_ref[...], owners.bit_length() - 1)
        segment = segment.astype(jnp.float32)
        shape = (blocks, blocks)
        i = lax.broadcasted_iota(jnp.int32, shape, 0)
        j = lax.broadcasted_iota(jnp.int32, shape, 1)
        column = jnp.broadcast_to(segment, shape)
        line = jnp.sum(jnp.where(i == j, column, 0.0), axis=0, keepdims=True)
        before = jnp.where((column == line) & (i < j), 1.0, 0.0)
        rank = jnp.sum(before, axis=0, keepdims=True)
        top = jnp.max(rank) + 1.0
        rank = rank.astype(jnp.int32)
        half = jnp.bitwise_and(rank, HALVES - 1)
        slot = lax.shift_right_logical(rank, HALVES.bit_length() - 1)
        code[...] = (line.astype(jnp.int32) * HALVES + half) * ROWS8 + slot
        codes = pltpu.make_async_copy(code, table, sem)
        codes.start()
        level = (top > HALVES * common).astype(jnp.int32)
        level = level + (top > HALVES * (common + SPARE)).astype(jnp.int32)
        mark1[...] = jnp.full(mark1.shape, EMPTY[0], jnp.float32)
        mark = jnp.where(level == 0, EMPTY[0], jnp.where(level == 1, EMPTY[1], EMPTY[2]))
        mark2[...] = jnp.broadcast_to(mark.astype(jnp.float32), mark2.shape)
        fills = [pltpu.make_async_copy(mark2, o2.at[:, :, :, 0], sem2)]
        for g in range(0, segments, mark1.shape[0]):
            to = o1.at[g : g + mark1.shape[0], :, :, 0]
            fills.append(pltpu.make_async_copy(mark1, to, sem1.at[g // mark1.shape[0]]))
        for copy in fills:
            copy.start()
        codes.wait()

        for i, (a, b) in enumerate(parts):
            for load in loads[i]:
                load.wait()
            for kind in range(2):
                for h in range(0, KV_HEADS, 2):
                    c = (kind * KV_HEADS + h) * LANES
                    part = jnp.dot(
                        x[:, a:b], w[a:b, c : c + 2 * LANES], preferred_element_type=jnp.float32
                    )
                    for k in range(2):
                        piece = part[:, k * LANES : (k + 1) * LANES]
                        buf[h + k, kind] = piece if i == 0 else buf[h + k, kind] + piece

        for copy in fills:
            copy.wait()

        def send(j, c):
            at = table[0, j]
            slot = at % ROWS8
            half = at // ROWS8 % HALVES
            seg = at // (ROWS8 * HALVES)
            src = buf.at[:, :, pl.ds(pl.multiple_of(j * block_rows, ROWS8), block_rows), :]

            def copy(out, slot):
                rows_at = pl.ds(pl.multiple_of(slot * block_rows, ROWS8), block_rows)
                dst = out.at[seg, :, half, :, rows_at, :]
                pltpu.make_async_copy(src, dst, sem).start()

            @pl.when(slot < caps[0])
            def _():
                copy(o1, slot)

            @pl.when(slot >= caps[0])
            def _():
                @pl.when(level == 0)
                def _():
                    copy(o2, slot - caps[0])

                @pl.when(level > 0)
                def _():
                    copy(o3, slot - caps[0])

            return c

        lax.fori_loop(0, blocks, send, 0, unroll=4)
        pltpu.make_async_copy(buf, buf, sem).wait()

    shapes = [
        pltpu.HBM((segments, KV_HEADS, HALVES, 2, cap * block_rows, LANES), jnp.float32)
        for cap in caps
    ]
    hbm = pl.BlockSpec(memory_space=pltpu.HBM)
    return pl.pallas_call(
        body,
        out_shape=shapes,
        in_specs=[pl.BlockSpec(memory_space=pltpu.VMEM), hbm, hbm],
        out_specs=[hbm for _ in caps],
        scratch_shapes=[
            pltpu.VMEM((rows, dv), jnp.bfloat16),
            pltpu.VMEM((dv, width), jnp.bfloat16),
            pltpu.VMEM((KV_HEADS, 2, rows, LANES), jnp.float32),
            pltpu.VMEM((few, KV_HEADS, HALVES, caps[0] * block_rows, LANES), jnp.float32),
            pltpu.VMEM((segments, KV_HEADS, HALVES, caps[1] * block_rows, LANES), jnp.float32),
            pltpu.VMEM((1, blocks), jnp.int32),
            pltpu.SMEM((1, blocks), jnp.int32),
            pltpu.SemaphoreType.DMA((2 * len(parts) + 2 + segments // few,)),
        ],
        compiler_params=pltpu.CompilerParams(vmem_limit_bytes=40 * 2**20),
        name="project_and_pack",
    )(
        placement,
        pltpu.with_memory_space_constraint(visual, pltpu.HBM),
        pltpu.with_memory_space_constraint(kv_weight, pltpu.HBM),
    )


def attend(state, queries, me, kv, rows, with_mark=False):
    every = queries.shape[0]
    width = queries.shape[1]
    group = width // LANES
    sources, _, slots, _ = kv.shape
    scale = LANES ** (-0.5) * math.log2(math.e)
    take = min(sources, 1 << (TILE // slots).bit_length() - 1)
    while sources % take:
        take //= 2
    keys = take * slots
    part = PART
    while keys % part:
        part //= 2
    steps = sources // take
    first = state is None
    owners = every // rows
    columns = (group + 1) * LANES

    def body(me_ref, *refs):
        refs = list(refs)
        s_ref = None if first else refs.pop(0)
        q_ref, kv_ref, o_ref = refs[:3]
        f_ref = refs[3] if with_mark else None
        q_s, m_s, l_s, acc_s, k_s, v_s = refs[-6:]
        step = pl.program_id(0)

        @pl.when(step == 0)
        def _():
            ones = (lax.broadcasted_iota(jnp.int32, (every, LANES), 1) == 0).astype(jnp.float32)
            ones = ones.astype(jnp.bfloat16)
            me = me_ref[0]
            for p in range(owners):
                core = jnp.bitwise_and(me ^ p, HALVES - 1)
                away = lax.shift_right_logical(me ^ p, HALVES.bit_length() - 1)
                at = pl.multiple_of((core * KV_HEADS + away) * rows, rows)
                to = slice(p * rows, (p + 1) * rows)
                for j in range(group):
                    x = q_ref[pl.ds(at, rows), j * LANES : (j + 1) * LANES] * scale
                    hi = x.astype(jnp.bfloat16)
                    lo = (x - hi.astype(jnp.float32)).astype(jnp.bfloat16)
                    q_s[j, to, 0 * LANES : 1 * LANES] = hi
                    q_s[j, to, 1 * LANES : 2 * LANES] = lo
                    q_s[j, to, 2 * LANES : 3 * LANES] = hi
            for j in range(group):
                q_s[j, :, 3 * LANES : 4 * LANES] = ones
            if first:
                m_s[...] = jnp.full(m_s.shape, BIAS, jnp.float32)
                l_s[...] = jnp.zeros(l_s.shape, jnp.float32)
                acc_s[...] = jnp.zeros(acc_s.shape, jnp.float32)
            else:
                stats = s_ref[:, :, group * LANES :].reshape(every, LANES)
                lane0 = lax.broadcasted_iota(jnp.int32, (every, LANES), 1) == 0
                for j in range(group):
                    acc_s[j] = s_ref[:, :, j * LANES : (j + 1) * LANES].reshape(every, LANES)
                    m_s[j] = jnp.broadcast_to(stats[:, j : j + 1], (every, LANES))
                    total = jnp.broadcast_to(
                        stats[:, LANES // 2 + j : LANES // 2 + j + 1], (every, LANES)
                    )
                    l_s[j] = jnp.where(lane0, total, 0.0)

        live = kv_ref[:, 0] < LIVE_BELOW
        key = jnp.where(live, kv_ref[:, 0], 0.0).reshape(keys, LANES)
        value = jnp.where(live, kv_ref[:, 1], 0.0).reshape(keys, LANES)
        lane = lax.broadcasted_iota(jnp.int32, (take, slots, LANES), 2)
        bias = jnp.where(live | (lane != 0), 0.0, BIAS).reshape(keys, LANES)
        k_hi = key.astype(jnp.bfloat16)
        k_s[:, 0 * LANES : 1 * LANES] = k_hi
        k_s[:, 1 * LANES : 2 * LANES] = k_hi
        k_s[:, 2 * LANES : 3 * LANES] = (key - k_hi.astype(jnp.float32)).astype(jnp.bfloat16)
        k_s[:, 3 * LANES : 4 * LANES] = bias.astype(jnp.bfloat16)
        v_hi = value.astype(jnp.bfloat16)
        v_s[:, :LANES] = v_hi
        v_s[:, LANES:] = (value - v_hi.astype(jnp.float32)).astype(jnp.bfloat16)
        if with_mark:
            mark = jnp.max(jnp.max(kv_ref[:, 0].reshape(keys, LANES), axis=0, keepdims=True))
            mark = jnp.broadcast_to(mark, f_ref.shape)

            @pl.when(step == 0)
            def _():
                f_ref[...] = mark

            @pl.when(step > 0)
            def _():
                f_ref[...] = jnp.maximum(f_ref[...], mark)

        def score(t, j):
            return lax.dot_general(
                q_s[j],
                k_s[t * part : (t + 1) * part],
                (((1,), (1,)), ((), ())),
                preferred_element_type=jnp.float32,
            )

        def weigh(j, scores):
            old = m_s[j]
            fresh = jnp.maximum(old, jnp.max(scores, axis=1, keepdims=True))
            factor = jnp.exp2(old - fresh)
            weights = jnp.exp2(scores - jnp.tile(fresh, (1, part // LANES)))
            sums = weights[:, :LANES]
            for i in range(1, part // LANES):
                sums = sums + weights[:, i * LANES : (i + 1) * LANES]
            l_s[j] = l_s[j] * factor + sums
            m_s[j] = fresh
            w_hi = weights.astype(jnp.bfloat16)
            return factor, w_hi, (weights - w_hi.astype(jnp.float32)).astype(jnp.bfloat16)

        def gather(t, j, factor, w_hi, w_lo):
            at = slice(t * part, (t + 1) * part)
            both = jnp.dot(w_hi, v_s[at], preferred_element_type=jnp.float32)
            rest = jnp.dot(w_lo, v_s[at, :LANES], preferred_element_type=jnp.float32)
            acc_s[j] = acc_s[j] * factor + (both[:, :LANES] + both[:, LANES:] + rest)

        items = [(t, j) for t in range(keys // part) for j in range(group)]
        scores = score(*items[0])
        behind = None
        for n, item in enumerate(items):
            ahead = score(*items[n + 1]) if n + 1 < len(items) else None
            weighed = weigh(item[1], scores)
            if behind is not None:
                gather(*behind)
            behind = (*item, *weighed)
            scores = ahead
        gather(*behind)

        @pl.when(step == steps - 1)
        def _():
            lane = lax.broadcasted_iota(jnp.int32, (every, LANES), 1)
            stats = jnp.zeros((every, LANES), jnp.float32)
            for j in range(group):
                o_ref[:, :, j * LANES : (j + 1) * LANES] = acc_s[j].reshape(owners, rows, LANES)
                total = jnp.sum(l_s[j], axis=1, keepdims=True)
                stats = jnp.where(lane == j, m_s[j], stats)
                stats = jnp.where(lane == LANES // 2 + j, total, stats)
            o_ref[:, :, group * LANES :] = stats.reshape(owners, rows, LANES)

    state_spec = pl.BlockSpec((owners, rows, columns), lambda i, me: (0, 0, 0))
    in_specs = [
        pl.BlockSpec((every, width), lambda i, me: (0, 0)),
        pl.BlockSpec((take, 2, slots, LANES), lambda i, me: (i, 0, 0, 0)),
    ]
    args = (queries, kv)
    if not first:
        in_specs = [state_spec] + in_specs
        args = (state,) + args
    out_shape = [jax.ShapeDtypeStruct((owners, rows, columns), jnp.float32)]
    out_specs = [state_spec]
    if with_mark:
        out_shape.append(jax.ShapeDtypeStruct((ROWS8, LANES), jnp.float32))
        out_specs.append(pl.BlockSpec((ROWS8, LANES), lambda i, me: (0, 0)))
    out = pl.pallas_call(
        body,
        out_shape=out_shape,
        grid_spec=pltpu.PrefetchScalarGridSpec(
            num_scalar_prefetch=1,
            grid=(steps,),
            in_specs=in_specs,
            out_specs=out_specs,
            scratch_shapes=[
                pltpu.VMEM((group, every, 4 * LANES), jnp.bfloat16),
                pltpu.VMEM((group, every, LANES), jnp.float32),
                pltpu.VMEM((group, every, LANES), jnp.float32),
                pltpu.VMEM((group, every, LANES), jnp.float32),
                pltpu.VMEM((keys, 4 * LANES), jnp.bfloat16),
                pltpu.VMEM((keys, 2 * LANES), jnp.bfloat16),
            ],
        ),
        compiler_params=pltpu.CompilerParams(vmem_limit_bytes=50 * 2**20),
        name="attend_first" if first else "attend_more",
    )(me, *args)
    return out if with_mark else out[0]


def combine(parts):
    owners, rows, columns = parts.shape
    group = columns // LANES - 1

    def body(x_ref, o_ref):
        for h in range(owners // HALVES):
            a, b = HALVES * h, HALVES * h + 1
            stats_a = x_ref[a, :, group * LANES :]
            stats_b = x_ref[b, :, group * LANES :]
            peak = jnp.maximum(stats_a, stats_b)
            fa, fb = jnp.exp2(stats_a - peak), jnp.exp2(stats_b - peak)
            total = pltpu.roll(stats_a, LANES // 2, 1) * fa + pltpu.roll(stats_b, LANES // 2, 1) * fb
            fa, fb = fa / total, fb / total
            for j in range(group):
                cols = slice(j * LANES, (j + 1) * LANES)
                out = x_ref[a, :, cols] * fa[:, j : j + 1] + x_ref[b, :, cols] * fb[:, j : j + 1]
                o_ref[:, (h * group + j) * LANES : (h * group + j + 1) * LANES] = out

    return pl.pallas_call(
        body,
        out_shape=jax.ShapeDtypeStruct((rows, owners // HALVES * group * LANES), jnp.float32),
        compiler_params=pltpu.CompilerParams(vmem_limit_bytes=20 * 2**20),
        name="combine",
    )(parts)


def on_device(visual, text_queries, kv_weight, placement):
    axes = ("grp", "blk")
    segments = lax.axis_size("grp")
    owners = lax.axis_size("blk")
    devices = segments * owners
    blocks = placement.shape[0]
    block_rows = visual.shape[0] // blocks
    rows = text_queries.shape[0]
    per_pair = max(2, blocks // devices + 1)
    most = owners * per_pair // HALVES
    caps = CAPS + (most - CAPS[0],)
    common = sum(CAPS)

    owner = placement.reshape(blocks)
    packed = project_and_pack(placement, visual, kv_weight, caps, segments)

    me = lax.axis_index("blk").astype(jnp.int32)
    text, *packed = lax.optimization_barrier((text_queries, *packed))
    width = text.shape[1] // KV_HEADS
    pieces = []
    for away in range(KV_HEADS):
        z = lax.shift_right_logical(me, HALVES.bit_length() - 1) ^ away
        piece = lax.dynamic_slice_in_dim(text, z * width, width, 1)
        if away:
            pairs = [(k, k ^ (away * HALVES)) for k in range(owners)]
            piece = lax.ppermute(piece, "blk", pairs)
        pieces.append(piece)
    own_core = jnp.concatenate(pieces, axis=0)
    other = lax.ppermute(own_core, "blk", [(k, k ^ 1) for k in range(owners)])
    queries = jnp.concatenate([own_core, other], axis=0)
    packed[1], queries = lax.optimization_barrier((packed[1], queries))
    me = me.reshape(1)

    def exchange(chunk):
        chunk = chunk.reshape(devices, 2, -1, LANES)
        return lax.all_to_all(chunk, axes, 0, 0, tiled=True)

    def beyond(slots, state):
        counts = jnp.sum(
            (owner[None, :] // owners == jnp.arange(segments)[:, None]).astype(jnp.int32), axis=1
        )
        mine = jnp.max(counts) > HALVES * common
        half = jnp.arange(HALVES)[None, :]
        held = (counts[:, None] + (HALVES - 1) - half) // HALVES - caps[0]
        held = jnp.where(mine, held, 0)[:, None, :, None, None, None]
        slot = (jnp.arange(slots * block_rows) // block_rows)[:, None]
        chunk = packed[2][:, :, :, :, : slots * block_rows]
        chunk = jnp.where(slot < held, chunk, EMPTY[0])
        return attend(state, queries, me, exchange(chunk), rows)

    first = exchange(packed[0])
    second = exchange(packed[1])
    state = attend(None, queries, me, first, rows)
    state, mark = attend(state, queries, me, second, rows, with_mark=True)
    mark = mark[0, 0]
    level = (mark > 2 * EMPTY[0]).astype(jnp.int32) + (mark > 2 * EMPTY[1]).astype(jnp.int32)
    state = lax.switch(
        level,
        [
            lambda s: s,
            lambda s: beyond(CAPS[1] + SPARE, s),
            lambda s: beyond(caps[2], s),
        ],
        state,
    )
    parts = lax.all_to_all(state, "blk", 0, 0, tiled=True)
    return combine(parts)


def solution(mesh):
    placed = (P(("grp", "blk"), None), P(("grp", "blk"), None), P(), P(("grp", "blk"), None))
    return jax.shard_map(
        on_device, mesh=mesh, in_specs=placed, out_specs=P(("grp", "blk"), None), check_vma=False
    )
```

```python
import functools
import math

import jax
import jax.numpy as jnp
from jax import lax
from jax.experimental import pallas as pl
from jax.experimental.pallas import tpu as pltpu
from jax.sharding import PartitionSpec as P

HEADS = 28
KV_HEADS = 4
GROUP = HEADS // KV_HEADS
LANES = 128
HALVES = 2
CAPS = (4, 1)
SPARE = 1
BIAS = -(2.0**99)
EMPTY = (1e30, 4e30, 16e30)
LIVE_BELOW = 1e29
ROWS8 = 8
TILE = 1024
PART = 512
DEPTHS = (512, 1024)


def project_and_pack(placement, visual, kv_weight, caps, segments):
    rows, dv = visual.shape
    width = kv_weight.shape[1]
    blocks = placement.shape[0]
    block_rows = rows // blocks
    owners = KV_HEADS * HALVES
    common = caps[0] + caps[1]
    cuts = [0]
    while cuts[-1] < dv:
        cuts.append(min(dv, cuts[-1] + DEPTHS[min(len(cuts) - 1, len(DEPTHS) - 1)]))
    parts = list(zip(cuts[:-1], cuts[1:]))
    few = math.gcd(segments, 4)

    def body(owner_ref, x_hbm, w_hbm, o1, o2, o3, x, w, buf, mark1, mark2, code, table, sems):
        loads = []
        for i, (a, b) in enumerate(parts):
            loads.append(
                (
                    pltpu.make_async_copy(x_hbm.at[:, a:b], x.at[:, a:b], sems.at[2 * i]),
                    pltpu.make_async_copy(w_hbm.at[a:b], w.at[a:b], sems.at[2 * i + 1]),
                )
            )
            for load in loads[-1]:
                load.start()
        sem, sem2 = (sems.at[2 * len(parts) + i] for i in range(2))
        sem1 = sems.at[2 * len(parts) + 2 :]

        segment = lax.shift_right_logical(owner_ref[...], owners.bit_length() - 1)
        segment = segment.astype(jnp.float32)
        shape = (blocks, blocks)
        i = lax.broadcasted_iota(jnp.int32, shape, 0)
        j = lax.broadcasted_iota(jnp.int32, shape, 1)
        column = jnp.broadcast_to(segment, shape)
        line = jnp.sum(jnp.where(i == j, column, 0.0), axis=0, keepdims=True)
        before = jnp.where((column == line) & (i < j), 1.0, 0.0)
        rank = jnp.sum(before, axis=0, keepdims=True)
        top = jnp.max(rank) + 1.0
        rank = rank.astype(jnp.int32)
        half = jnp.bitwise_and(rank, HALVES - 1)
        slot = lax.shift_right_logical(rank, HALVES.bit_length() - 1)
        code[...] = (line.astype(jnp.int32) * HALVES + half) * ROWS8 + slot
        codes = pltpu.make_async_copy(code, table, sem)
        codes.start()
        level = (top > HALVES * common).astype(jnp.int32)
        level = level + (top > HALVES * (common + SPARE)).astype(jnp.int32)
        mark1[...] = jnp.full(mark1.shape, EMPTY[0], jnp.float32)
        mark = jnp.where(level == 0, EMPTY[0], jnp.where(level == 1, EMPTY[1], EMPTY[2]))
        mark2[...] = jnp.broadcast_to(mark.astype(jnp.float32), mark2.shape)
        fills = [pltpu.make_async_copy(mark2, o2.at[:, :, :, 0], sem2)]
        for g in range(0, segments, mark1.shape[0]):
            to = o1.at[g : g + mark1.shape[0], :, :, 0]
            fills.append(pltpu.make_async_copy(mark1, to, sem1.at[g // mark1.shape[0]]))
        for copy in fills:
            copy.start()
        codes.wait()

        for i, (a, b) in enumerate(parts):
            for load in loads[i]:
                load.wait()
            for kind in range(2):
                for h in range(0, KV_HEADS, 2):
                    c = (kind * KV_HEADS + h) * LANES
                    part = jnp.dot(
                        x[:, a:b], w[a:b, c : c + 2 * LANES], preferred_element_type=jnp.float32
                    )
                    for k in range(2):
                        piece = part[:, k * LANES : (k + 1) * LANES]
                        buf[h + k, kind] = piece if i == 0 else buf[h + k, kind] + piece

        for copy in fills:
            copy.wait()

        def send(j, c):
            at = table[0, j]
            slot = at % ROWS8
            half = at // ROWS8 % HALVES
            seg = at // (ROWS8 * HALVES)
            src = buf.at[:, :, pl.ds(pl.multiple_of(j * block_rows, ROWS8), block_rows), :]

            def copy(out, slot):
                rows_at = pl.ds(pl.multiple_of(slot * block_rows, ROWS8), block_rows)
                dst = out.at[seg, :, half, :, rows_at, :]
                pltpu.make_async_copy(src, dst, sem).start()

            @pl.when(slot < caps[0])
            def _():
                copy(o1, slot)

            @pl.when(slot >= caps[0])
            def _():
                @pl.when(level == 0)
                def _():
                    copy(o2, slot - caps[0])

                @pl.when(level > 0)
                def _():
                    copy(o3, slot - caps[0])

            return c

        lax.fori_loop(0, blocks, send, 0, unroll=4)
        pltpu.make_async_copy(buf, buf, sem).wait()

    shapes = [
        pltpu.HBM((segments, KV_HEADS, HALVES, 2, cap * block_rows, LANES), jnp.float32)
        for cap in caps
    ]
    hbm = pl.BlockSpec(memory_space=pltpu.HBM)
    return pl.pallas_call(
        body,
        out_shape=shapes,
        in_specs=[pl.BlockSpec(memory_space=pltpu.VMEM), hbm, hbm],
        out_specs=[hbm for _ in caps],
        scratch_shapes=[
            pltpu.VMEM((rows, dv), jnp.bfloat16),
            pltpu.VMEM((dv, width), jnp.bfloat16),
            pltpu.VMEM((KV_HEADS, 2, rows, LANES), jnp.float32),
            pltpu.VMEM((few, KV_HEADS, HALVES, caps[0] * block_rows, LANES), jnp.float32),
            pltpu.VMEM((segments, KV_HEADS, HALVES, caps[1] * block_rows, LANES), jnp.float32),
            pltpu.VMEM((1, blocks), jnp.int32),
            pltpu.SMEM((1, blocks), jnp.int32),
            pltpu.SemaphoreType.DMA((2 * len(parts) + 2 + segments // few,)),
        ],
        compiler_params=pltpu.CompilerParams(vmem_limit_bytes=40 * 2**20),
        name="project_and_pack",
    )(
        placement,
        pltpu.with_memory_space_constraint(visual, pltpu.HBM),
        pltpu.with_memory_space_constraint(kv_weight, pltpu.HBM),
    )


def attend(state, queries, me, kv, rows, with_mark=False):
    every = HALVES * queries[0].shape[0]
    width = queries[0].shape[1]
    group = width // LANES
    sources, _, slots, _ = kv.shape
    scale = LANES ** (-0.5) * math.log2(math.e)
    take = min(sources, 1 << (TILE // slots).bit_length() - 1)
    while sources % take:
        take //= 2
    keys = take * slots
    part = PART
    while keys % part:
        part //= 2
    steps = sources // take
    first = state is None
    owners = every // rows
    columns = (group + 1) * LANES

    def body(me_ref, *refs):
        refs = list(refs)
        s_ref = None if first else refs.pop(0)
        own_ref, other_ref, kv_ref, o_ref = refs[:4]
        f_ref = refs[4] if with_mark else None
        q_s, m_s, l_s, acc_s, k_s, v_s = refs[-6:]
        step = pl.program_id(0)

        @pl.when(step == 0)
        def _():
            ones = (lax.broadcasted_iota(jnp.int32, (every, LANES), 1) == 0).astype(jnp.float32)
            ones = ones.astype(jnp.bfloat16)
            core = jnp.bitwise_and(me_ref[0], HALVES - 1)
            for p in range(owners):
                at = slice(p // HALVES * rows, (p // HALVES + 1) * rows)
                to = slice(p * rows, (p + 1) * rows)
                for j in range(group):
                    cols = slice(j * LANES, (j + 1) * LANES)
                    x = jnp.where(core == p % HALVES, own_ref[at, cols], other_ref[at, cols]) * scale
                    hi = x.astype(jnp.bfloat16)
                    lo = (x - hi.astype(jnp.float32)).astype(jnp.bfloat16)
                    q_s[j, to, 0 * LANES : 1 * LANES] = hi
                    q_s[j, to, 1 * LANES : 2 * LANES] = lo
                    q_s[j, to, 2 * LANES : 3 * LANES] = hi
            for j in range(group):
                q_s[j, :, 3 * LANES : 4 * LANES] = ones
            if first:
                m_s[...] = jnp.full(m_s.shape, BIAS, jnp.float32)
                l_s[...] = jnp.zeros(l_s.shape, jnp.float32)
                acc_s[...] = jnp.zeros(acc_s.shape, jnp.float32)
            else:
                stats = s_ref[:, :, group * LANES :].reshape(every, LANES)
                lane0 = lax.broadcasted_iota(jnp.int32, (every, LANES), 1) == 0
                for j in range(group):
                    acc_s[j] = s_ref[:, :, j * LANES : (j + 1) * LANES].reshape(every, LANES)
                    m_s[j] = jnp.broadcast_to(stats[:, j : j + 1], (every, LANES))
                    total = jnp.broadcast_to(
                        stats[:, LANES // 2 + j : LANES // 2 + j + 1], (every, LANES)
                    )
                    l_s[j] = jnp.where(lane0, total, 0.0)

        live = kv_ref[:, 0] < LIVE_BELOW
        key = jnp.where(live, kv_ref[:, 0], 0.0).reshape(keys, LANES)
        value = jnp.where(live, kv_ref[:, 1], 0.0).reshape(keys, LANES)
        lane = lax.broadcasted_iota(jnp.int32, (take, slots, LANES), 2)
        bias = jnp.where(live | (lane != 0), 0.0, BIAS).reshape(keys, LANES)
        k_hi = key.astype(jnp.bfloat16)
        k_s[:, 0 * LANES : 1 * LANES] = k_hi
        k_s[:, 1 * LANES : 2 * LANES] = k_hi
        k_s[:, 2 * LANES : 3 * LANES] = (key - k_hi.astype(jnp.float32)).astype(jnp.bfloat16)
        k_s[:, 3 * LANES : 4 * LANES] = bias.astype(jnp.bfloat16)
        v_hi = value.astype(jnp.bfloat16)
        v_s[:, :LANES] = v_hi
        v_s[:, LANES:] = (value - v_hi.astype(jnp.float32)).astype(jnp.bfloat16)
        if with_mark:
            mark = jnp.max(jnp.max(kv_ref[:, 0].reshape(keys, LANES), axis=0, keepdims=True))
            mark = jnp.broadcast_to(mark, f_ref.shape)

            @pl.when(step == 0)
            def _():
                f_ref[...] = mark

            @pl.when(step > 0)
            def _():
                f_ref[...] = jnp.maximum(f_ref[...], mark)

        def score(t, j):
            return lax.dot_general(
                q_s[j],
                k_s[t * part : (t + 1) * part],
                (((1,), (1,)), ((), ())),
                preferred_element_type=jnp.float32,
            )

        def weigh(j, scores):
            old = m_s[j]
            fresh = jnp.maximum(old, jnp.max(scores, axis=1, keepdims=True))
            factor = jnp.exp2(old - fresh)
            weights = jnp.exp2(scores - jnp.tile(fresh, (1, part // LANES)))
            sums = weights[:, :LANES]
            for i in range(1, part // LANES):
                sums = sums + weights[:, i * LANES : (i + 1) * LANES]
            l_s[j] = l_s[j] * factor + sums
            m_s[j] = fresh
            w_hi = weights.astype(jnp.bfloat16)
            return factor, w_hi, (weights - w_hi.astype(jnp.float32)).astype(jnp.bfloat16)

        def gather(t, j, factor, w_hi, w_lo):
            at = slice(t * part, (t + 1) * part)
            both = jnp.dot(w_hi, v_s[at], preferred_element_type=jnp.float32)
            rest = jnp.dot(w_lo, v_s[at, :LANES], preferred_element_type=jnp.float32)
            acc_s[j] = acc_s[j] * factor + (both[:, :LANES] + both[:, LANES:] + rest)

        items = [(t, j) for t in range(keys // part) for j in range(group)]
        scores = score(*items[0])
        behind = None
        for n, item in enumerate(items):
            ahead = score(*items[n + 1]) if n + 1 < len(items) else None
            weighed = weigh(item[1], scores)
            if behind is not None:
                gather(*behind)
            behind = (*item, *weighed)
            scores = ahead
        gather(*behind)

        @pl.when(step == steps - 1)
        def _():
            lane = lax.broadcasted_iota(jnp.int32, (every, LANES), 1)
            stats = jnp.zeros((every, LANES), jnp.float32)
            for j in range(group):
                o_ref[:, :, j * LANES : (j + 1) * LANES] = acc_s[j].reshape(owners, rows, LANES)
                total = jnp.sum(l_s[j], axis=1, keepdims=True)
                stats = jnp.where(lane == j, m_s[j], stats)
                stats = jnp.where(lane == LANES // 2 + j, total, stats)
            o_ref[:, :, group * LANES :] = stats.reshape(owners, rows, LANES)

    state_spec = pl.BlockSpec((owners, rows, columns), lambda i, me: (0, 0, 0))
    in_specs = [
        pl.BlockSpec((every // HALVES, width), lambda i, me: (0, 0)),
        pl.BlockSpec((every // HALVES, width), lambda i, me: (0, 0)),
        pl.BlockSpec((take, 2, slots, LANES), lambda i, me: (i, 0, 0, 0)),
    ]
    args = (*queries, kv)
    if not first:
        in_specs = [state_spec] + in_specs
        args = (state,) + args
    out_shape = [jax.ShapeDtypeStruct((owners, rows, columns), jnp.float32)]
    out_specs = [state_spec]
    if with_mark:
        out_shape.append(jax.ShapeDtypeStruct((ROWS8, LANES), jnp.float32))
        out_specs.append(pl.BlockSpec((ROWS8, LANES), lambda i, me: (0, 0)))
    out = pl.pallas_call(
        body,
        out_shape=out_shape,
        grid_spec=pltpu.PrefetchScalarGridSpec(
            num_scalar_prefetch=1,
            grid=(steps,),
            in_specs=in_specs,
            out_specs=out_specs,
            scratch_shapes=[
                pltpu.VMEM((group, every, 4 * LANES), jnp.bfloat16),
                pltpu.VMEM((group, every, LANES), jnp.float32),
                pltpu.VMEM((group, every, LANES), jnp.float32),
                pltpu.VMEM((group, every, LANES), jnp.float32),
                pltpu.VMEM((keys, 4 * LANES), jnp.bfloat16),
                pltpu.VMEM((keys, 2 * LANES), jnp.bfloat16),
            ],
        ),
        compiler_params=pltpu.CompilerParams(vmem_limit_bytes=50 * 2**20),
        name="attend_first" if first else "attend_more",
    )(me, *args)
    return out if with_mark else out[0]


def combine(parts):
    owners, rows, columns = parts.shape
    group = columns // LANES - 1

    def body(x_ref, o_ref):
        for h in range(owners // HALVES):
            a, b = HALVES * h, HALVES * h + 1
            stats_a = x_ref[a, :, group * LANES :]
            stats_b = x_ref[b, :, group * LANES :]
            peak = jnp.maximum(stats_a, stats_b)
            fa, fb = jnp.exp2(stats_a - peak), jnp.exp2(stats_b - peak)
            total = pltpu.roll(stats_a, LANES // 2, 1) * fa + pltpu.roll(stats_b, LANES // 2, 1) * fb
            fa, fb = fa / total, fb / total
            for j in range(group):
                cols = slice(j * LANES, (j + 1) * LANES)
                out = x_ref[a, :, cols] * fa[:, j : j + 1] + x_ref[b, :, cols] * fb[:, j : j + 1]
                o_ref[:, (h * group + j) * LANES : (h * group + j + 1) * LANES] = out

    return pl.pallas_call(
        body,
        out_shape=jax.ShapeDtypeStruct((rows, owners // HALVES * group * LANES), jnp.float32),
        compiler_params=pltpu.CompilerParams(vmem_limit_bytes=20 * 2**20),
        name="combine",
    )(parts)


def on_device(visual, text_queries, kv_weight, placement):
    axes = ("grp", "blk")
    segments = lax.axis_size("grp")
    owners = lax.axis_size("blk")
    devices = segments * owners
    blocks = placement.shape[0]
    block_rows = visual.shape[0] // blocks
    rows = text_queries.shape[0]
    per_pair = max(2, blocks // devices + 1)
    most = owners * per_pair // HALVES
    caps = CAPS + (most - CAPS[0],)
    common = sum(CAPS)

    owner = placement.reshape(blocks)
    packed = list(project_and_pack(placement, visual, kv_weight, caps, segments))

    q = text_queries.reshape(rows, KV_HEADS, -1).transpose(1, 0, 2)
    same_core = [[z * HALVES + c for z in range(KV_HEADS)] for c in range(HALVES)]
    own_core = lax.all_to_all(q, "blk", 0, 0, axis_index_groups=same_core, tiled=True)
    own_core = own_core.reshape(KV_HEADS * rows, -1)
    other = lax.ppermute(own_core, "blk", [(k, k ^ 1) for k in range(owners)])
    packed[1], other = lax.optimization_barrier((packed[1], other))
    queries = (own_core, other)
    me = lax.axis_index("blk").astype(jnp.int32).reshape(1)

    def exchange(chunk):
        chunk = chunk.reshape(devices, 2, -1, LANES)
        return lax.all_to_all(chunk, axes, 0, 0, tiled=True)

    def beyond(slots, state):
        counts = jnp.sum(
            (owner[None, :] // owners == jnp.arange(segments)[:, None]).astype(jnp.int32), axis=1
        )
        mine = jnp.max(counts) > HALVES * common
        half = jnp.arange(HALVES)[None, :]
        held = (counts[:, None] + (HALVES - 1) - half) // HALVES - caps[0]
        held = jnp.where(mine, held, 0)[:, None, :, None, None, None]
        slot = (jnp.arange(slots * block_rows) // block_rows)[:, None]
        chunk = packed[2][:, :, :, :, : slots * block_rows]
        chunk = jnp.where(slot < held, chunk, EMPTY[0])
        return attend(state, queries, me, exchange(chunk), rows)

    first = exchange(packed[0])
    second = exchange(packed[1])
    state = attend(None, queries, me, first, rows)
    state, mark = attend(state, queries, me, second, rows, with_mark=True)
    mark = mark[0, 0]
    level = (mark > 2 * EMPTY[0]).astype(jnp.int32) + (mark > 2 * EMPTY[1]).astype(jnp.int32)
    state = lax.switch(
        level,
        [
            lambda s: s,
            lambda s: beyond(CAPS[1] + SPARE, s),
            lambda s: beyond(caps[2], s),
        ],
        state,
    )
    parts = lax.all_to_all(state, "blk", 0, 0, tiled=True)
    return combine(parts)


def solution(mesh):
    placed = (P(("grp", "blk"), None), P(("grp", "blk"), None), P(), P(("grp", "blk"), None))
    return jax.shard_map(
        on_device, mesh=mesh, in_specs=placed, out_specs=P(("grp", "blk"), None), check_vma=False
    )
```

```python
import functools
import math

import jax
import jax.numpy as jnp
from jax import lax
from jax.experimental import pallas as pl
from jax.experimental.pallas import tpu as pltpu
from jax.sharding import PartitionSpec as P

HEADS = 28
KV_HEADS = 4
GROUP = HEADS // KV_HEADS
LANES = 128
HALVES = 2
CAPS = (4, 1)
SPARE = 1
BIAS = -(2.0**99)
EMPTY = (1e30, 4e30, 16e30)
LIVE_BELOW = 1e29
ROWS8 = 8
TILE = 1024
PART = 512
DEPTHS = (512, 1024)


def project_and_pack(placement, visual, kv_weight, caps, segments):
    rows, dv = visual.shape
    width = kv_weight.shape[1]
    blocks = placement.shape[1]
    block_rows = rows // blocks
    owners = KV_HEADS * HALVES
    common = caps[0] + caps[1]
    cuts = [0]
    while cuts[-1] < dv:
        cuts.append(min(dv, cuts[-1] + DEPTHS[min(len(cuts) - 1, len(DEPTHS) - 1)]))
    parts = list(zip(cuts[:-1], cuts[1:]))
    few = math.gcd(segments, 4)

    def body(owner_ref, x_hbm, w_hbm, o1, o2, o3, x, w, buf, mark1, mark2, code, table, sems):
        loads = []
        for i, (a, b) in enumerate(parts):
            loads.append(
                (
                    pltpu.make_async_copy(x_hbm.at[:, a:b], x.at[:, a:b], sems.at[2 * i]),
                    pltpu.make_async_copy(w_hbm.at[a:b], w.at[a:b], sems.at[2 * i + 1]),
                )
            )
            for load in loads[-1]:
                load.start()
        sem, sem2 = (sems.at[2 * len(parts) + i] for i in range(2))
        sem1 = sems.at[2 * len(parts) + 2 :]

        segment = lax.shift_right_logical(owner_ref[...], owners.bit_length() - 1)
        line = segment.astype(jnp.float32)
        shape = (blocks, blocks)
        i = lax.broadcasted_iota(jnp.int32, shape, 0)
        j = lax.broadcasted_iota(jnp.int32, shape, 1)
        column = jnp.sum(jnp.where(i == j, line, 0.0), axis=1, keepdims=True)
        before = jnp.where((column == line) & (i < j), 1.0, 0.0)
        rank = jnp.sum(before, axis=0, keepdims=True)
        top = jnp.max(rank) + 1.0
        rank = rank.astype(jnp.int32)
        half = jnp.bitwise_and(rank, HALVES - 1)
        slot = lax.shift_right_logical(rank, HALVES.bit_length() - 1)
        code[...] = (line.astype(jnp.int32) * HALVES + half) * ROWS8 + slot
        codes = pltpu.make_async_copy(code, table, sem)
        codes.start()
        level = (top > HALVES * common).astype(jnp.int32)
        level = level + (top > HALVES * (common + SPARE)).astype(jnp.int32)
        mark1[...] = jnp.full(mark1.shape, EMPTY[0], jnp.float32)
        mark = jnp.where(level == 0, EMPTY[0], jnp.where(level == 1, EMPTY[1], EMPTY[2]))
        mark2[...] = jnp.broadcast_to(mark.astype(jnp.float32), mark2.shape)
        fills = [pltpu.make_async_copy(mark2, o2.at[:, :, :, :, :LANES], sem2)]
        for g in range(0, segments, mark1.shape[0]):
            to = o1.at[g : g + mark1.shape[0], :, :, :, :LANES]
            fills.append(pltpu.make_async_copy(mark1, to, sem1.at[g // mark1.shape[0]]))
        for copy in fills:
            copy.start()
        codes.wait()

        for i, (a, b) in enumerate(parts):
            for load in loads[i]:
                load.wait()
            for kind in range(2):
                for h in range(0, KV_HEADS, 2):
                    c = (kind * KV_HEADS + h) * LANES
                    part = jnp.dot(
                        x[:, a:b], w[a:b, c : c + 2 * LANES], preferred_element_type=jnp.float32
                    )
                    at = slice(kind * LANES, (kind + 1) * LANES)
                    for k in range(2):
                        piece = part[:, k * LANES : (k + 1) * LANES]
                        buf[h + k, :, at] = piece if i == 0 else buf[h + k, :, at] + piece

        for copy in fills:
            copy.wait()

        def send(j, c):
            at = table[0, j]
            slot = at % ROWS8
            half = at // ROWS8 % HALVES
            seg = at // (ROWS8 * HALVES)
            src = buf.at[:, pl.ds(pl.multiple_of(j * block_rows, ROWS8), block_rows), :]

            def copy(out, slot):
                rows_at = pl.ds(pl.multiple_of(slot * block_rows, ROWS8), block_rows)
                dst = out.at[seg, :, half, rows_at, :]
                pltpu.make_async_copy(src, dst, sem).start()

            @pl.when(slot < caps[0])
            def _():
                copy(o1, slot)

            @pl.when(slot >= caps[0])
            def _():
                @pl.when(level == 0)
                def _():
                    copy(o2, slot - caps[0])

                @pl.when(level > 0)
                def _():
                    copy(o3, slot - caps[0])

            return c

        lax.fori_loop(0, blocks, send, 0, unroll=4)
        pltpu.make_async_copy(buf, buf, sem).wait()

    shapes = [
        pltpu.HBM((segments, KV_HEADS, HALVES, cap * block_rows, 2 * LANES), jnp.float32)
        for cap in caps
    ]
    hbm = pl.BlockSpec(memory_space=pltpu.HBM)
    return pl.pallas_call(
        body,
        out_shape=shapes,
        in_specs=[pl.BlockSpec(memory_space=pltpu.VMEM), hbm, hbm],
        out_specs=[hbm for _ in caps],
        scratch_shapes=[
            pltpu.VMEM((rows, dv), jnp.bfloat16),
            pltpu.VMEM((dv, width), jnp.bfloat16),
            pltpu.VMEM((KV_HEADS, rows, 2 * LANES), jnp.float32),
            pltpu.VMEM((few, KV_HEADS, HALVES, caps[0] * block_rows, LANES), jnp.float32),
            pltpu.VMEM((segments, KV_HEADS, HALVES, caps[1] * block_rows, LANES), jnp.float32),
            pltpu.VMEM((1, blocks), jnp.int32),
            pltpu.SMEM((1, blocks), jnp.int32),
            pltpu.SemaphoreType.DMA((2 * len(parts) + 2 + segments // few,)),
        ],
        compiler_params=pltpu.CompilerParams(vmem_limit_bytes=40 * 2**20),
        name="project_and_pack",
    )(
        placement,
        pltpu.with_memory_space_constraint(visual, pltpu.HBM),
        pltpu.with_memory_space_constraint(kv_weight, pltpu.HBM),
    )


def split_heads(text):
    rows, width = text.shape[0], text.shape[1] // KV_HEADS

    def body(x_ref, o_ref):
        for h in range(KV_HEADS):
            o_ref[h] = x_ref[:, h * width : (h + 1) * width]

    return pl.pallas_call(
        body, out_shape=jax.ShapeDtypeStruct((KV_HEADS, rows, width), text.dtype), name="split_heads"
    )(text)


def attend(state, queries, me, kv, rows, with_mark=False):
    every = HALVES * queries[0].shape[0]
    width = queries[0].shape[1]
    group = width // LANES
    sources, slots, _ = kv.shape
    scale = LANES ** (-0.5) * math.log2(math.e)
    take = min(sources, 1 << (TILE // slots).bit_length() - 1)
    while sources % take:
        take //= 2
    keys = take * slots
    part = PART
    while keys % part:
        part //= 2
    steps = sources // take
    first = state is None
    owners = every // rows
    columns = (group + 1) * LANES

    def body(me_ref, *refs):
        refs = list(refs)
        s_ref = None if first else refs.pop(0)
        own_ref, other_ref, kv_ref, o_ref = refs[:4]
        f_ref = refs[4] if with_mark else None
        q_s, m_s, l_s, acc_s, k_s, v_s = refs[-6:]
        step = pl.program_id(0)

        @pl.when(step == 0)
        def _():
            ones = (lax.broadcasted_iota(jnp.int32, (every, LANES), 1) == 0).astype(jnp.float32)
            ones = ones.astype(jnp.bfloat16)
            core = jnp.bitwise_and(me_ref[0], HALVES - 1)
            for p in range(owners):
                at = slice(p // HALVES * rows, (p // HALVES + 1) * rows)
                to = slice(p * rows, (p + 1) * rows)
                for j in range(group):
                    cols = slice(j * LANES, (j + 1) * LANES)
                    x = jnp.where(core == p % HALVES, own_ref[at, cols], other_ref[at, cols]) * scale
                    hi = x.astype(jnp.bfloat16)
                    lo = (x - hi.astype(jnp.float32)).astype(jnp.bfloat16)
                    q_s[j, to, 0 * LANES : 1 * LANES] = hi
                    q_s[j, to, 1 * LANES : 2 * LANES] = lo
                    q_s[j, to, 2 * LANES : 3 * LANES] = hi
            for j in range(group):
                q_s[j, :, 3 * LANES : 4 * LANES] = ones
            if first:
                m_s[...] = jnp.full(m_s.shape, BIAS, jnp.float32)
                l_s[...] = jnp.zeros(l_s.shape, jnp.float32)
                acc_s[...] = jnp.zeros(acc_s.shape, jnp.float32)
            else:
                stats = s_ref[:, :, group * LANES :].reshape(every, LANES)
                lane0 = lax.broadcasted_iota(jnp.int32, (every, LANES), 1) == 0
                for j in range(group):
                    acc_s[j] = s_ref[:, :, j * LANES : (j + 1) * LANES].reshape(every, LANES)
                    m_s[j] = jnp.broadcast_to(stats[:, j : j + 1], (every, LANES))
                    total = jnp.broadcast_to(
                        stats[:, LANES // 2 + j : LANES // 2 + j + 1], (every, LANES)
                    )
                    l_s[j] = jnp.where(lane0, total, 0.0)

        live = kv_ref[:, :, :LANES] < LIVE_BELOW
        key = jnp.where(live, kv_ref[:, :, :LANES], 0.0).reshape(keys, LANES)
        value = jnp.where(live, kv_ref[:, :, LANES:], 0.0).reshape(keys, LANES)
        lane = lax.broadcasted_iota(jnp.int32, (take, slots, LANES), 2)
        bias = jnp.where(live | (lane != 0), 0.0, BIAS).reshape(keys, LANES)
        k_hi = key.astype(jnp.bfloat16)
        k_s[:, 0 * LANES : 1 * LANES] = k_hi
        k_s[:, 1 * LANES : 2 * LANES] = k_hi
        k_s[:, 2 * LANES : 3 * LANES] = (key - k_hi.astype(jnp.float32)).astype(jnp.bfloat16)
        k_s[:, 3 * LANES : 4 * LANES] = bias.astype(jnp.bfloat16)
        v_hi = value.astype(jnp.bfloat16)
        v_s[:, :LANES] = v_hi
        v_s[:, LANES:] = (value - v_hi.astype(jnp.float32)).astype(jnp.bfloat16)
        if with_mark:
            mark = jnp.max(jnp.max(kv_ref[:, :, :LANES].reshape(keys, LANES), axis=0, keepdims=True))
            level = (mark > 2 * EMPTY[0]).astype(jnp.int32)
            level = level + (mark > 2 * EMPTY[1]).astype(jnp.int32)

            @pl.when(step == 0)
            def _():
                f_ref[0, 0] = level

            @pl.when(step > 0)
            def _():
                f_ref[0, 0] = jnp.maximum(f_ref[0, 0], level)

        def score(t, j):
            return lax.dot_general(
                q_s[j],
                k_s[t * part : (t + 1) * part],
                (((1,), (1,)), ((), ())),
                preferred_element_type=jnp.float32,
            )

        def weigh(j, scores):
            old = m_s[j]
            fresh = jnp.maximum(old, jnp.max(scores, axis=1, keepdims=True))
            factor = jnp.exp2(old - fresh)
            weights = jnp.exp2(scores - jnp.tile(fresh, (1, part // LANES)))
            sums = weights[:, :LANES]
            for i in range(1, part // LANES):
                sums = sums + weights[:, i * LANES : (i + 1) * LANES]
            l_s[j] = l_s[j] * factor + sums
            m_s[j] = fresh
            w_hi = weights.astype(jnp.bfloat16)
            return factor, w_hi, (weights - w_hi.astype(jnp.float32)).astype(jnp.bfloat16)

        def gather(t, j, factor, w_hi, w_lo):
            at = slice(t * part, (t + 1) * part)
            both = jnp.dot(w_hi, v_s[at], preferred_element_type=jnp.float32)
            rest = jnp.dot(w_lo, v_s[at, :LANES], preferred_element_type=jnp.float32)
            acc_s[j] = acc_s[j] * factor + (both[:, :LANES] + both[:, LANES:] + rest)

        items = [(t, j) for t in range(keys // part) for j in range(group)]
        scores = score(*items[0])
        behind = None
        for n, item in enumerate(items):
            ahead = score(*items[n + 1]) if n + 1 < len(items) else None
            weighed = weigh(item[1], scores)
            if behind is not None:
                gather(*behind)
            behind = (*item, *weighed)
            scores = ahead
        gather(*behind)

        @pl.when(step == steps - 1)
        def _():
            lane = lax.broadcasted_iota(jnp.int32, (every, LANES), 1)
            stats = jnp.zeros((every, LANES), jnp.float32)
            for j in range(group):
                o_ref[:, :, j * LANES : (j + 1) * LANES] = acc_s[j].reshape(owners, rows, LANES)
                total = jnp.sum(l_s[j], axis=1, keepdims=True)
                stats = jnp.where(lane == j, m_s[j], stats)
                stats = jnp.where(lane == LANES // 2 + j, total, stats)
            o_ref[:, :, group * LANES :] = stats.reshape(owners, rows, LANES)

    state_spec = pl.BlockSpec((owners, rows, columns), lambda i, me: (0, 0, 0))
    in_specs = [
        pl.BlockSpec((every // HALVES, width), lambda i, me: (0, 0)),
        pl.BlockSpec((every // HALVES, width), lambda i, me: (0, 0)),
        pl.BlockSpec((take, slots, 2 * LANES), lambda i, me: (i, 0, 0)),
    ]
    args = (*queries, kv)
    if not first:
        in_specs = [state_spec] + in_specs
        args = (state,) + args
    out_shape = [jax.ShapeDtypeStruct((owners, rows, columns), jnp.float32)]
    out_specs = [state_spec]
    if with_mark:
        out_shape.append(jax.ShapeDtypeStruct((1, 1), jnp.int32))
        out_specs.append(pl.BlockSpec(memory_space=pltpu.SMEM))
    out = pl.pallas_call(
        body,
        out_shape=out_shape,
        grid_spec=pltpu.PrefetchScalarGridSpec(
            num_scalar_prefetch=1,
            grid=(steps,),
            in_specs=in_specs,
            out_specs=out_specs,
            scratch_shapes=[
                pltpu.VMEM((group, every, 4 * LANES), jnp.bfloat16),
                pltpu.VMEM((group, every, LANES), jnp.float32),
                pltpu.VMEM((group, every, LANES), jnp.float32),
                pltpu.VMEM((group, every, LANES), jnp.float32),
                pltpu.VMEM((keys, 4 * LANES), jnp.bfloat16),
                pltpu.VMEM((keys, 2 * LANES), jnp.bfloat16),
            ],
        ),
        compiler_params=pltpu.CompilerParams(vmem_limit_bytes=50 * 2**20),
        name="attend_first" if first else "attend_more",
    )(me, *args)
    return out if with_mark else out[0]


def combine(parts):
    owners, rows, columns = parts.shape
    group = columns // LANES - 1

    def body(x_ref, o_ref):
        for h in range(owners // HALVES):
            a, b = HALVES * h, HALVES * h + 1
            stats_a = x_ref[a, :, group * LANES :]
            stats_b = x_ref[b, :, group * LANES :]
            peak = jnp.maximum(stats_a, stats_b)
            fa, fb = jnp.exp2(stats_a - peak), jnp.exp2(stats_b - peak)
            total = pltpu.roll(stats_a, LANES // 2, 1) * fa + pltpu.roll(stats_b, LANES // 2, 1) * fb
            fa, fb = fa / total, fb / total
            for j in range(group):
                cols = slice(j * LANES, (j + 1) * LANES)
                out = x_ref[a, :, cols] * fa[:, j : j + 1] + x_ref[b, :, cols] * fb[:, j : j + 1]
                o_ref[:, (h * group + j) * LANES : (h * group + j + 1) * LANES] = out

    return pl.pallas_call(
        body,
        out_shape=jax.ShapeDtypeStruct((rows, owners // HALVES * group * LANES), jnp.float32),
        compiler_params=pltpu.CompilerParams(vmem_limit_bytes=20 * 2**20),
        name="combine",
    )(parts)


def on_device(visual, text_queries, kv_weight, placement):
    axes = ("grp", "blk")
    segments = lax.axis_size("grp")
    owners = lax.axis_size("blk")
    devices = segments * owners
    blocks = placement.shape[0]
    block_rows = visual.shape[0] // blocks
    rows = text_queries.shape[0]
    per_pair = max(2, blocks // devices + 1)
    most = owners * per_pair // HALVES
    caps = CAPS + (most - CAPS[0],)
    common = sum(CAPS)

    owner = placement.reshape(blocks)
    packed = list(project_and_pack(owner.reshape(1, blocks), visual, kv_weight, caps, segments))

    q = split_heads(text_queries)
    same_core = [[z * HALVES + c for z in range(KV_HEADS)] for c in range(HALVES)]
    own_core = lax.all_to_all(q, "blk", 0, 0, axis_index_groups=same_core, tiled=True)
    own_core = own_core.reshape(KV_HEADS * rows, -1)
    other = lax.ppermute(own_core, "blk", [(k, k ^ 1) for k in range(owners)])
    packed[1], other = lax.optimization_barrier((packed[1], other))
    queries = (own_core, other)
    me = lax.axis_index("blk").astype(jnp.int32).reshape(1)

    def exchange(chunk):
        chunk = chunk.reshape(devices, -1, 2 * LANES)
        return lax.all_to_all(chunk, axes, 0, 0, tiled=True)

    def beyond(slots, state):
        counts = jnp.sum(
            (owner[None, :] // owners == jnp.arange(segments)[:, None]).astype(jnp.int32), axis=1
        )
        mine = jnp.max(counts) > HALVES * common
        half = jnp.arange(HALVES)[None, :]
        held = (counts[:, None] + (HALVES - 1) - half) // HALVES - caps[0]
        held = jnp.where(mine, held, 0)[:, None, :, None, None]
        slot = (jnp.arange(slots * block_rows) // block_rows)[:, None]
        chunk = packed[2][:, :, :, : slots * block_rows]
        chunk = jnp.where(slot < held, chunk, EMPTY[0])
        return attend(state, queries, me, exchange(chunk), rows)

    first = exchange(packed[0])
    second = exchange(packed[1])
    state = attend(None, queries, me, first, rows)
    state, level = attend(state, queries, me, second, rows, with_mark=True)
    state = lax.switch(
        level[0, 0],
        [
            lambda s: s,
            lambda s: beyond(CAPS[1] + SPARE, s),
            lambda s: beyond(caps[2], s),
        ],
        state,
    )
    parts = lax.all_to_all(state, "blk", 0, 0, tiled=True)
    return combine(parts)


def solution(mesh):
    placed = (P(("grp", "blk"), None), P(("grp", "blk"), None), P(), P(("grp", "blk"), None))
    return jax.shard_map(
        on_device, mesh=mesh, in_specs=placed, out_specs=P(("grp", "blk"), None), check_vma=False
    )
```

```python
import functools
import math

import jax
import jax.numpy as jnp
from jax import lax
from jax.experimental import pallas as pl
from jax.experimental.pallas import tpu as pltpu
from jax.sharding import PartitionSpec as P

HEADS = 28
KV_HEADS = 4
GROUP = HEADS // KV_HEADS
LANES = 128
HALVES = 2
CAPS = (8, 2)
SPARE = 1
BIAS = -(2.0**99)
EMPTY = (1e30, 4e30, 16e30)
LIVE_BELOW = 1e29
ROWS8 = 8
TILE = 1024
PART = 512
DEPTHS = (512, 1024)


def project_and_pack(placement, visual, kv_weight, caps, segments):
    rows, dv = visual.shape
    width = kv_weight.shape[1]
    blocks = placement.shape[1]
    block_rows = rows // blocks
    owners = KV_HEADS * HALVES
    common = caps[0] + caps[1]
    most = caps[0] + caps[2]
    cuts = [0]
    while cuts[-1] < dv:
        cuts.append(min(dv, cuts[-1] + DEPTHS[min(len(cuts) - 1, len(DEPTHS) - 1)]))
    parts = list(zip(cuts[:-1], cuts[1:]))
    few = math.gcd(segments, 4)

    def body(owner_ref, x_hbm, w_hbm, o1, o2, o3, x, w, buf, mark1, mark2, code, table, sems):
        loads = []
        for i, (a, b) in enumerate(parts):
            loads.append(
                (
                    pltpu.make_async_copy(x_hbm.at[:, a:b], x.at[:, a:b], sems.at[2 * i]),
                    pltpu.make_async_copy(w_hbm.at[a:b], w.at[a:b], sems.at[2 * i + 1]),
                )
            )
            for load in loads[-1]:
                load.start()
        sem, sem2 = (sems.at[2 * len(parts) + i] for i in range(2))
        sem1 = sems.at[2 * len(parts) + 2 :]

        segment = lax.shift_right_logical(owner_ref[...], owners.bit_length() - 1)
        line = segment.astype(jnp.float32)
        shape = (blocks, blocks)
        i = lax.broadcasted_iota(jnp.int32, shape, 0)
        j = lax.broadcasted_iota(jnp.int32, shape, 1)
        column = jnp.sum(jnp.where(i == j, line, 0.0), axis=1, keepdims=True)
        before = jnp.where((column == line) & (i < j), 1.0, 0.0)
        rank = jnp.sum(before, axis=0, keepdims=True)
        top = jnp.max(rank) + 1.0
        rank = rank.astype(jnp.int32)
        code[...] = line.astype(jnp.int32) * most + rank
        codes = pltpu.make_async_copy(code, table, sem)
        codes.start()
        level = (top > common).astype(jnp.int32)
        level = level + (top > common + SPARE).astype(jnp.int32)
        mark1[...] = jnp.full(mark1.shape, EMPTY[0], jnp.float32)
        mark = jnp.where(level == 0, EMPTY[0], jnp.where(level == 1, EMPTY[1], EMPTY[2]))
        mark2[...] = jnp.broadcast_to(mark.astype(jnp.float32), mark2.shape)
        fills = [pltpu.make_async_copy(mark2, o2.at[:, :, :, :LANES], sem2)]
        for g in range(0, segments, mark1.shape[0]):
            to = o1.at[g : g + mark1.shape[0], :, :, :LANES]
            fills.append(pltpu.make_async_copy(mark1, to, sem1.at[g // mark1.shape[0]]))
        for copy in fills:
            copy.start()
        codes.wait()

        for i, (a, b) in enumerate(parts):
            for load in loads[i]:
                load.wait()
            for kind in range(2):
                for h in range(0, KV_HEADS, 2):
                    c = (kind * KV_HEADS + h) * LANES
                    part = jnp.dot(
                        x[:, a:b], w[a:b, c : c + 2 * LANES], preferred_element_type=jnp.float32
                    )
                    at = slice(kind * LANES, (kind + 1) * LANES)
                    for k in range(2):
                        piece = part[:, k * LANES : (k + 1) * LANES]
                        buf[h + k, :, at] = piece if i == 0 else buf[h + k, :, at] + piece

        for copy in fills:
            copy.wait()

        def send(j, c):
            at = table[0, j]
            slot = at % most
            seg = at // most
            src = buf.at[:, pl.ds(pl.multiple_of(j * block_rows, ROWS8), block_rows), :]

            def copy(out, slot):
                rows_at = pl.ds(pl.multiple_of(slot * block_rows, ROWS8), block_rows)
                dst = out.at[seg, :, rows_at, :]
                pltpu.make_async_copy(src, dst, sem).start()

            @pl.when(slot < caps[0])
            def _():
                copy(o1, slot)

            @pl.when(slot >= caps[0])
            def _():
                @pl.when(level == 0)
                def _():
                    copy(o2, slot - caps[0])

                @pl.when(level > 0)
                def _():
                    copy(o3, slot - caps[0])

            return c

        lax.fori_loop(0, blocks, send, 0, unroll=4)
        pltpu.make_async_copy(buf, buf, sem).wait()

    shapes = [
        pltpu.HBM((segments, KV_HEADS, cap * block_rows, 2 * LANES), jnp.float32)
        for cap in caps
    ]
    hbm = pl.BlockSpec(memory_space=pltpu.HBM)
    return pl.pallas_call(
        body,
        out_shape=shapes,
        in_specs=[pl.BlockSpec(memory_space=pltpu.VMEM), hbm, hbm],
        out_specs=[hbm for _ in caps],
        scratch_shapes=[
            pltpu.VMEM((rows, dv), jnp.bfloat16),
            pltpu.VMEM((dv, width), jnp.bfloat16),
            pltpu.VMEM((KV_HEADS, rows, 2 * LANES), jnp.float32),
            pltpu.VMEM((few, KV_HEADS, caps[0] * block_rows, LANES), jnp.float32),
            pltpu.VMEM((segments, KV_HEADS, caps[1] * block_rows, LANES), jnp.float32),
            pltpu.VMEM((1, blocks), jnp.int32),
            pltpu.SMEM((1, blocks), jnp.int32),
            pltpu.SemaphoreType.DMA((2 * len(parts) + 2 + segments // few,)),
        ],
        compiler_params=pltpu.CompilerParams(vmem_limit_bytes=40 * 2**20),
        name="project_and_pack",
    )(
        placement,
        pltpu.with_memory_space_constraint(visual, pltpu.HBM),
        pltpu.with_memory_space_constraint(kv_weight, pltpu.HBM),
    )


def split_heads(text):
    rows, width = text.shape[0], text.shape[1] // KV_HEADS

    def body(x_ref, o_ref):
        for h in range(KV_HEADS):
            o_ref[h] = x_ref[:, h * width : (h + 1) * width]

    return pl.pallas_call(
        body, out_shape=jax.ShapeDtypeStruct((KV_HEADS, rows, width), text.dtype), name="split_heads"
    )(text)


def attend(state, queries, me, kv, rows, with_mark=False):
    every = HALVES * queries[0].shape[0]
    width = queries[0].shape[1]
    group = width // LANES
    sources, slots, _ = kv.shape
    scale = LANES ** (-0.5) * math.log2(math.e)
    take = min(sources, 1 << (TILE // slots).bit_length() - 1)
    while sources % take:
        take //= 2
    keys = take * slots
    part = PART
    while keys % part:
        part //= 2
    steps = sources // take
    first = state is None
    owners = every // rows
    columns = (group + 1) * LANES

    def body(me_ref, *refs):
        refs = list(refs)
        s_ref = None if first else refs.pop(0)
        own_ref, other_ref, kv_ref, o_ref = refs[:4]
        f_ref = refs[4] if with_mark else None
        q_s, m_s, l_s, acc_s, k_s, v_s = refs[-6:]
        step = pl.program_id(0)

        @pl.when(step == 0)
        def _():
            ones = (lax.broadcasted_iota(jnp.int32, (every, LANES), 1) == 0).astype(jnp.float32)
            ones = ones.astype(jnp.bfloat16)
            core = jnp.bitwise_and(me_ref[0], HALVES - 1)
            for p in range(owners):
                at = slice(p // HALVES * rows, (p // HALVES + 1) * rows)
                to = slice(p * rows, (p + 1) * rows)
                for j in range(group):
                    cols = slice(j * LANES, (j + 1) * LANES)
                    x = jnp.where(core == p % HALVES, own_ref[at, cols], other_ref[at, cols]) * scale
                    hi = x.astype(jnp.bfloat16)
                    lo = (x - hi.astype(jnp.float32)).astype(jnp.bfloat16)
                    q_s[j, to, 0 * LANES : 1 * LANES] = hi
                    q_s[j, to, 1 * LANES : 2 * LANES] = lo
                    q_s[j, to, 2 * LANES : 3 * LANES] = hi
            for j in range(group):
                q_s[j, :, 3 * LANES : 4 * LANES] = ones
            if first:
                m_s[...] = jnp.full(m_s.shape, BIAS, jnp.float32)
                l_s[...] = jnp.zeros(l_s.shape, jnp.float32)
                acc_s[...] = jnp.zeros(acc_s.shape, jnp.float32)
            else:
                stats = s_ref[:, :, group * LANES :].reshape(every, LANES)
                lane0 = lax.broadcasted_iota(jnp.int32, (every, LANES), 1) == 0
                for j in range(group):
                    acc_s[j] = s_ref[:, :, j * LANES : (j + 1) * LANES].reshape(every, LANES)
                    m_s[j] = jnp.broadcast_to(stats[:, j : j + 1], (every, LANES))
                    total = jnp.broadcast_to(
                        stats[:, LANES // 2 + j : LANES // 2 + j + 1], (every, LANES)
                    )
                    l_s[j] = jnp.where(lane0, total, 0.0)

        live = kv_ref[:, :, :LANES] < LIVE_BELOW
        key = jnp.where(live, kv_ref[:, :, :LANES], 0.0).reshape(keys, LANES)
        value = jnp.where(live, kv_ref[:, :, LANES:], 0.0).reshape(keys, LANES)
        lane = lax.broadcasted_iota(jnp.int32, (take, slots, LANES), 2)
        bias = jnp.where(live | (lane != 0), 0.0, BIAS).reshape(keys, LANES)
        k_hi = key.astype(jnp.bfloat16)
        k_s[:, 0 * LANES : 1 * LANES] = k_hi
        k_s[:, 1 * LANES : 2 * LANES] = k_hi
        k_s[:, 2 * LANES : 3 * LANES] = (key - k_hi.astype(jnp.float32)).astype(jnp.bfloat16)
        k_s[:, 3 * LANES : 4 * LANES] = bias.astype(jnp.bfloat16)
        v_hi = value.astype(jnp.bfloat16)
        v_s[:, :LANES] = v_hi
        v_s[:, LANES:] = (value - v_hi.astype(jnp.float32)).astype(jnp.bfloat16)
        if with_mark:
            mark = jnp.max(jnp.max(kv_ref[:, :, :LANES].reshape(keys, LANES), axis=0, keepdims=True))
            level = (mark > 2 * EMPTY[0]).astype(jnp.int32)
            level = level + (mark > 2 * EMPTY[1]).astype(jnp.int32)

            @pl.when(step == 0)
            def _():
                f_ref[0, 0] = level

            @pl.when(step > 0)
            def _():
                f_ref[0, 0] = jnp.maximum(f_ref[0, 0], level)

        def score(t, j):
            return lax.dot_general(
                q_s[j],
                k_s[t * part : (t + 1) * part],
                (((1,), (1,)), ((), ())),
                preferred_element_type=jnp.float32,
            )

        def weigh(j, scores):
            old = m_s[j]
            fresh = jnp.maximum(old, jnp.max(scores, axis=1, keepdims=True))
            factor = jnp.exp2(old - fresh)
            weights = jnp.exp2(scores - jnp.tile(fresh, (1, part // LANES)))
            sums = weights[:, :LANES]
            for i in range(1, part // LANES):
                sums = sums + weights[:, i * LANES : (i + 1) * LANES]
            l_s[j] = l_s[j] * factor + sums
            m_s[j] = fresh
            w_hi = weights.astype(jnp.bfloat16)
            return factor, w_hi, (weights - w_hi.astype(jnp.float32)).astype(jnp.bfloat16)

        def gather(t, j, factor, w_hi, w_lo):
            at = slice(t * part, (t + 1) * part)
            both = jnp.dot(w_hi, v_s[at], preferred_element_type=jnp.float32)
            rest = jnp.dot(w_lo, v_s[at, :LANES], preferred_element_type=jnp.float32)
            acc_s[j] = acc_s[j] * factor + (both[:, :LANES] + both[:, LANES:] + rest)

        items = [(t, j) for t in range(keys // part) for j in range(group)]
        scores = score(*items[0])
        behind = None
        for n, item in enumerate(items):
            ahead = score(*items[n + 1]) if n + 1 < len(items) else None
            weighed = weigh(item[1], scores)
            if behind is not None:
                gather(*behind)
            behind = (*item, *weighed)
            scores = ahead
        gather(*behind)

        @pl.when(step == steps - 1)
        def _():
            lane = lax.broadcasted_iota(jnp.int32, (every, LANES), 1)
            stats = jnp.zeros((every, LANES), jnp.float32)
            for j in range(group):
                o_ref[:, :, j * LANES : (j + 1) * LANES] = acc_s[j].reshape(owners, rows, LANES)
                total = jnp.sum(l_s[j], axis=1, keepdims=True)
                stats = jnp.where(lane == j, m_s[j], stats)
                stats = jnp.where(lane == LANES // 2 + j, total, stats)
            o_ref[:, :, group * LANES :] = stats.reshape(owners, rows, LANES)

    state_spec = pl.BlockSpec((owners, rows, columns), lambda i, me: (0, 0, 0))
    in_specs = [
        pl.BlockSpec((every // HALVES, width), lambda i, me: (0, 0)),
        pl.BlockSpec((every // HALVES, width), lambda i, me: (0, 0)),
        pl.BlockSpec((take, slots, 2 * LANES), lambda i, me: (i, 0, 0)),
    ]
    args = (*queries, kv)
    if not first:
        in_specs = [state_spec] + in_specs
        args = (state,) + args
    out_shape = [jax.ShapeDtypeStruct((owners, rows, columns), jnp.float32)]
    out_specs = [state_spec]
    if with_mark:
        out_shape.append(jax.ShapeDtypeStruct((1, 1), jnp.int32))
        out_specs.append(pl.BlockSpec(memory_space=pltpu.SMEM))
    out = pl.pallas_call(
        body,
        out_shape=out_shape,
        grid_spec=pltpu.PrefetchScalarGridSpec(
            num_scalar_prefetch=1,
            grid=(steps,),
            in_specs=in_specs,
            out_specs=out_specs,
            scratch_shapes=[
                pltpu.VMEM((group, every, 4 * LANES), jnp.bfloat16),
                pltpu.VMEM((group, every, LANES), jnp.float32),
                pltpu.VMEM((group, every, LANES), jnp.float32),
                pltpu.VMEM((group, every, LANES), jnp.float32),
                pltpu.VMEM((keys, 4 * LANES), jnp.bfloat16),
                pltpu.VMEM((keys, 2 * LANES), jnp.bfloat16),
            ],
        ),
        compiler_params=pltpu.CompilerParams(vmem_limit_bytes=50 * 2**20),
        name="attend_first" if first else "attend_more",
    )(me, *args)
    return out if with_mark else out[0]


def combine(parts):
    owners, rows, columns = parts.shape
    group = columns // LANES - 1

    def body(x_ref, o_ref):
        for h in range(owners // HALVES):
            a, b = HALVES * h, HALVES * h + 1
            stats_a = x_ref[a, :, group * LANES :]
            stats_b = x_ref[b, :, group * LANES :]
            peak = jnp.maximum(stats_a, stats_b)
            fa, fb = jnp.exp2(stats_a - peak), jnp.exp2(stats_b - peak)
            total = pltpu.roll(stats_a, LANES // 2, 1) * fa + pltpu.roll(stats_b, LANES // 2, 1) * fb
            fa, fb = fa / total, fb / total
            for j in range(group):
                cols = slice(j * LANES, (j + 1) * LANES)
                out = x_ref[a, :, cols] * fa[:, j : j + 1] + x_ref[b, :, cols] * fb[:, j : j + 1]
                o_ref[:, (h * group + j) * LANES : (h * group + j + 1) * LANES] = out

    return pl.pallas_call(
        body,
        out_shape=jax.ShapeDtypeStruct((rows, owners // HALVES * group * LANES), jnp.float32),
        compiler_params=pltpu.CompilerParams(vmem_limit_bytes=20 * 2**20),
        name="combine",
    )(parts)


def on_device(visual, text_queries, kv_weight, placement):
    axes = ("grp", "blk")
    segments = lax.axis_size("grp")
    owners = lax.axis_size("blk")
    devices = segments * owners
    blocks = placement.shape[0]
    block_rows = visual.shape[0] // blocks
    rows = text_queries.shape[0]
    per_pair = max(2, blocks // devices + 1)
    most = owners * per_pair
    caps = CAPS + (most - CAPS[0],)
    common = sum(CAPS)

    owner = placement.reshape(blocks)
    packed = list(project_and_pack(owner.reshape(1, blocks), visual, kv_weight, caps, segments))

    q = split_heads(text_queries)
    same_core = [[z * HALVES + c for z in range(KV_HEADS)] for c in range(HALVES)]
    own_core = lax.all_to_all(q, "blk", 0, 0, axis_index_groups=same_core, tiled=True)
    own_core = own_core.reshape(KV_HEADS * rows, -1)
    other = lax.ppermute(own_core, "blk", [(k, k ^ 1) for k in range(owners)])
    packed[1], other = lax.optimization_barrier((packed[1], other))
    queries = (own_core, other)
    me = lax.axis_index("blk").astype(jnp.int32).reshape(1)

    def exchange(chunk):
        groups = [
            [g * owners + z * HALVES + c for g in range(segments) for z in range(KV_HEADS)]
            for c in range(HALVES)
        ]
        chunk = chunk.reshape(segments * KV_HEADS, -1, 2 * LANES)
        return lax.all_to_all(chunk, axes, 0, 0, axis_index_groups=groups, tiled=True)

    def beyond(slots, state):
        counts = jnp.sum(
            (owner[None, :] // owners == jnp.arange(segments)[:, None]).astype(jnp.int32), axis=1
        )
        held = jnp.where(jnp.max(counts) > common, counts - caps[0], 0)[:, None, None, None]
        slot = (jnp.arange(slots * block_rows) // block_rows)[:, None]
        chunk = packed[2][:, :, : slots * block_rows]
        chunk = jnp.where(slot < held, chunk, EMPTY[0])
        return attend(state, queries, me, exchange(chunk), rows)

    first = exchange(packed[0])
    second = exchange(packed[1])
    state = attend(None, queries, me, first, rows)
    state, level = attend(state, queries, me, second, rows, with_mark=True)
    state = lax.switch(
        level[0, 0],
        [
            lambda s: s,
            lambda s: beyond(CAPS[1] + SPARE, s),
            lambda s: beyond(caps[2], s),
        ],
        state,
    )
    parts = lax.all_to_all(state, "blk", 0, 0, tiled=True)
    return combine(parts)


def solution(mesh):
    placed = (P(("grp", "blk"), None), P(("grp", "blk"), None), P(), P(("grp", "blk"), None))
    return jax.shard_map(
        on_device, mesh=mesh, in_specs=placed, out_specs=P(("grp", "blk"), None), check_vma=False
    )
```

```python
import functools
import math

import jax
import jax.numpy as jnp
from jax import lax
from jax.experimental import pallas as pl
from jax.experimental.pallas import tpu as pltpu
from jax.sharding import PartitionSpec as P

HEADS = 28
KV_HEADS = 4
GROUP = HEADS // KV_HEADS
LANES = 128
HALVES = 2
CAPS = (8, 3)
SPARE = 1
BIAS = -(2.0**99)
EMPTY = (1e30, 4e30, 16e30)
LIVE_BELOW = 1e29
ROWS8 = 8
TILE = 1024
PART = 512
DEPTHS = (512, 1024)


def project_and_pack(placement, visual, kv_weight, caps, segments):
    rows, dv = visual.shape
    width = kv_weight.shape[1]
    blocks = placement.shape[1]
    block_rows = rows // blocks
    owners = KV_HEADS * HALVES
    common = caps[0] + caps[1]
    most = caps[0] + caps[2]
    cuts = [0]
    while cuts[-1] < dv:
        cuts.append(min(dv, cuts[-1] + DEPTHS[min(len(cuts) - 1, len(DEPTHS) - 1)]))
    parts = list(zip(cuts[:-1], cuts[1:]))
    few = math.gcd(segments, 4)

    def body(owner_ref, x_hbm, w_hbm, o1, o2, o3, x, w, buf, mark1, mark2, code, table, sems):
        loads = []
        for i, (a, b) in enumerate(parts):
            loads.append(
                (
                    pltpu.make_async_copy(x_hbm.at[:, a:b], x.at[:, a:b], sems.at[2 * i]),
                    pltpu.make_async_copy(w_hbm.at[a:b], w.at[a:b], sems.at[2 * i + 1]),
                )
            )
            for load in loads[-1]:
                load.start()
        sem, sem2 = (sems.at[2 * len(parts) + i] for i in range(2))
        sem1 = sems.at[2 * len(parts) + 2 :]

        segment = lax.shift_right_logical(owner_ref[...], owners.bit_length() - 1)
        line = segment.astype(jnp.float32)
        shape = (blocks, blocks)
        i = lax.broadcasted_iota(jnp.int32, shape, 0)
        j = lax.broadcasted_iota(jnp.int32, shape, 1)
        column = jnp.sum(jnp.where(i == j, line, 0.0), axis=1, keepdims=True)
        before = jnp.where((column == line) & (i < j), 1.0, 0.0)
        rank = jnp.sum(before, axis=0, keepdims=True)
        top = jnp.max(rank) + 1.0
        rank = rank.astype(jnp.int32)
        code[...] = line.astype(jnp.int32) * most + rank
        codes = pltpu.make_async_copy(code, table, sem)
        codes.start()
        level = (top > common).astype(jnp.int32)
        level = level + (top > common + SPARE).astype(jnp.int32)
        mark1[...] = jnp.full(mark1.shape, EMPTY[0], jnp.float32)
        mark = jnp.where(level == 0, EMPTY[0], jnp.where(level == 1, EMPTY[1], EMPTY[2]))
        mark2[...] = jnp.broadcast_to(mark.astype(jnp.float32), mark2.shape)
        fills = [pltpu.make_async_copy(mark2, o2.at[:, :, :, :LANES], sem2)]
        for g in range(0, segments, mark1.shape[0]):
            to = o1.at[g : g + mark1.shape[0], :, :, :LANES]
            fills.append(pltpu.make_async_copy(mark1, to, sem1.at[g // mark1.shape[0]]))
        for copy in fills:
            copy.start()
        codes.wait()

        for i, (a, b) in enumerate(parts):
            for load in loads[i]:
                load.wait()
            for kind in range(2):
                for h in range(0, KV_HEADS, 2):
                    c = (kind * KV_HEADS + h) * LANES
                    part = jnp.dot(
                        x[:, a:b], w[a:b, c : c + 2 * LANES], preferred_element_type=jnp.float32
                    )
                    at = slice(kind * LANES, (kind + 1) * LANES)
                    for k in range(2):
                        piece = part[:, k * LANES : (k + 1) * LANES]
                        buf[h + k, :, at] = piece if i == 0 else buf[h + k, :, at] + piece

        for copy in fills:
            copy.wait()

        def send(j, c):
            at = table[0, j]
            slot = at % most
            seg = at // most
            src = buf.at[:, pl.ds(pl.multiple_of(j * block_rows, ROWS8), block_rows), :]

            def copy(out, slot):
                rows_at = pl.ds(pl.multiple_of(slot * block_rows, ROWS8), block_rows)
                dst = out.at[seg, :, rows_at, :]
                pltpu.make_async_copy(src, dst, sem).start()

            @pl.when(slot < caps[0])
            def _():
                copy(o1, slot)

            @pl.when(slot >= caps[0])
            def _():
                @pl.when(level == 0)
                def _():
                    copy(o2, slot - caps[0])

                @pl.when(level > 0)
                def _():
                    copy(o3, slot - caps[0])

            return c

        lax.fori_loop(0, blocks, send, 0, unroll=4)
        pltpu.make_async_copy(buf, buf, sem).wait()

    shapes = [
        pltpu.HBM((segments, KV_HEADS, cap * block_rows, 2 * LANES), jnp.float32)
        for cap in caps
    ]
    hbm = pl.BlockSpec(memory_space=pltpu.HBM)
    return pl.pallas_call(
        body,
        out_shape=shapes,
        in_specs=[pl.BlockSpec(memory_space=pltpu.VMEM), hbm, hbm],
        out_specs=[hbm for _ in caps],
        scratch_shapes=[
            pltpu.VMEM((rows, dv), jnp.bfloat16),
            pltpu.VMEM((dv, width), jnp.bfloat16),
            pltpu.VMEM((KV_HEADS, rows, 2 * LANES), jnp.float32),
            pltpu.VMEM((few, KV_HEADS, caps[0] * block_rows, LANES), jnp.float32),
            pltpu.VMEM((segments, KV_HEADS, caps[1] * block_rows, LANES), jnp.float32),
            pltpu.VMEM((1, blocks), jnp.int32),
            pltpu.SMEM((1, blocks), jnp.int32),
            pltpu.SemaphoreType.DMA((2 * len(parts) + 2 + segments // few,)),
        ],
        compiler_params=pltpu.CompilerParams(vmem_limit_bytes=40 * 2**20),
        name="project_and_pack",
    )(
        placement,
        pltpu.with_memory_space_constraint(visual, pltpu.HBM),
        pltpu.with_memory_space_constraint(kv_weight, pltpu.HBM),
    )


def split_heads(text):
    rows, width = text.shape[0], text.shape[1] // KV_HEADS

    def body(x_ref, o_ref):
        for h in range(KV_HEADS):
            o_ref[h] = x_ref[:, h * width : (h + 1) * width]

    return pl.pallas_call(
        body, out_shape=jax.ShapeDtypeStruct((KV_HEADS, rows, width), text.dtype), name="split_heads"
    )(text)


def attend(state, queries, me, kv, rows, with_mark=False):
    every = HALVES * queries[0].shape[0]
    width = queries[0].shape[1]
    group = width // LANES
    sources, slots, _ = kv.shape
    scale = LANES ** (-0.5) * math.log2(math.e)
    take = min(sources, 1 << (TILE // slots).bit_length() - 1)
    while sources % take:
        take //= 2
    keys = take * slots
    part = PART
    while keys % part:
        part //= 2
    steps = sources // take
    first = state is None
    owners = every // rows
    columns = (group + 1) * LANES

    def body(me_ref, *refs):
        refs = list(refs)
        s_ref = None if first else refs.pop(0)
        own_ref, other_ref, kv_ref, o_ref = refs[:4]
        f_ref = refs[4] if with_mark else None
        q_s, m_s, l_s, acc_s, k_s, v_s = refs[-6:]
        step = pl.program_id(0)

        @pl.when(step == 0)
        def _():
            ones = (lax.broadcasted_iota(jnp.int32, (every, LANES), 1) == 0).astype(jnp.float32)
            ones = ones.astype(jnp.bfloat16)
            core = jnp.bitwise_and(me_ref[0], HALVES - 1)
            for p in range(owners):
                at = slice(p // HALVES * rows, (p // HALVES + 1) * rows)
                to = slice(p * rows, (p + 1) * rows)
                for j in range(group):
                    cols = slice(j * LANES, (j + 1) * LANES)
                    x = jnp.where(core == p % HALVES, own_ref[at, cols], other_ref[at, cols]) * scale
                    hi = x.astype(jnp.bfloat16)
                    lo = (x - hi.astype(jnp.float32)).astype(jnp.bfloat16)
                    q_s[j, to, 0 * LANES : 1 * LANES] = hi
                    q_s[j, to, 1 * LANES : 2 * LANES] = lo
                    q_s[j, to, 2 * LANES : 3 * LANES] = hi
            for j in range(group):
                q_s[j, :, 3 * LANES : 4 * LANES] = ones
            if first:
                m_s[...] = jnp.full(m_s.shape, BIAS, jnp.float32)
                l_s[...] = jnp.zeros(l_s.shape, jnp.float32)
                acc_s[...] = jnp.zeros(acc_s.shape, jnp.float32)
            else:
                stats = s_ref[:, :, group * LANES :].reshape(every, LANES)
                lane0 = lax.broadcasted_iota(jnp.int32, (every, LANES), 1) == 0
                for j in range(group):
                    acc_s[j] = s_ref[:, :, j * LANES : (j + 1) * LANES].reshape(every, LANES)
                    m_s[j] = jnp.broadcast_to(stats[:, j : j + 1], (every, LANES))
                    total = jnp.broadcast_to(
                        stats[:, LANES // 2 + j : LANES // 2 + j + 1], (every, LANES)
                    )
                    l_s[j] = jnp.where(lane0, total, 0.0)

        live = kv_ref[:, :, :LANES] < LIVE_BELOW
        key = jnp.where(live, kv_ref[:, :, :LANES], 0.0).reshape(keys, LANES)
        value = jnp.where(live, kv_ref[:, :, LANES:], 0.0).reshape(keys, LANES)
        lane = lax.broadcasted_iota(jnp.int32, (take, slots, LANES), 2)
        bias = jnp.where(live | (lane != 0), 0.0, BIAS).reshape(keys, LANES)
        k_hi = key.astype(jnp.bfloat16)
        k_s[:, 0 * LANES : 1 * LANES] = k_hi
        k_s[:, 1 * LANES : 2 * LANES] = k_hi
        k_s[:, 2 * LANES : 3 * LANES] = (key - k_hi.astype(jnp.float32)).astype(jnp.bfloat16)
        k_s[:, 3 * LANES : 4 * LANES] = bias.astype(jnp.bfloat16)
        v_hi = value.astype(jnp.bfloat16)
        v_s[:, :LANES] = v_hi
        v_s[:, LANES:] = (value - v_hi.astype(jnp.float32)).astype(jnp.bfloat16)
        if with_mark:
            mark = jnp.max(jnp.max(kv_ref[:, :, :LANES].reshape(keys, LANES), axis=0, keepdims=True))
            level = (mark > 2 * EMPTY[0]).astype(jnp.int32)
            level = level + (mark > 2 * EMPTY[1]).astype(jnp.int32)

            @pl.when(step == 0)
            def _():
                f_ref[0, 0] = level

            @pl.when(step > 0)
            def _():
                f_ref[0, 0] = jnp.maximum(f_ref[0, 0], level)

        def score(t, j):
            return lax.dot_general(
                q_s[j],
                k_s[t * part : (t + 1) * part],
                (((1,), (1,)), ((), ())),
                preferred_element_type=jnp.float32,
            )

        def weigh(j, scores):
            old = m_s[j]
            fresh = jnp.maximum(old, jnp.max(scores, axis=1, keepdims=True))
            factor = jnp.exp2(old - fresh)
            weights = jnp.exp2(scores - jnp.tile(fresh, (1, part // LANES)))
            sums = weights[:, :LANES]
            for i in range(1, part // LANES):
                sums = sums + weights[:, i * LANES : (i + 1) * LANES]
            l_s[j] = l_s[j] * factor + sums
            m_s[j] = fresh
            w_hi = weights.astype(jnp.bfloat16)
            return factor, w_hi, (weights - w_hi.astype(jnp.float32)).astype(jnp.bfloat16)

        def gather(t, j, factor, w_hi, w_lo):
            at = slice(t * part, (t + 1) * part)
            both = jnp.dot(w_hi, v_s[at], preferred_element_type=jnp.float32)
            rest = jnp.dot(w_lo, v_s[at, :LANES], preferred_element_type=jnp.float32)
            acc_s[j] = acc_s[j] * factor + (both[:, :LANES] + both[:, LANES:] + rest)

        items = [(t, j) for t in range(keys // part) for j in range(group)]
        scores = score(*items[0])
        behind = None
        for n, item in enumerate(items):
            ahead = score(*items[n + 1]) if n + 1 < len(items) else None
            weighed = weigh(item[1], scores)
            if behind is not None:
                gather(*behind)
            behind = (*item, *weighed)
            scores = ahead
        gather(*behind)

        @pl.when(step == steps - 1)
        def _():
            lane = lax.broadcasted_iota(jnp.int32, (every, LANES), 1)
            stats = jnp.zeros((every, LANES), jnp.float32)
            for j in range(group):
                o_ref[:, :, j * LANES : (j + 1) * LANES] = acc_s[j].reshape(owners, rows, LANES)
                total = jnp.sum(l_s[j], axis=1, keepdims=True)
                stats = jnp.where(lane == j, m_s[j], stats)
                stats = jnp.where(lane == LANES // 2 + j, total, stats)
            o_ref[:, :, group * LANES :] = stats.reshape(owners, rows, LANES)

    state_spec = pl.BlockSpec((owners, rows, columns), lambda i, me: (0, 0, 0))
    in_specs = [
        pl.BlockSpec((every // HALVES, width), lambda i, me: (0, 0)),
        pl.BlockSpec((every // HALVES, width), lambda i, me: (0, 0)),
        pl.BlockSpec((take, slots, 2 * LANES), lambda i, me: (i, 0, 0)),
    ]
    args = (*queries, kv)
    if not first:
        in_specs = [state_spec] + in_specs
        args = (state,) + args
    out_shape = [jax.ShapeDtypeStruct((owners, rows, columns), jnp.float32)]
    out_specs = [state_spec]
    if with_mark:
        out_shape.append(jax.ShapeDtypeStruct((1, 1), jnp.int32))
        out_specs.append(pl.BlockSpec(memory_space=pltpu.SMEM))
    out = pl.pallas_call(
        body,
        out_shape=out_shape,
        grid_spec=pltpu.PrefetchScalarGridSpec(
            num_scalar_prefetch=1,
            grid=(steps,),
            in_specs=in_specs,
            out_specs=out_specs,
            scratch_shapes=[
                pltpu.VMEM((group, every, 4 * LANES), jnp.bfloat16),
                pltpu.VMEM((group, every, LANES), jnp.float32),
                pltpu.VMEM((group, every, LANES), jnp.float32),
                pltpu.VMEM((group, every, LANES), jnp.float32),
                pltpu.VMEM((keys, 4 * LANES), jnp.bfloat16),
                pltpu.VMEM((keys, 2 * LANES), jnp.bfloat16),
            ],
        ),
        compiler_params=pltpu.CompilerParams(vmem_limit_bytes=50 * 2**20),
        name="attend_first" if first else "attend_more",
    )(me, *args)
    return out if with_mark else out[0]


def combine(parts):
    owners, rows, columns = parts.shape
    group = columns // LANES - 1

    def body(x_ref, o_ref):
        for h in range(owners // HALVES):
            a, b = HALVES * h, HALVES * h + 1
            stats_a = x_ref[a, :, group * LANES :]
            stats_b = x_ref[b, :, group * LANES :]
            peak = jnp.maximum(stats_a, stats_b)
            fa, fb = jnp.exp2(stats_a - peak), jnp.exp2(stats_b - peak)
            total = pltpu.roll(stats_a, LANES // 2, 1) * fa + pltpu.roll(stats_b, LANES // 2, 1) * fb
            fa, fb = fa / total, fb / total
            for j in range(group):
                cols = slice(j * LANES, (j + 1) * LANES)
                out = x_ref[a, :, cols] * fa[:, j : j + 1] + x_ref[b, :, cols] * fb[:, j : j + 1]
                o_ref[:, (h * group + j) * LANES : (h * group + j + 1) * LANES] = out

    return pl.pallas_call(
        body,
        out_shape=jax.ShapeDtypeStruct((rows, owners // HALVES * group * LANES), jnp.float32),
        compiler_params=pltpu.CompilerParams(vmem_limit_bytes=20 * 2**20),
        name="combine",
    )(parts)


def on_device(visual, text_queries, kv_weight, placement):
    segments = lax.axis_size("grp")
    owners = lax.axis_size("z") * lax.axis_size("core")
    devices = segments * owners
    blocks = placement.shape[0]
    block_rows = visual.shape[0] // blocks
    rows = text_queries.shape[0]
    per_pair = max(2, blocks // devices + 1)
    most = owners * per_pair
    caps = CAPS + (most - CAPS[0],)
    common = sum(CAPS)

    owner = placement.reshape(blocks)
    packed = list(project_and_pack(owner.reshape(1, blocks), visual, kv_weight, caps, segments))

    q = split_heads(text_queries)
    own_core = lax.all_to_all(q, "z", 0, 0, tiled=True)
    own_core = own_core.reshape(KV_HEADS * rows, -1)
    other = lax.ppermute(own_core, "core", [(k, k ^ 1) for k in range(HALVES)])
    packed[1], other = lax.optimization_barrier((packed[1], other))
    queries = (own_core, other)
    me = lax.axis_index(("z", "core")).astype(jnp.int32).reshape(1)

    def exchange(chunk):
        chunk = chunk.reshape(segments * KV_HEADS, -1, 2 * LANES)
        return lax.all_to_all(chunk, ("grp", "z"), 0, 0, tiled=True)

    def beyond(slots, state):
        counts = jnp.sum(
            (owner[None, :] // owners == jnp.arange(segments)[:, None]).astype(jnp.int32), axis=1
        )
        held = jnp.where(jnp.max(counts) > common, counts - caps[0], 0)[:, None, None, None]
        slot = (jnp.arange(slots * block_rows) // block_rows)[:, None]
        chunk = packed[2][:, :, : slots * block_rows]
        chunk = jnp.where(slot < held, chunk, EMPTY[0])
        return attend(state, queries, me, exchange(chunk), rows)

    first = exchange(packed[0])
    second = exchange(packed[1])
    state = attend(None, queries, me, first, rows)
    state, level = attend(state, queries, me, second, rows, with_mark=True)
    state = lax.switch(
        level[0, 0],
        [
            lambda s: s,
            lambda s: beyond(CAPS[1] + SPARE, s),
            lambda s: beyond(caps[2], s),
        ],
        state,
    )
    parts = lax.all_to_all(state, ("z", "core"), 0, 0, tiled=True)
    return combine(parts)


def solution(mesh):
    shape = (mesh.shape["grp"], mesh.shape["blk"] // HALVES, HALVES)
    fine = jax.sharding.Mesh(mesh.devices.reshape(shape), ("grp", "z", "core"))
    every = P(("grp", "z", "core"), None)
    return jax.shard_map(
        on_device,
        mesh=fine,
        in_specs=(every, every, P(), every),
        out_specs=every,
        check_vma=False,
    )
```

```python
import functools
import math

import jax
import jax.numpy as jnp
from jax import lax
from jax.experimental import pallas as pl
from jax.experimental.pallas import tpu as pltpu
from jax.sharding import PartitionSpec as P

HEADS = 28
KV_HEADS = 4
GROUP = HEADS // KV_HEADS
LANES = 128
HALVES = 2
CAPS = (4, 1)
SPARE = 1
BIAS = -(2.0**99)
EMPTY = (1e30, 4e30, 16e30)
LIVE_BELOW = 1e29
ROWS8 = 8
TILE = 1024
PART = 512
DEPTHS = (512, 1024)


def project_and_pack(placement, visual, kv_weight, caps, segments):
    rows, dv = visual.shape
    width = kv_weight.shape[1]
    blocks = placement.shape[1]
    block_rows = rows // blocks
    owners = KV_HEADS * HALVES
    common = caps[0] + caps[1]
    cuts = [0]
    while cuts[-1] < dv:
        cuts.append(min(dv, cuts[-1] + DEPTHS[min(len(cuts) - 1, len(DEPTHS) - 1)]))
    parts = list(zip(cuts[:-1], cuts[1:]))
    few = math.gcd(segments, 4)

    def body(owner_ref, x_hbm, w_hbm, o1, o2, o3, x, w, buf, mark1, mark2, code, table, sems):
        loads = []
        for i, (a, b) in enumerate(parts):
            loads.append(
                (
                    pltpu.make_async_copy(x_hbm.at[:, a:b], x.at[:, a:b], sems.at[2 * i]),
                    pltpu.make_async_copy(w_hbm.at[a:b], w.at[a:b], sems.at[2 * i + 1]),
                )
            )
            for load in loads[-1]:
                load.start()
        sem, sem2 = (sems.at[2 * len(parts) + i] for i in range(2))
        sem1 = sems.at[2 * len(parts) + 2 :]

        segment = lax.shift_right_logical(owner_ref[...], owners.bit_length() - 1)
        line = segment.astype(jnp.float32)
        shape = (blocks, blocks)
        i = lax.broadcasted_iota(jnp.int32, shape, 0)
        j = lax.broadcasted_iota(jnp.int32, shape, 1)
        column = jnp.sum(jnp.where(i == j, line, 0.0), axis=1, keepdims=True)
        before = jnp.where((column == line) & (i < j), 1.0, 0.0)
        rank = jnp.sum(before, axis=0, keepdims=True)
        top = jnp.max(rank) + 1.0
        rank = rank.astype(jnp.int32)
        half = jnp.bitwise_and(rank, HALVES - 1)
        slot = lax.shift_right_logical(rank, HALVES.bit_length() - 1)
        code[...] = (line.astype(jnp.int32) * HALVES + half) * ROWS8 + slot
        codes = pltpu.make_async_copy(code, table, sem)
        codes.start()
        level = (top > HALVES * common).astype(jnp.int32)
        level = level + (top > HALVES * (common + SPARE)).astype(jnp.int32)
        mark1[...] = jnp.full(mark1.shape, EMPTY[0], jnp.float32)
        mark = jnp.where(level == 0, EMPTY[0], jnp.where(level == 1, EMPTY[1], EMPTY[2]))
        mark2[...] = jnp.broadcast_to(mark.astype(jnp.float32), mark2.shape)
        fills = [pltpu.make_async_copy(mark2, o2.at[:, :, :, :, :LANES], sem2)]
        for g in range(0, segments, mark1.shape[0]):
            to = o1.at[g : g + mark1.shape[0], :, :, :, :LANES]
            fills.append(pltpu.make_async_copy(mark1, to, sem1.at[g // mark1.shape[0]]))
        for copy in fills:
            copy.start()
        codes.wait()

        for i, (a, b) in enumerate(parts):
            for load in loads[i]:
                load.wait()
            for kind in range(2):
                for h in range(0, KV_HEADS, 2):
                    c = (kind * KV_HEADS + h) * LANES
                    part = jnp.dot(
                        x[:, a:b], w[a:b, c : c + 2 * LANES], preferred_element_type=jnp.float32
                    )
                    at = slice(kind * LANES, (kind + 1) * LANES)
                    for k in range(2):
                        piece = part[:, k * LANES : (k + 1) * LANES]
                        buf[h + k, :, at] = piece if i == 0 else buf[h + k, :, at] + piece

        for copy in fills:
            copy.wait()

        def send(j, c):
            at = table[0, j]
            slot = jnp.bitwise_and(at, ROWS8 - 1)
            half = jnp.bitwise_and(lax.shift_right_logical(at, 3), HALVES - 1)
            seg = lax.shift_right_logical(at, 4)
            src = buf.at[:, pl.ds(pl.multiple_of(j * block_rows, ROWS8), block_rows), :]

            def copy(out, slot):
                rows_at = pl.ds(pl.multiple_of(slot * block_rows, ROWS8), block_rows)
                dst = out.at[seg, :, half, rows_at, :]
                pltpu.make_async_copy(src, dst, sem).start()

            @pl.when(slot < caps[0])
            def _():
                copy(o1, slot)

            @pl.when(slot >= caps[0])
            def _():
                @pl.when(level == 0)
                def _():
                    copy(o2, slot - caps[0])

                @pl.when(level > 0)
                def _():
                    copy(o3, slot - caps[0])

            return c

        lax.fori_loop(0, blocks, send, 0, unroll=4)
        pltpu.make_async_copy(buf, buf, sem).wait()

    shapes = [
        pltpu.HBM((segments, KV_HEADS, HALVES, cap * block_rows, 2 * LANES), jnp.float32)
        for cap in caps
    ]
    hbm = pl.BlockSpec(memory_space=pltpu.HBM)
    return pl.pallas_call(
        body,
        out_shape=shapes,
        in_specs=[pl.BlockSpec(memory_space=pltpu.VMEM), hbm, hbm],
        out_specs=[hbm for _ in caps],
        scratch_shapes=[
            pltpu.VMEM((rows, dv), jnp.bfloat16),
            pltpu.VMEM((dv, width), jnp.bfloat16),
            pltpu.VMEM((KV_HEADS, rows, 2 * LANES), jnp.float32),
            pltpu.VMEM((few, KV_HEADS, HALVES, caps[0] * block_rows, LANES), jnp.float32),
            pltpu.VMEM((segments, KV_HEADS, HALVES, caps[1] * block_rows, LANES), jnp.float32),
            pltpu.VMEM((1, blocks), jnp.int32),
            pltpu.SMEM((1, blocks), jnp.int32),
            pltpu.SemaphoreType.DMA((2 * len(parts) + 2 + segments // few,)),
        ],
        compiler_params=pltpu.CompilerParams(vmem_limit_bytes=40 * 2**20),
        name="project_and_pack",
    )(
        placement,
        pltpu.with_memory_space_constraint(visual, pltpu.HBM),
        pltpu.with_memory_space_constraint(kv_weight, pltpu.HBM),
    )


def attend(state, queries, me, kv, rows, with_mark=False):
    every = HALVES * queries[0].shape[0]
    width = queries[0].shape[1]
    group = width // LANES
    sources, slots, _ = kv.shape
    scale = LANES ** (-0.5) * math.log2(math.e)
    take = min(sources, 1 << (TILE // slots).bit_length() - 1)
    while sources % take:
        take //= 2
    keys = take * slots
    part = PART
    while keys % part:
        part //= 2
    steps = sources // take
    first = state is None
    owners = every // rows
    columns = (group + 1) * LANES

    def body(me_ref, *refs):
        refs = list(refs)
        s_ref = None if first else refs.pop(0)
        own_ref, other_ref, kv_ref, o_ref = refs[:4]
        f_ref = refs[4] if with_mark else None
        q_s, m_s, l_s, acc_s, k_s, v_s = refs[-6:]
        step = pl.program_id(0)

        @pl.when(step == 0)
        def _():
            ones = (lax.broadcasted_iota(jnp.int32, (every, LANES), 1) == 0).astype(jnp.float32)
            ones = ones.astype(jnp.bfloat16)
            core = jnp.bitwise_and(me_ref[0], HALVES - 1)
            for p in range(owners):
                away = lax.shift_right_logical(me_ref[0] ^ p, HALVES.bit_length() - 1)
                at = pl.ds(pl.multiple_of(away * rows, rows), rows)
                to = slice(p * rows, (p + 1) * rows)
                for j in range(group):
                    cols = slice(j * LANES, (j + 1) * LANES)
                    x = jnp.where(core == p % HALVES, own_ref[at, cols], other_ref[at, cols]) * scale
                    hi = x.astype(jnp.bfloat16)
                    lo = (x - hi.astype(jnp.float32)).astype(jnp.bfloat16)
                    q_s[j, to, 0 * LANES : 1 * LANES] = hi
                    q_s[j, to, 1 * LANES : 2 * LANES] = lo
                    q_s[j, to, 2 * LANES : 3 * LANES] = hi
            for j in range(group):
                q_s[j, :, 3 * LANES : 4 * LANES] = ones
            if first:
                m_s[...] = jnp.full(m_s.shape, BIAS, jnp.float32)
                l_s[...] = jnp.zeros(l_s.shape, jnp.float32)
                acc_s[...] = jnp.zeros(acc_s.shape, jnp.float32)
            else:
                stats = s_ref[:, :, group * LANES :].reshape(every, LANES)
                lane0 = lax.broadcasted_iota(jnp.int32, (every, LANES), 1) == 0
                for j in range(group):
                    acc_s[j] = s_ref[:, :, j * LANES : (j + 1) * LANES].reshape(every, LANES)
                    m_s[j] = jnp.broadcast_to(stats[:, j : j + 1], (every, LANES))
                    total = jnp.broadcast_to(
                        stats[:, LANES // 2 + j : LANES // 2 + j + 1], (every, LANES)
                    )
                    l_s[j] = jnp.where(lane0, total, 0.0)

        live = kv_ref[:, :, :LANES] < LIVE_BELOW
        key = jnp.where(live, kv_ref[:, :, :LANES], 0.0).reshape(keys, LANES)
        value = jnp.where(live, kv_ref[:, :, LANES:], 0.0).reshape(keys, LANES)
        lane = lax.broadcasted_iota(jnp.int32, (take, slots, LANES), 2)
        bias = jnp.where(live | (lane != 0), 0.0, BIAS).reshape(keys, LANES)
        k_hi = key.astype(jnp.bfloat16)
        k_s[:, 0 * LANES : 1 * LANES] = k_hi
        k_s[:, 1 * LANES : 2 * LANES] = k_hi
        k_s[:, 2 * LANES : 3 * LANES] = (key - k_hi.astype(jnp.float32)).astype(jnp.bfloat16)
        k_s[:, 3 * LANES : 4 * LANES] = bias.astype(jnp.bfloat16)
        v_hi = value.astype(jnp.bfloat16)
        v_s[:, :LANES] = v_hi
        v_s[:, LANES:] = (value - v_hi.astype(jnp.float32)).astype(jnp.bfloat16)
        if with_mark:
            mark = jnp.max(jnp.max(kv_ref[:, :, :LANES].reshape(keys, LANES), axis=0, keepdims=True))
            level = (mark > 2 * EMPTY[0]).astype(jnp.int32)
            level = level + (mark > 2 * EMPTY[1]).astype(jnp.int32)

            @pl.when(step == 0)
            def _():
                f_ref[0, 0] = level

            @pl.when(step > 0)
            def _():
                f_ref[0, 0] = jnp.maximum(f_ref[0, 0], level)

        def score(t, j):
            return lax.dot_general(
                q_s[j],
                k_s[t * part : (t + 1) * part],
                (((1,), (1,)), ((), ())),
                preferred_element_type=jnp.float32,
            )

        def weigh(j, scores):
            old = m_s[j]
            fresh = jnp.maximum(old, jnp.max(scores, axis=1, keepdims=True))
            factor = jnp.exp2(old - fresh)
            weights = jnp.exp2(scores - jnp.tile(fresh, (1, part // LANES)))
            sums = weights[:, :LANES]
            for i in range(1, part // LANES):
                sums = sums + weights[:, i * LANES : (i + 1) * LANES]
            l_s[j] = l_s[j] * factor + sums
            m_s[j] = fresh
            w_hi = weights.astype(jnp.bfloat16)
            return factor, w_hi, (weights - w_hi.astype(jnp.float32)).astype(jnp.bfloat16)

        def gather(t, j, factor, w_hi, w_lo):
            at = slice(t * part, (t + 1) * part)
            both = jnp.dot(w_hi, v_s[at], preferred_element_type=jnp.float32)
            rest = jnp.dot(w_lo, v_s[at, :LANES], preferred_element_type=jnp.float32)
            acc_s[j] = acc_s[j] * factor + (both[:, :LANES] + both[:, LANES:] + rest)

        items = [(t, j) for t in range(keys // part) for j in range(group)]
        scores = score(*items[0])
        behind = None
        for n, item in enumerate(items):
            ahead = score(*items[n + 1]) if n + 1 < len(items) else None
            weighed = weigh(item[1], scores)
            if behind is not None:
                gather(*behind)
            behind = (*item, *weighed)
            scores = ahead
        gather(*behind)

        @pl.when(step == steps - 1)
        def _():
            lane = lax.broadcasted_iota(jnp.int32, (every, LANES), 1)
            stats = jnp.zeros((every, LANES), jnp.float32)
            for j in range(group):
                o_ref[:, :, j * LANES : (j + 1) * LANES] = acc_s[j].reshape(owners, rows, LANES)
                total = jnp.sum(l_s[j], axis=1, keepdims=True)
                stats = jnp.where(lane == j, m_s[j], stats)
                stats = jnp.where(lane == LANES // 2 + j, total, stats)
            o_ref[:, :, group * LANES :] = stats.reshape(owners, rows, LANES)

    state_spec = pl.BlockSpec((owners, rows, columns), lambda i, me: (0, 0, 0))
    in_specs = [
        pl.BlockSpec((every // HALVES, width), lambda i, me: (0, 0)),
        pl.BlockSpec((every // HALVES, width), lambda i, me: (0, 0)),
        pl.BlockSpec((take, slots, 2 * LANES), lambda i, me: (i, 0, 0)),
    ]
    args = (*queries, kv)
    if not first:
        in_specs = [state_spec] + in_specs
        args = (state,) + args
    out_shape = [jax.ShapeDtypeStruct((owners, rows, columns), jnp.float32)]
    out_specs = [state_spec]
    if with_mark:
        out_shape.append(jax.ShapeDtypeStruct((1, 1), jnp.int32))
        out_specs.append(pl.BlockSpec(memory_space=pltpu.SMEM))
    out = pl.pallas_call(
        body,
        out_shape=out_shape,
        grid_spec=pltpu.PrefetchScalarGridSpec(
            num_scalar_prefetch=1,
            grid=(steps,),
            in_specs=in_specs,
            out_specs=out_specs,
            scratch_shapes=[
                pltpu.VMEM((group, every, 4 * LANES), jnp.bfloat16),
                pltpu.VMEM((group, every, LANES), jnp.float32),
                pltpu.VMEM((group, every, LANES), jnp.float32),
                pltpu.VMEM((group, every, LANES), jnp.float32),
                pltpu.VMEM((keys, 4 * LANES), jnp.bfloat16),
                pltpu.VMEM((keys, 2 * LANES), jnp.bfloat16),
            ],
        ),
        compiler_params=pltpu.CompilerParams(vmem_limit_bytes=50 * 2**20),
        name="attend_first" if first else "attend_more",
    )(me, *args)
    return out if with_mark else out[0]


def combine(parts):
    owners, rows, columns = parts.shape
    group = columns // LANES - 1

    def body(x_ref, o_ref):
        for h in range(owners // HALVES):
            a, b = HALVES * h, HALVES * h + 1
            stats_a = x_ref[a, :, group * LANES :]
            stats_b = x_ref[b, :, group * LANES :]
            peak = jnp.maximum(stats_a, stats_b)
            fa, fb = jnp.exp2(stats_a - peak), jnp.exp2(stats_b - peak)
            total = pltpu.roll(stats_a, LANES // 2, 1) * fa + pltpu.roll(stats_b, LANES // 2, 1) * fb
            fa, fb = fa / total, fb / total
            for j in range(group):
                cols = slice(j * LANES, (j + 1) * LANES)
                out = x_ref[a, :, cols] * fa[:, j : j + 1] + x_ref[b, :, cols] * fb[:, j : j + 1]
                o_ref[:, (h * group + j) * LANES : (h * group + j + 1) * LANES] = out

    return pl.pallas_call(
        body,
        out_shape=jax.ShapeDtypeStruct((rows, owners // HALVES * group * LANES), jnp.float32),
        compiler_params=pltpu.CompilerParams(vmem_limit_bytes=20 * 2**20),
        name="combine",
    )(parts)


def on_device(visual, text_queries, kv_weight, placement):
    axes = ("grp", "blk")
    segments = lax.axis_size("grp")
    owners = lax.axis_size("blk")
    devices = segments * owners
    blocks = placement.shape[0]
    block_rows = visual.shape[0] // blocks
    rows = text_queries.shape[0]
    per_pair = max(2, blocks // devices + 1)
    most = owners * per_pair // HALVES
    caps = CAPS + (most - CAPS[0],)
    common = sum(CAPS)

    owner = placement.reshape(blocks)
    packed = list(project_and_pack(owner.reshape(1, blocks), visual, kv_weight, caps, segments))

    me = lax.axis_index("blk").astype(jnp.int32)
    width = text_queries.shape[1] // KV_HEADS
    pieces = []
    for away in range(KV_HEADS):
        z = lax.shift_right_logical(me, HALVES.bit_length() - 1) ^ away
        piece = lax.dynamic_slice_in_dim(text_queries, z * width, width, 1)
        if away:
            pairs = [(k, k ^ (away * HALVES)) for k in range(owners)]
            piece = lax.ppermute(piece, "blk", pairs)
        pieces.append(piece)
    packed[0], *pieces = lax.optimization_barrier((packed[0], *pieces))
    own_core = jnp.concatenate(pieces, axis=0)
    other = lax.ppermute(own_core, "blk", [(k, k ^ 1) for k in range(owners)])
    packed[1], other = lax.optimization_barrier((packed[1], other))
    queries = (own_core, other)
    me = me.reshape(1)

    def exchange(chunk):
        chunk = chunk.reshape(devices, -1, 2 * LANES)
        return lax.all_to_all(chunk, axes, 0, 0, tiled=True)

    def beyond(slots, state):
        counts = jnp.sum(
            (owner[None, :] // owners == jnp.arange(segments)[:, None]).astype(jnp.int32), axis=1
        )
        mine = jnp.max(counts) > HALVES * common
        half = jnp.arange(HALVES)[None, :]
        held = (counts[:, None] + (HALVES - 1) - half) // HALVES - caps[0]
        held = jnp.where(mine, held, 0)[:, None, :, None, None]
        slot = (jnp.arange(slots * block_rows) // block_rows)[:, None]
        chunk = packed[2][:, :, :, : slots * block_rows]
        chunk = jnp.where(slot < held, chunk, EMPTY[0])
        return attend(state, queries, me, exchange(chunk), rows)

    first = exchange(packed[0])
    second = exchange(packed[1])
    state = attend(None, queries, me, first, rows)
    state, level = attend(state, queries, me, second, rows, with_mark=True)
    state = lax.switch(
        level[0, 0],
        [
            lambda s: s,
            lambda s: beyond(CAPS[1] + SPARE, s),
            lambda s: beyond(caps[2], s),
        ],
        state,
    )
    parts = lax.all_to_all(state, "blk", 0, 0, tiled=True)
    return combine(parts)


def solution(mesh):
    placed = (P(("grp", "blk"), None), P(("grp", "blk"), None), P(), P(("grp", "blk"), None))
    return jax.shard_map(
        on_device, mesh=mesh, in_specs=placed, out_specs=P(("grp", "blk"), None), check_vma=False
    )
```

```python
import functools
import math

import jax
import jax.numpy as jnp
from jax import lax
from jax.experimental import pallas as pl
from jax.experimental.pallas import tpu as pltpu
from jax.sharding import PartitionSpec as P

HEADS = 28
KV_HEADS = 4
GROUP = HEADS // KV_HEADS
LANES = 128
HALVES = 2
CAPS = (8, 3)
SPARE = 1
BIAS = -(2.0**99)
EMPTY = (1e30, 4e30, 16e30)
LIVE_BELOW = 1e29
ROWS8 = 8
TILE = 1536
PART = 512
DEPTHS = (512, 1024)


def project_and_pack(placement, visual, kv_weight, caps, segments):
    rows, dv = visual.shape
    width = kv_weight.shape[1]
    blocks = placement.shape[1]
    block_rows = rows // blocks
    owners = KV_HEADS * HALVES
    common = caps[0] + caps[1]
    most = caps[0] + caps[2]
    cuts = [0]
    while cuts[-1] < dv:
        cuts.append(min(dv, cuts[-1] + DEPTHS[min(len(cuts) - 1, len(DEPTHS) - 1)]))
    parts = list(zip(cuts[:-1], cuts[1:]))
    few = math.gcd(segments, 4)

    def body(owner_ref, x_hbm, w_hbm, o1, o2, o3, x, w, buf, mark1, mark2, code, table, sems):
        loads = []
        for i, (a, b) in enumerate(parts):
            loads.append(
                (
                    pltpu.make_async_copy(x_hbm.at[:, a:b], x.at[:, a:b], sems.at[2 * i]),
                    pltpu.make_async_copy(w_hbm.at[a:b], w.at[a:b], sems.at[2 * i + 1]),
                )
            )
            for load in loads[-1]:
                load.start()
        sem, sem2 = (sems.at[2 * len(parts) + i] for i in range(2))
        sem1 = sems.at[2 * len(parts) + 2 :]

        segment = lax.shift_right_logical(owner_ref[...], owners.bit_length() - 1)
        line = segment.astype(jnp.float32)
        shape = (blocks, blocks)
        i = lax.broadcasted_iota(jnp.int32, shape, 0)
        j = lax.broadcasted_iota(jnp.int32, shape, 1)
        column = jnp.sum(jnp.where(i == j, line, 0.0), axis=1, keepdims=True)
        before = jnp.where((column == line) & (i < j), 1.0, 0.0)
        rank = jnp.sum(before, axis=0, keepdims=True)
        top = jnp.max(rank) + 1.0
        rank = rank.astype(jnp.int32)
        code[...] = line.astype(jnp.int32) * most + rank
        codes = pltpu.make_async_copy(code, table, sem)
        codes.start()
        level = (top > common).astype(jnp.int32)
        level = level + (top > common + SPARE).astype(jnp.int32)
        mark1[...] = jnp.full(mark1.shape, EMPTY[0], jnp.float32)
        mark = jnp.where(level == 0, EMPTY[0], jnp.where(level == 1, EMPTY[1], EMPTY[2]))
        mark2[...] = jnp.broadcast_to(mark.astype(jnp.float32), mark2.shape)
        fills = [pltpu.make_async_copy(mark2, o2.at[:, :, :, :LANES], sem2)]
        for g in range(0, segments, mark1.shape[0]):
            to = o1.at[g : g + mark1.shape[0], :, :, :LANES]
            fills.append(pltpu.make_async_copy(mark1, to, sem1.at[g // mark1.shape[0]]))
        for copy in fills:
            copy.start()
        codes.wait()

        for i, (a, b) in enumerate(parts):
            for load in loads[i]:
                load.wait()
            for kind in range(2):
                for h in range(0, KV_HEADS, 2):
                    c = (kind * KV_HEADS + h) * LANES
                    part = jnp.dot(
                        x[:, a:b], w[a:b, c : c + 2 * LANES], preferred_element_type=jnp.float32
                    )
                    at = slice(kind * LANES, (kind + 1) * LANES)
                    for k in range(2):
                        piece = part[:, k * LANES : (k + 1) * LANES]
                        buf[h + k, :, at] = piece if i == 0 else buf[h + k, :, at] + piece

        for copy in fills:
            copy.wait()

        def send(j, c):
            at = table[0, j]
            slot = at % most
            seg = at // most
            src = buf.at[:, pl.ds(pl.multiple_of(j * block_rows, ROWS8), block_rows), :]

            def copy(out, slot):
                rows_at = pl.ds(pl.multiple_of(slot * block_rows, ROWS8), block_rows)
                dst = out.at[seg, :, rows_at, :]
                pltpu.make_async_copy(src, dst, sem).start()

            @pl.when(slot < caps[0])
            def _():
                copy(o1, slot)

            @pl.when(slot >= caps[0])
            def _():
                @pl.when(level == 0)
                def _():
                    copy(o2, slot - caps[0])

                @pl.when(level > 0)
                def _():
                    copy(o3, slot - caps[0])

            return c

        lax.fori_loop(0, blocks, send, 0, unroll=4)
        pltpu.make_async_copy(buf, buf, sem).wait()

    shapes = [
        pltpu.HBM((segments, KV_HEADS, cap * block_rows, 2 * LANES), jnp.float32)
        for cap in caps
    ]
    hbm = pl.BlockSpec(memory_space=pltpu.HBM)
    return pl.pallas_call(
        body,
        out_shape=shapes,
        in_specs=[pl.BlockSpec(memory_space=pltpu.VMEM), hbm, hbm],
        out_specs=[hbm for _ in caps],
        scratch_shapes=[
            pltpu.VMEM((rows, dv), jnp.bfloat16),
            pltpu.VMEM((dv, width), jnp.bfloat16),
            pltpu.VMEM((KV_HEADS, rows, 2 * LANES), jnp.float32),
            pltpu.VMEM((few, KV_HEADS, caps[0] * block_rows, LANES), jnp.float32),
            pltpu.VMEM((segments, KV_HEADS, caps[1] * block_rows, LANES), jnp.float32),
            pltpu.VMEM((1, blocks), jnp.int32),
            pltpu.SMEM((1, blocks), jnp.int32),
            pltpu.SemaphoreType.DMA((2 * len(parts) + 2 + segments // few,)),
        ],
        compiler_params=pltpu.CompilerParams(vmem_limit_bytes=40 * 2**20),
        name="project_and_pack",
    )(
        placement,
        pltpu.with_memory_space_constraint(visual, pltpu.HBM),
        pltpu.with_memory_space_constraint(kv_weight, pltpu.HBM),
    )


def attend(state, queries, me, kv, rows, with_mark=False):
    every = HALVES * queries[0].shape[0]
    width = queries[0].shape[1]
    group = width // LANES
    sources, slots, _ = kv.shape
    scale = LANES ** (-0.5) * math.log2(math.e)
    take = min(sources, 1 << (TILE // slots).bit_length() - 1)
    while sources % take:
        take //= 2
    keys = take * slots
    part = PART
    while keys % part:
        part //= 2
    steps = sources // take
    first = state is None
    owners = every // rows
    columns = (group + 1) * LANES

    def body(me_ref, *refs):
        refs = list(refs)
        s_ref = None if first else refs.pop(0)
        own_ref, other_ref, kv_ref, o_ref = refs[:4]
        f_ref = refs[4] if with_mark else None
        q_s, m_s, l_s, acc_s, k_s, v_s = refs[-6:]
        step = pl.program_id(0)

        @pl.when(step == 0)
        def _():
            ones = (lax.broadcasted_iota(jnp.int32, (every, LANES), 1) == 0).astype(jnp.float32)
            ones = ones.astype(jnp.bfloat16)
            core = jnp.bitwise_and(me_ref[0], HALVES - 1)
            for p in range(owners):
                away = lax.shift_right_logical(me_ref[0] ^ p, HALVES.bit_length() - 1)
                at = pl.ds(pl.multiple_of(away * rows, rows), rows)
                to = slice(p * rows, (p + 1) * rows)
                for j in range(group):
                    cols = slice(j * LANES, (j + 1) * LANES)
                    x = jnp.where(core == p % HALVES, own_ref[at, cols], other_ref[at, cols]) * scale
                    hi = x.astype(jnp.bfloat16)
                    lo = (x - hi.astype(jnp.float32)).astype(jnp.bfloat16)
                    q_s[j, to, 0 * LANES : 1 * LANES] = hi
                    q_s[j, to, 1 * LANES : 2 * LANES] = lo
                    q_s[j, to, 2 * LANES : 3 * LANES] = hi
            for j in range(group):
                q_s[j, :, 3 * LANES : 4 * LANES] = ones
            if first:
                m_s[...] = jnp.full(m_s.shape, BIAS, jnp.float32)
                l_s[...] = jnp.zeros(l_s.shape, jnp.float32)
                acc_s[...] = jnp.zeros(acc_s.shape, jnp.float32)
            else:
                stats = s_ref[:, :, group * LANES :].reshape(every, LANES)
                lane0 = lax.broadcasted_iota(jnp.int32, (every, LANES), 1) == 0
                for j in range(group):
                    acc_s[j] = s_ref[:, :, j * LANES : (j + 1) * LANES].reshape(every, LANES)
                    m_s[j] = jnp.broadcast_to(stats[:, j : j + 1], (every, LANES))
                    total = jnp.broadcast_to(
                        stats[:, LANES // 2 + j : LANES // 2 + j + 1], (every, LANES)
                    )
                    l_s[j] = jnp.where(lane0, total, 0.0)

        live = kv_ref[:, :, :LANES] < LIVE_BELOW
        key = jnp.where(live, kv_ref[:, :, :LANES], 0.0).reshape(keys, LANES)
        value = jnp.where(live, kv_ref[:, :, LANES:], 0.0).reshape(keys, LANES)
        lane = lax.broadcasted_iota(jnp.int32, (take, slots, LANES), 2)
        bias = jnp.where(live | (lane != 0), 0.0, BIAS).reshape(keys, LANES)
        k_hi = key.astype(jnp.bfloat16)
        k_s[:, 0 * LANES : 1 * LANES] = k_hi
        k_s[:, 1 * LANES : 2 * LANES] = k_hi
        k_s[:, 2 * LANES : 3 * LANES] = (key - k_hi.astype(jnp.float32)).astype(jnp.bfloat16)
        k_s[:, 3 * LANES : 4 * LANES] = bias.astype(jnp.bfloat16)
        v_hi = value.astype(jnp.bfloat16)
        v_s[:, :LANES] = v_hi
        v_s[:, LANES:] = (value - v_hi.astype(jnp.float32)).astype(jnp.bfloat16)
        if with_mark:
            mark = jnp.max(jnp.max(kv_ref[:, :, :LANES].reshape(keys, LANES), axis=0, keepdims=True))
            level = (mark > 2 * EMPTY[0]).astype(jnp.int32)
            level = level + (mark > 2 * EMPTY[1]).astype(jnp.int32)

            @pl.when(step == 0)
            def _():
                f_ref[0, 0] = level

            @pl.when(step > 0)
            def _():
                f_ref[0, 0] = jnp.maximum(f_ref[0, 0], level)

        def score(t, j):
            return lax.dot_general(
                q_s[j],
                k_s[t * part : (t + 1) * part],
                (((1,), (1,)), ((), ())),
                preferred_element_type=jnp.float32,
            )

        def weigh(j, scores):
            old = m_s[j]
            fresh = jnp.maximum(old, jnp.max(scores, axis=1, keepdims=True))
            factor = jnp.exp2(old - fresh)
            weights = jnp.exp2(scores - jnp.tile(fresh, (1, part // LANES)))
            sums = weights[:, :LANES]
            for i in range(1, part // LANES):
                sums = sums + weights[:, i * LANES : (i + 1) * LANES]
            l_s[j] = l_s[j] * factor + sums
            m_s[j] = fresh
            w_hi = weights.astype(jnp.bfloat16)
            return factor, w_hi, (weights - w_hi.astype(jnp.float32)).astype(jnp.bfloat16)

        def gather(t, j, factor, w_hi, w_lo):
            at = slice(t * part, (t + 1) * part)
            both = jnp.dot(w_hi, v_s[at], preferred_element_type=jnp.float32)
            rest = jnp.dot(w_lo, v_s[at, :LANES], preferred_element_type=jnp.float32)
            acc_s[j] = acc_s[j] * factor + (both[:, :LANES] + both[:, LANES:] + rest)

        items = [(t, j) for t in range(keys // part) for j in range(group)]
        scores = score(*items[0])
        behind = None
        for n, item in enumerate(items):
            ahead = score(*items[n + 1]) if n + 1 < len(items) else None
            weighed = weigh(item[1], scores)
            if behind is not None:
                gather(*behind)
            behind = (*item, *weighed)
            scores = ahead
        gather(*behind)

        @pl.when(step == steps - 1)
        def _():
            lane = lax.broadcasted_iota(jnp.int32, (every, LANES), 1)
            stats = jnp.zeros((every, LANES), jnp.float32)
            for j in range(group):
                o_ref[:, :, j * LANES : (j + 1) * LANES] = acc_s[j].reshape(owners, rows, LANES)
                total = jnp.sum(l_s[j], axis=1, keepdims=True)
                stats = jnp.where(lane == j, m_s[j], stats)
                stats = jnp.where(lane == LANES // 2 + j, total, stats)
            o_ref[:, :, group * LANES :] = stats.reshape(owners, rows, LANES)

    state_spec = pl.BlockSpec((owners, rows, columns), lambda i, me: (0, 0, 0))
    in_specs = [
        pl.BlockSpec((every // HALVES, width), lambda i, me: (0, 0)),
        pl.BlockSpec((every // HALVES, width), lambda i, me: (0, 0)),
        pl.BlockSpec((take, slots, 2 * LANES), lambda i, me: (i, 0, 0)),
    ]
    args = (*queries, kv)
    if not first:
        in_specs = [state_spec] + in_specs
        args = (state,) + args
    out_shape = [jax.ShapeDtypeStruct((owners, rows, columns), jnp.float32)]
    out_specs = [state_spec]
    if with_mark:
        out_shape.append(jax.ShapeDtypeStruct((1, 1), jnp.int32))
        out_specs.append(pl.BlockSpec(memory_space=pltpu.SMEM))
    out = pl.pallas_call(
        body,
        out_shape=out_shape,
        grid_spec=pltpu.PrefetchScalarGridSpec(
            num_scalar_prefetch=1,
            grid=(steps,),
            in_specs=in_specs,
            out_specs=out_specs,
            scratch_shapes=[
                pltpu.VMEM((group, every, 4 * LANES), jnp.bfloat16),
                pltpu.VMEM((group, every, LANES), jnp.float32),
                pltpu.VMEM((group, every, LANES), jnp.float32),
                pltpu.VMEM((group, every, LANES), jnp.float32),
                pltpu.VMEM((keys, 4 * LANES), jnp.bfloat16),
                pltpu.VMEM((keys, 2 * LANES), jnp.bfloat16),
            ],
        ),
        compiler_params=pltpu.CompilerParams(vmem_limit_bytes=50 * 2**20),
        name="attend_first" if first else "attend_more",
    )(me, *args)
    return out if with_mark else out[0]


def combine(parts):
    owners, rows, columns = parts.shape
    group = columns // LANES - 1

    def body(x_ref, o_ref):
        for h in range(owners // HALVES):
            a, b = HALVES * h, HALVES * h + 1
            stats_a = x_ref[a, :, group * LANES :]
            stats_b = x_ref[b, :, group * LANES :]
            peak = jnp.maximum(stats_a, stats_b)
            fa, fb = jnp.exp2(stats_a - peak), jnp.exp2(stats_b - peak)
            total = pltpu.roll(stats_a, LANES // 2, 1) * fa + pltpu.roll(stats_b, LANES // 2, 1) * fb
            fa, fb = fa / total, fb / total
            for j in range(group):
                cols = slice(j * LANES, (j + 1) * LANES)
                out = x_ref[a, :, cols] * fa[:, j : j + 1] + x_ref[b, :, cols] * fb[:, j : j + 1]
                o_ref[:, (h * group + j) * LANES : (h * group + j + 1) * LANES] = out

    return pl.pallas_call(
        body,
        out_shape=jax.ShapeDtypeStruct((rows, owners // HALVES * group * LANES), jnp.float32),
        compiler_params=pltpu.CompilerParams(vmem_limit_bytes=20 * 2**20),
        name="combine",
    )(parts)


def on_device(visual, text_queries, kv_weight, placement):
    segments = lax.axis_size("grp")
    owners = lax.axis_size("z") * lax.axis_size("core")
    devices = segments * owners
    blocks = placement.shape[0]
    block_rows = visual.shape[0] // blocks
    rows = text_queries.shape[0]
    per_pair = max(2, blocks // devices + 1)
    most = owners * per_pair
    caps = CAPS + (most - CAPS[0],)
    common = sum(CAPS)

    owner = placement.reshape(blocks)
    packed = list(project_and_pack(owner.reshape(1, blocks), visual, kv_weight, caps, segments))

    me = lax.axis_index(("z", "core")).astype(jnp.int32)
    width = text_queries.shape[1] // KV_HEADS
    pieces = []
    for away in range(KV_HEADS):
        z = lax.axis_index("z").astype(jnp.int32) ^ away
        piece = lax.dynamic_slice_in_dim(text_queries, z * width, width, 1)
        if away:
            piece = lax.ppermute(piece, "z", [(k, k ^ away) for k in range(KV_HEADS)])
        pieces.append(piece)
    packed[0], *pieces = lax.optimization_barrier((packed[0], *pieces))
    own_core = jnp.concatenate(pieces, axis=0)
    other = lax.ppermute(own_core, "core", [(k, k ^ 1) for k in range(HALVES)])
    packed[1], other = lax.optimization_barrier((packed[1], other))
    queries = (own_core, other)
    me = me.reshape(1)

    def exchange(chunk):
        chunk = chunk.reshape(segments * KV_HEADS, -1, 2 * LANES)
        return lax.all_to_all(chunk, ("grp", "z"), 0, 0, tiled=True)

    def beyond(slots, state):
        counts = jnp.sum(
            (owner[None, :] // owners == jnp.arange(segments)[:, None]).astype(jnp.int32), axis=1
        )
        held = jnp.where(jnp.max(counts) > common, counts - caps[0], 0)[:, None, None, None]
        slot = (jnp.arange(slots * block_rows) // block_rows)[:, None]
        chunk = packed[2][:, :, : slots * block_rows]
        chunk = jnp.where(slot < held, chunk, EMPTY[0])
        return attend(state, queries, me, exchange(chunk), rows)

    first = exchange(packed[0])
    second = exchange(packed[1])
    state = attend(None, queries, me, first, rows)
    state, level = attend(state, queries, me, second, rows, with_mark=True)
    state = lax.switch(
        level[0, 0],
        [
            lambda s: s,
            lambda s: beyond(CAPS[1] + SPARE, s),
            lambda s: beyond(caps[2], s),
        ],
        state,
    )
    parts = lax.all_to_all(state, ("z", "core"), 0, 0, tiled=True)
    return combine(parts)


def solution(mesh):
    shape = (mesh.shape["grp"], mesh.shape["blk"] // HALVES, HALVES)
    fine = jax.sharding.Mesh(mesh.devices.reshape(shape), ("grp", "z", "core"))
    every = P(("grp", "z", "core"), None)
    return jax.shard_map(
        on_device,
        mesh=fine,
        in_specs=(every, every, P(), every),
        out_specs=every,
        check_vma=False,
    )
```
